256 devices in a mesh: dp: 4 (over x), space: 64 (over y, z, core).
Axes of the slice: x: 4, y: 4, z: 8, core: 2. Of those that a mesh axis runs over, the one named last changes fastest.
Arguments:
- features: bfloat16 [4, 64, 96, 1024], P('dp', 'space'), may hold values from -6 to 6
- cotangent: bfloat16 [4, 64, 192, 128], P('dp', 'space'), may hold values from -6 to 6
- conv_weight: bfloat16 [96, 2592], replicated, may hold values from -0.125 to 0.125
- down_weight: bfloat16 [192, 768], replicated, may hold values from -0.21875 to 0.21875
- neighbours: int32 [4, 64, 26], P('dp', 'space'), may hold values from -1 to 63, as said below
Outputs:
- coarse_out: bfloat16 [4, 64, 192, 128], P('dp', 'space')
- grad_features: float32 [4, 64, 96, 1024], P('dp', 'space')
- grad_conv: float32 [96, 2592], replicated
- grad_down: float32 [192, 768], replicated
The draws below stay inside these ranges and needn't reach their ends.
Inputs may be any that keep to these rules, and one draw needn't show every extreme that they name: The blocks of a tile sit at distinct cells of a grid; if neighbours[t, s, d] = p is not -1 then neighbours[t, p, 25 - d] = s; a row never names its own block and names a device at most once.
All inputs are finite; a program needn't handle non-finite values.
Results may differ from the reference program's by a relative error of at most 0.0095.
Values may be sent and summed in bfloat16 or wider, within the bound.
No kernel may reach another device: no remote copies, remote signals or barrier semaphores. Data moves between devices by JAX's collectives and lax.ppermute only.
A program may use at most 128 MiB of HBM per device.

```python
import jax
import jax.numpy as jnp
from jax import lax

C = 96
C2 = 192
DEPTH = 16
SIDE = 8
VOX = 1024
COARSE = 128
CUBES = 64
TILES = 4


DIRECTIONS = [(step_x, step_y, step_z) for step_x in (-1, 0, 1) for step_y in (-1, 0, 1) for step_z in (-1, 0, 1) if (step_x, step_y, step_z) != (0, 0, 0)]


def tile_table(key):
    width_x = CUBES // 4
    spot_count = 2 * CUBES
    shuffled = jax.random.permutation(key, spot_count).astype(jnp.int32)
    chosen = shuffled[:CUBES]
    owner_at = jnp.full((spot_count,), -1, jnp.int32).at[chosen].set(jnp.arange(CUBES, dtype=jnp.int32))
    coord_x = chosen // 8
    coord_y = chosen // 2 % 4
    coord_z = chosen % 2
    unit_steps = jnp.array(DIRECTIONS, dtype=jnp.int32)
    near_x = coord_x[:, None] + unit_steps[None, :, 0]
    near_y = coord_y[:, None] + unit_steps[None, :, 1]
    near_z = coord_z[:, None] + unit_steps[None, :, 2]
    inside = (near_x >= 0) & (near_x < width_x) & (near_y >= 0) & (near_y < 4) & (near_z >= 0) & (near_z < 2)
    spot_index = (jnp.clip(near_x, 0, width_x - 1) * 4 + jnp.clip(near_y, 0, 3)) * 2 + jnp.clip(near_z, 0, 1)
    return jnp.where(inside, owner_at[spot_index], -1).astype(jnp.int32)


def draw_neighbours(key, part):
    return jnp.stack([tile_table(jax.random.fold_in(key, 17 + number)) for number in range(TILES)])


def block_levels(rng, shape, pieces, smallest, largest):
    def one(position, blocks):
        heights = jax.random.uniform(jax.random.fold_in(jax.random.fold_in(rng, 6), position), (blocks,), jnp.float32, smallest / len(pieces), largest / len(pieces))
        return jnp.repeat(jnp.exp(heights), shape[position] // blocks).reshape((-1,) + (1,) * (len(shape) - position - 1))

    gain = one(*pieces[0])
    for cut in pieces[1:]:
        gain = gain * one(*cut)
    return gain


def bell_draw(stream_key, dims, spread, bound, shards=(), kind=jnp.bfloat16):
    values = spread * jax.random.normal(stream_key, dims, jnp.float32)
    if shards:
        values = values * block_levels(stream_key, dims, shards, -0.22, 0.18)
    return jnp.clip(values, -bound, bound).astype(kind)


def setup_inputs(seed: int = 0) -> dict:
    key_list = jax.random.split(jax.random.key(seed), 6)
    return {
        "features": bell_draw(key_list[0], (TILES, CUBES, C, VOX), 1.0, 6.0, ((0, 4), (1, 64))),
        "cotangent": bell_draw(key_list[1], (TILES, CUBES, C2, COARSE), 1.0, 6.0, ((0, 4), (1, 64))),
        "conv_weight": bell_draw(key_list[2], (C, 27 * C), (27 * C) ** -0.5, 0.125),
        "down_weight": bell_draw(key_list[3], (C2, 8 * C), (8 * C) ** -0.5, 0.21875),
        "neighbours": draw_neighbours(jax.random.fold_in(key_list[5], 71), 0),
    }


DIRECTIONS = [(step_x, step_y, step_z) for step_x in (-1, 0, 1) for step_y in (-1, 0, 1) for step_z in (-1, 0, 1) if (step_x, step_y, step_z) != (0, 0, 0)]
EPSILON = 1e-06

def cut_inner(offset, extent):
    if offset < 0:
        return slice(0, 1)
    if offset > 0:
        return slice(extent - 1, extent)
    return slice(0, extent)

def cut_outer(offset, extent):
    if offset < 0:
        return slice(0, 1)
    if offset > 0:
        return slice(extent + 1, extent + 2)
    return slice(1, extent + 1)

def inner_layer(block_data, offset):
    return block_data[:, cut_inner(offset[0], block_data.shape[1]), cut_inner(offset[1], block_data.shape[2]), cut_inner(offset[2], block_data.shape[3])]

def to_block(flat_data):
    return flat_data.reshape(flat_data.shape[0], SIDE, SIDE, DEPTH)

def conv_taps(padded, weight_matrix):
    channels = padded.shape[0]
    size_x, size_y, size_z = (padded.shape[1] - 2, padded.shape[2] - 2, padded.shape[3] - 2)
    accumulated = jnp.zeros((weight_matrix.shape[0], size_x * size_y * size_z), jnp.float32)
    for step_x in range(3):
        for step_y in range(3):
            columns = jnp.concatenate([padded[:, step_x:step_x + size_x, step_y:step_y + size_y, step_z:step_z + size_z] for step_z in range(3)], axis=0).reshape(3 * channels, size_x * size_y * size_z)
            start_col = (step_x * 3 + step_y) * 3 * channels
            accumulated = accumulated + jnp.dot(weight_matrix[:, start_col:start_col + 3 * channels], columns, preferred_element_type=jnp.float32)
    return accumulated

def weight_taps(padded, grad_out):
    channels = padded.shape[0]
    size_x, size_y, size_z = (padded.shape[1] - 2, padded.shape[2] - 2, padded.shape[3] - 2)
    blocks_out = []
    for step_x in range(3):
        for step_y in range(3):
            columns = jnp.concatenate([padded[:, step_x:step_x + size_x, step_y:step_y + size_y, step_z:step_z + size_z] for step_z in range(3)], axis=0).reshape(3 * channels, size_x * size_y * size_z)
            blocks_out.append(lax.dot_general(grad_out, columns, (((1,), (1,)), ((), ())), preferred_element_type=jnp.float32))
    return jnp.concatenate(blocks_out, axis=1)

def flipped(weight_matrix):
    channels = weight_matrix.shape[0]
    return weight_matrix.reshape(channels, 27, channels)[:, ::-1, :].transpose(2, 1, 0).reshape(channels, 27 * channels)

def coarse_patches(hidden_block):
    channels, size_x, size_y, size_z = hidden_block.shape
    split = hidden_block.reshape(channels, size_x // 2, 2, size_y // 2, 2, size_z // 2, 2)
    return split.transpose(2, 4, 6, 0, 1, 3, 5).reshape(8 * channels, size_x // 2 * (size_y // 2) * (size_z // 2))

def from_patches(patch_data, channels, size_x, size_y, size_z):
    split = patch_data.reshape(2, 2, 2, channels, size_x // 2, size_y // 2, size_z // 2)
    return split.transpose(3, 4, 0, 5, 1, 6, 2).reshape(channels, size_x * size_y * size_z)

def silu_slope(activation):
    sigmoid_value = jax.nn.sigmoid(activation)
    return sigmoid_value * (1.0 + activation * (1.0 - sigmoid_value))

def normalized(accumulated):
    return accumulated * lax.rsqrt(jnp.mean(accumulated * accumulated) + EPSILON)

def padded_of(source_all, neighbours, tile_index, cube_index):
    own_block = to_block(source_all[tile_index, cube_index])
    owner_row = neighbours[tile_index, cube_index]
    padded = jnp.pad(own_block, ((0, 0), (1, 1), (1, 1), (1, 1)))
    for number, offset in enumerate(DIRECTIONS):
        other_block = to_block(source_all[tile_index, jnp.clip(owner_row[number], 0, CUBES - 1).astype(jnp.int32)])
        facing = inner_layer(other_block, (-offset[0], -offset[1], -offset[2]))
        mask_value = (owner_row[number] >= 0).astype(padded.dtype)
        padded = padded.at[:, cut_outer(offset[0], SIDE), cut_outer(offset[1], SIDE), cut_outer(offset[2], DEPTH)].set(facing * mask_value)
    return padded

def reference(features, cotangent, conv_weight, down_weight, neighbours):
    flip_weight = flipped(conv_weight)

    def first_pass(carry, flat_index):
        tile_index = flat_index // CUBES
        cube_index = flat_index % CUBES
        padded = padded_of(features, neighbours, tile_index, cube_index)
        preact = conv_taps(padded, conv_weight)
        hidden = jax.nn.silu(preact).astype(jnp.bfloat16)
        patches = coarse_patches(hidden.reshape(C, SIDE, SIDE, DEPTH))
        coarse_block = jnp.dot(down_weight, patches, preferred_element_type=jnp.float32).astype(jnp.bfloat16)
        cot_block = cotangent[tile_index, cube_index]
        down_part = lax.dot_general(cot_block, patches, (((1,), (1,)), ((), ())), preferred_element_type=jnp.float32)
        spread_back = from_patches(jnp.dot(down_weight.T, cot_block, preferred_element_type=jnp.float32), C, SIDE, SIDE, DEPTH)
        grad_pre = (spread_back * silu_slope(preact)).astype(jnp.bfloat16)
        conv_part = weight_taps(padded, grad_pre)
        return ((carry[0] + conv_part, carry[1] + down_part), (coarse_block, grad_pre))
    start = (jnp.zeros((C, 27 * C), jnp.float32), jnp.zeros((C2, 8 * C), jnp.float32))
    totals, outputs = lax.scan(first_pass, start, jnp.arange(TILES * CUBES, dtype=jnp.int32))
    coarse_out = outputs[0].reshape(TILES, CUBES, C2, COARSE)
    grad_all = outputs[1].reshape(TILES, CUBES, C, VOX)

    def second_pass(flat_index):
        tile_index = flat_index // CUBES
        cube_index = flat_index % CUBES
        grad_padded = padded_of(grad_all, neighbours, tile_index, cube_index)
        return conv_taps(grad_padded, flip_weight)
    grad_features = lax.map(second_pass, jnp.arange(TILES * CUBES, dtype=jnp.int32)).reshape(TILES, CUBES, C, VOX)
    return (coarse_out, grad_features, normalized(totals[0]), normalized(totals[1]))
```

```python
import jax
import jax.numpy as jnp
import numpy as np
from jax import lax
from jax.experimental import pallas as pl
from jax.experimental.pallas import tpu as pltpu
from jax.sharding import Mesh, PartitionSpec as P

C = 96
C2 = 192
SIDE = 8
DEPTH = 16
VOX = 1024
LANES = 128
SLOTS = 1024
COL = 24
HALF_ROWS = 1664
CONV_ROWS = 1008
EPSILON = 1e-06
F32 = jnp.float32
BF16 = jnp.bfloat16
PARAMS = pltpu.CompilerParams(vmem_limit_bytes=56 << 20)


def slot_tables():
    directions = [
        (ex, ey, ez)
        for ex in (-1, 0, 1)
        for ey in (-1, 0, 1)
        for ez in (-1, 0, 1)
        if (ex, ey, ez) != (0, 0, 0)
    ]
    natural = np.full((SLOTS, 1), -1, np.int32)
    parity = np.full((SLOTS, 1), -1, np.int32)
    number = np.full((SLOTS, 1), -1, np.int32)

    def side(position, extent):
        if position == 0:
            return -1, extent - 1
        if position == extent + 1:
            return 1, 0
        return 0, position - 1

    def fill(slot, px, py, pz):
        (ex, x), (ey, y), (ez, z) = side(px, SIDE), side(py, SIDE), side(pz, DEPTH)
        natural[slot] = (x * SIDE + y) * DEPTH + z
        parity[slot] = (x * SIDE + y) * DEPTH + z % 2 * 8 + z // 2
        number[slot] = directions.index((ex, ey, ez))

    rim = [(x, y) for x in range(10) for y in range(10) if x in (0, 9) or y in (0, 9)]
    for place, (x, y) in enumerate(rim):
        for z in range(DEPTH + 2):
            fill(place * COL + z, x, y, z)
    for x in range(SIDE):
        for y in range(SIDE):
            fill(864 + x * 8 + y, x + 1, y + 1, 0)
            fill(928 + x * 8 + y, x + 1, y + 1, DEPTH + 1)
    return natural, parity, number


NATURAL, PARITY, NUMBER = slot_tables()


def one_hot(index, count):
    wide = lax.broadcasted_iota(jnp.int32, (index.shape[0], count), 1)
    return jnp.where(wide == index, 1.0, 0.0).astype(BF16)


def dot(a, b, ca=1, cb=0):
    return lax.dot_general(a, b, (((ca,), (cb,)), ((), ())), preferred_element_type=F32)


def spread_kernel(f_ref, nbr_ref, vox_ref, num_ref, out_ref):
    wide = jnp.concatenate([f_ref[...], jnp.zeros((LANES - C, VOX), BF16)], axis=0)
    for part in range(4):
        rows = pl.ds(part * 256, 256)
        got = dot(one_hot(vox_ref[rows, :], VOX), wide, 1, 1)
        match = lax.broadcasted_iota(jnp.int32, (256, 26), 1) == num_ref[rows, :]
        owner = jnp.sum(
            jnp.where(match, (nbr_ref[...] + 1).astype(F32), 0.0), axis=1, keepdims=True
        ) - 1.0
        lane = lax.broadcasted_iota(jnp.int32, (256, LANES), 1)
        out_ref[rows, :] = jnp.where(lane >= C, owner, got).astype(BF16)


def route_kernel(owner_ref, rows_ref, out_ref):
    for part in range(4):
        rows = pl.ds(part * 256, 256)
        owner = owner_ref[rows, C : C + 1].astype(F32).astype(jnp.int32)
        place = lax.broadcasted_iota(jnp.int32, (256, 1), 0) & 15
        pick = one_hot(owner * 16 + place, SLOTS)
        out_ref[rows, :] = dot(pick, rows_ref[...]).astype(BF16)


def fill_halo(pad_ref, halo_ref):
    def put(first, count, place):
        pad_ref[pl.ds(first * COL, count * COL), :] = halo_ref[
            pl.ds(place * COL, count * COL), :
        ].astype(F32)

    put(0, 11, 0)
    for x in range(1, 8):
        put(x * 10 + 9, 2, 11 + 2 * (x - 1))
    put(89, 11, 25)
    for x in range(SIDE):
        start = ((x + 1) * 10 + 1) * COL
        pad_ref[pl.ds(start, 8, stride=COL), :] = halo_ref[pl.ds(864 + x * 8, 8), :].astype(F32)
        pad_ref[pl.ds(start + DEPTH + 1, 8, stride=COL), :] = halo_ref[
            pl.ds(928 + x * 8, 8), :
        ].astype(F32)


def shifted_columns(pad_ref, cols_ref):
    for x in range(10):
        for y in range(10):
            base = (x * 10 + y) * COL
            rows = [pad_ref[pl.ds(base + s, 8, stride=2), :] for s in range(4)]
            for dz in range(3):
                cols_ref[x, y, :, pl.ds(dz * LANES, LANES)] = jnp.concatenate(
                    [rows[dz], rows[dz + 1]], axis=0
                ).astype(BF16)


def window(cols_ref, dx, dy):
    return cols_ref[dx : dx + 8, dy : dy + 8].reshape(VOX, 3 * LANES)


def conv(cols_ref, w_ref):
    total = None
    for tap in range(9):
        part = dot(window(cols_ref, tap // 3, tap % 3), w_ref[tap])
        total = part if total is None else total + part
    return total


def forward_kernel(
    f_ref, halo_ref, cot_ref, w_ref, dw_ref, vox_ref,
    coarse_ref, grad_ref, cols_ref, patch_ref, send_ref,
    pad_ref, act_ref,
):
    wide = jnp.concatenate([f_ref[...].astype(F32), jnp.zeros((LANES - C, VOX), F32)], axis=0)
    own = wide.T
    for x in range(SIDE):
        for y in range(SIDE):
            pad_ref[pl.ds(((x + 1) * 10 + y + 1) * COL + 1, DEPTH), :] = own[
                (x * 8 + y) * 16 : (x * 8 + y + 1) * 16, :
            ]
    fill_halo(pad_ref, halo_ref)
    shifted_columns(pad_ref, cols_ref)
    act_ref[...] = conv(cols_ref, w_ref)
    back = dot(cot_ref[...], dw_ref[...], 0, 0)
    for j in range(8):
        jx, jy, jz = j // 4, j // 2 % 2, j % 2
        spots = [
            ((2 * ux + jx) * 8 + 2 * uy + jy) * 16 + jz * 8 for ux in range(4) for uy in range(4)
        ]
        a = jnp.concatenate([act_ref[pl.ds(s, 8), :] for s in spots], axis=0)
        g = 1.0 / (1.0 + jnp.exp(-a))
        patch_ref[:, pl.ds(j * LANES, LANES)] = (a * g).astype(BF16)
        slope = g * (1.0 + a * (1.0 - g))
        grad = back[:, j * LANES : (j + 1) * LANES] * slope
        for n, s in enumerate(spots):
            act_ref[pl.ds(s, 8), :] = grad[n * 8 : n * 8 + 8, :]
    grad_ref[...] = act_ref[...].astype(BF16)
    for part in range(4):
        rows = pl.ds(part * 256, 256)
        send_ref[rows, :] = dot(one_hot(vox_ref[rows, :], VOX), grad_ref[...]).astype(BF16)
    coarse_ref[...] = dot(dw_ref[...], patch_ref[...], 1, 1).astype(BF16)


def weight_kernel(core_ref, grad_ref, cols_ref, patch_ref, cot_ref, keep_ref, send_ref, conv_ref, down_ref):
    turned = grad_ref[...].astype(F32).T[:C, :].astype(BF16)
    conv_ref[:, pl.ds(20 * LANES, LANES)] = jnp.zeros((C, LANES), F32)
    for tap in range(9):
        part = dot(turned, window(cols_ref, tap // 3, tap % 3))
        for dz in range(3):
            conv_ref[:, pl.ds((tap * 3 + dz) * C, C)] = part[:, dz * LANES : dz * LANES + C]
    part = dot(cot_ref[...], patch_ref[...])
    for j in range(8):
        down_ref[:, pl.ds(j * C, C)] = part[:, j * LANES : j * LANES + C]
    core = core_ref[0]
    for ref, half in ((keep_ref, core), (send_ref, 1 - core)):
        for lt in range(21):
            ref[pl.ds(lt * 48, 48), :] = conv_ref[
                pl.ds(pl.multiple_of(half * 48, 16), 48), pl.ds(lt * LANES, LANES)
            ].astype(ref.dtype)
        for lt in range(6):
            ref[pl.ds(CONV_ROWS + lt * 96, 96), :] = down_ref[
                pl.ds(pl.multiple_of(half * 96, 32), 96), pl.ds(lt * LANES, LANES)
            ].astype(ref.dtype)
        ref[pl.ds(1584, HALF_ROWS - 1584), :] = jnp.zeros((HALF_ROWS - 1584, LANES), ref.dtype)


def backward_kernel(grad_ref, halo_ref, w_ref, out_ref, pad_ref, cols_ref, act_ref):
    for x in range(SIDE):
        for y in range(SIDE):
            base = ((x + 1) * 10 + y + 1) * COL
            for par in range(2):
                pad_ref[pl.ds(base + 1 + par, 8, stride=2), :] = grad_ref[
                    pl.ds((x * 8 + y) * 16 + par * 8, 8), :
                ].astype(F32)
    fill_halo(pad_ref, halo_ref)
    shifted_columns(pad_ref, cols_ref)
    full = conv(cols_ref, w_ref)
    for n in range(64):
        for par in range(2):
            act_ref[pl.ds(n * 16 + par, 8, stride=2), :] = full[n * 16 + par * 8 : n * 16 + par * 8 + 8, :]
    out_ref[...] = act_ref[...].T[:C, :]


def finish_kernel(core_ref, mine_ref, other_ref, conv_ref, down_ref):
    def scale(first, last, count):
        total = jnp.zeros((8, LANES), F32)
        for ref in (mine_ref, other_ref):
            values = ref[pl.ds(first, last - first), :].astype(F32)
            total = total + jnp.sum((values * values).reshape(-1, 8, LANES), axis=0)
        return lax.rsqrt(jnp.sum(total, keepdims=True) * (1.0 / count) + EPSILON)

    conv_scale = scale(0, CONV_ROWS, C * 27 * C)
    down_scale = scale(CONV_ROWS, 1584, C2 * 8 * C)
    core = core_ref[0]
    for ref, half in ((mine_ref, core), (other_ref, 1 - core)):
        for lt in range(21):
            width = min(LANES, 27 * C - lt * LANES)
            values = ref[pl.ds(lt * 48, 48), :].astype(F32) * conv_scale
            conv_ref[pl.ds(pl.multiple_of(half * 48, 16), 48), pl.ds(lt * LANES, width)] = values[:, :width]
        for lt in range(6):
            values = ref[pl.ds(CONV_ROWS + lt * 96, 96), :].astype(F32) * down_scale
            down_ref[pl.ds(pl.multiple_of(half * 96, 32), 96), pl.ds(lt * LANES, LANES)] = values


def call(body, outs, scratch=(), scalars=0, ins=0, name=None):
    specs = [pl.BlockSpec(memory_space=pltpu.SMEM)] * scalars + [
        pl.BlockSpec(memory_space=pltpu.VMEM)
    ] * ins
    return pl.pallas_call(
        body,
        out_shape=[jax.ShapeDtypeStruct(shape, kind) for shape, kind in outs],
        in_specs=specs,
        out_specs=[pl.BlockSpec(memory_space=pltpu.VMEM)] * len(outs),
        scratch_shapes=list(scratch),
        compiler_params=PARAMS,
        name=name,
    )


SPACE = ("y", "z", "c")
PLANE = ("x", "y")


def trade(rows, axes, count):
    moved = lax.all_to_all(rows.reshape(count, -1, LANES), axes, 0, 0, tiled=True)
    return moved.reshape(-1, LANES)


def shards(features, cotangent, conv_weight, down_weight, neighbours):
    block = features[0, 0]
    cot = cotangent[0, 0]
    row = neighbours[0]
    core = lax.axis_index("c").astype(jnp.int32).reshape(1)
    other = [(0, 1), (1, 0)]
    rows_shape = ((SLOTS, LANES), BF16)
    natural, parity, number = jnp.asarray(NATURAL), jnp.asarray(PARITY), jnp.asarray(NUMBER)

    (spread,) = call(spread_kernel, [rows_shape], ins=4, name="spread")(block, row, natural, number)
    middle = trade(spread, SPACE, 64)
    route = call(route_kernel, [rows_shape], ins=2, name="route")
    (routed,) = route(middle, middle)
    halo = trade(routed, SPACE, 64)

    taps = conv_weight.reshape(C, 27, C)
    pad = ((0, 0), (0, LANES - C), (0, LANES - C))
    forward_w = jnp.pad(taps.transpose(1, 2, 0), pad).reshape(9, 3 * LANES, LANES)
    backward_w = jnp.pad(taps.transpose(1, 0, 2)[::-1], pad).reshape(9, 3 * LANES, LANES)
    down_w = jnp.pad(down_weight.reshape(C2, 8, C), ((0, 0), (0, 0), (0, LANES - C))).reshape(C2, 8 * LANES)

    pad_scratch = pltpu.VMEM((100 * COL, LANES), F32)
    act_scratch = pltpu.VMEM((VOX, LANES), F32)
    cols_shape = ((10, 10, DEPTH, 3 * LANES), BF16)
    coarse, grad, cols, patch, spread2 = call(
        forward_kernel,
        [((C2, LANES), BF16), rows_shape, cols_shape, ((LANES, 8 * LANES), BF16), rows_shape],
        [pad_scratch, act_scratch],
        ins=6,
        name="forward",
    )(block, halo, cot, forward_w, down_w, parity)

    keep, send = call(
        weight_kernel,
        [((HALF_ROWS, LANES), F32), ((HALF_ROWS, LANES), BF16)],
        [pltpu.VMEM((C, 21 * LANES), F32), pltpu.VMEM((C2, 8 * C), F32)],
        scalars=1,
        ins=4,
        name="weight_grad",
    )(core, grad, cols, patch, cot)
    got = lax.ppermute(send, "c", other)
    pair = (keep + got.astype(F32)).astype(BF16)
    plane = trade(pair, PLANE, 16).reshape(16, 104, LANES)
    part = jnp.sum(plane.astype(F32), axis=0).astype(BF16)
    line = trade(jnp.broadcast_to(part, (8, 104, LANES)), "z", 8).reshape(8, 104, LANES)
    whole = jnp.sum(line.astype(F32), axis=0).astype(BF16)
    mine = trade(jnp.broadcast_to(whole, (16, 104, LANES)), PLANE, 16)
    theirs = lax.ppermute(mine, "c", other)

    middle2 = trade(spread2, SPACE, 64)
    (routed2,) = route(middle, middle2)
    halo2 = trade(routed2, SPACE, 64)
    (grad_features,) = call(
        backward_kernel,
        [((C, VOX), F32)],
        [pad_scratch, pltpu.VMEM(*cols_shape), act_scratch],
        ins=3,
        name="backward",
    )(grad, halo2, backward_w)

    grad_conv, grad_down = call(
        finish_kernel, [((C, 27 * C), F32), ((C2, 8 * C), F32)], scalars=1, ins=2, name="finish"
    )(core, mine, theirs)
    return coarse[None, None], grad_features[None, None], grad_conv, grad_down


def solution(mesh):
    devices = mesh.devices
    fine = Mesh(devices.reshape(devices.shape[0], 4, -1, 2), ("x", "y", "z", "c"))
    block = P("x", SPACE, None, None)
    return jax.shard_map(
        shards,
        mesh=fine,
        in_specs=(block, block, P(), P(), P("x", SPACE, None)),
        out_specs=(block, block, P(), P()),
        check_vma=False,
    )
```

```python
import jax
import jax.numpy as jnp
from jax import lax
from jax.experimental import pallas as pl
from jax.experimental.pallas import tpu as pltpu
from jax.sharding import Mesh, PartitionSpec as P

C = 96
C2 = 192
SIDE = 8
DEPTH = 16
VOX = 1024
LANES = 128
SLOTS = 1024
COL = 24
HALF_ROWS = 1792
CONV_ROWS = 1008
EPSILON = 1e-06
F32 = jnp.float32
BF16 = jnp.bfloat16
PARAMS = pltpu.CompilerParams(vmem_limit_bytes=56 << 20)


RIM = [(x, y) for x in range(10) for y in range(10) if x in (0, 9) or y in (0, 9)]


def side(position, extent):
    if position == 0:
        return -1, extent - 1
    if position == extent + 1:
        return 1, 0
    return 0, position - 1


def direction(ex, ey, ez):
    place = ((ex + 1) * 3 + ey + 1) * 3 + ez + 1
    return place - (place > 13)


def one_hot(index, count):
    wide = lax.broadcasted_iota(jnp.int32, (index.shape[0], count), 1)
    return jnp.where(wide == index, 1.0, 0.0).astype(BF16)


def dot(a, b, ca=1, cb=0):
    return lax.dot_general(a, b, (((ca,), (cb,)), ((), ())), preferred_element_type=F32)


def spread_rows(src_ref, out_ref, parity):
    for place, (px, py) in enumerate(RIM):
        base = (side(px, SIDE)[1] * SIDE + side(py, SIDE)[1]) * DEPTH
        first = place * COL
        if parity:
            for par in range(2):
                out_ref[pl.ds(first + 1 + par, 8, stride=2), :] = src_ref[pl.ds(base + par * 8, 8), :]
        else:
            out_ref[pl.ds(first + 1, DEPTH), :] = src_ref[pl.ds(base, DEPTH), :]
        out_ref[pl.ds(first, 1), :] = src_ref[pl.ds(base + 15, 1), :]
        out_ref[pl.ds(first + 17, 1), :] = src_ref[pl.ds(base, 1), :]
        out_ref[pl.ds(first + 18, 6), :] = jnp.zeros((6, LANES), F32)
    for x in range(SIDE):
        out_ref[pl.ds(864 + x * 8, 8), :] = src_ref[pl.ds(x * 128 + 15, 8, stride=DEPTH), :]
        out_ref[pl.ds(928 + x * 8, 8), :] = src_ref[pl.ds(x * 128, 8, stride=DEPTH), :]
    out_ref[pl.ds(992, 32), :] = jnp.zeros((32, LANES), F32)


def spread_kernel(nbr_ref, f_ref, out_ref, src_ref, row_ref):
    wide = jnp.concatenate([f_ref[...].astype(F32), jnp.zeros((LANES - C, VOX), F32)], axis=0)
    src_ref[...] = wide.T
    spread_rows(src_ref, row_ref, False)

    def owner(ex, ey, ez):
        return nbr_ref[0, direction(ex, ey, ez)].astype(F32)

    lane = lax.broadcasted_iota(jnp.int32, (COL, LANES), 1)
    z = lax.broadcasted_iota(jnp.int32, (COL, LANES), 0)
    for place, (px, py) in enumerate(RIM):
        ex, ey = side(px, SIDE)[0], side(py, SIDE)[0]
        low, mid, high = (owner(ex, ey, ez) for ez in (-1, 0, 1))
        held = jnp.where(z == 0, low, jnp.where(z < 17, mid, jnp.where(z == 17, high, -1.0)))
        rows = pl.ds(place * COL, COL)
        row_ref[rows, :] = jnp.where(lane >= C, held, row_ref[rows, :])
    lane = lax.broadcasted_iota(jnp.int32, (64, LANES), 1)
    for first, ez in ((864, -1), (928, 1)):
        rows = pl.ds(first, 64)
        row_ref[rows, :] = jnp.where(lane >= C, owner(0, 0, ez), row_ref[rows, :])
    out_ref[...] = row_ref[...].astype(BF16)


def route_kernel(core_ref, owner_ref, mine_ref, other_ref, out_ref, row_ref):
    core = core_ref[0]
    for group in range(4):
        slots = slice(group * 8, group * 8 + 8)

        def pick(ref):
            return ref[...].astype(F32)[:, slots].reshape(256, LANES)

        owner = pick(owner_ref)[:, C : C + 1].astype(jnp.int32)
        place = lax.broadcasted_iota(jnp.int32, (256, 1), 0) & 7
        held = jnp.bitwise_and(owner, 1)
        spot = lax.shift_right_arithmetic(owner, 1) * 8 + place + jnp.where(held == core, 0, 256)
        spot = jnp.where(owner < 0, -1, spot)
        source = jnp.concatenate([pick(mine_ref), pick(other_ref)], axis=0).astype(BF16)
        row_ref[:, slots] = dot(one_hot(spot, 512), source).reshape(32, 8, LANES)
    out_ref[...] = row_ref[...].astype(BF16)


def fill_halo(pad_ref, halo_ref):
    def put(first, count, place):
        pad_ref[pl.ds(first * COL, count * COL), :] = halo_ref[
            pl.ds(place * COL, count * COL), :
        ].astype(F32)

    put(0, 11, 0)
    for x in range(1, 8):
        put(x * 10 + 9, 2, 11 + 2 * (x - 1))
    put(89, 11, 25)
    for x in range(SIDE):
        start = ((x + 1) * 10 + 1) * COL
        pad_ref[pl.ds(start, 8, stride=COL), :] = halo_ref[pl.ds(864 + x * 8, 8), :].astype(F32)
        pad_ref[pl.ds(start + DEPTH + 1, 8, stride=COL), :] = halo_ref[
            pl.ds(928 + x * 8, 8), :
        ].astype(F32)


def shifted_columns(pad_ref, cols_ref):
    for x in range(10):
        for y in range(10):
            base = (x * 10 + y) * COL
            rows = [pad_ref[pl.ds(base + s, 8, stride=2), :] for s in range(4)]
            for dz in range(3):
                cols_ref[x, y, :, pl.ds(dz * LANES, LANES)] = jnp.concatenate(
                    [rows[dz], rows[dz + 1]], axis=0
                ).astype(BF16)


def window(cols_ref, dx, dy):
    return cols_ref[dx : dx + 8, dy : dy + 8].reshape(VOX, 3 * LANES)


def conv(cols_ref, w_ref):
    total = None
    for tap in range(9):
        part = dot(window(cols_ref, tap // 3, tap % 3), w_ref[tap])
        total = part if total is None else total + part
    return total


def forward_kernel(
    core_ref, f_ref, halo_ref, cot_ref, w_ref, dw_ref,
    grad_ref, patch_ref, keep_ref, send_ref,
    pad_ref, cols_ref, act_ref, conv_ref, down_ref,
):
    wide = jnp.concatenate([f_ref[...].astype(F32), jnp.zeros((LANES - C, VOX), F32)], axis=0)
    own = wide.T
    for x in range(SIDE):
        for y in range(SIDE):
            pad_ref[pl.ds(((x + 1) * 10 + y + 1) * COL + 1, DEPTH), :] = own[
                (x * 8 + y) * 16 : (x * 8 + y + 1) * 16, :
            ]
    fill_halo(pad_ref, halo_ref)
    shifted_columns(pad_ref, cols_ref)
    act_ref[...] = conv(cols_ref, w_ref)
    back = dot(cot_ref[...], dw_ref[...], 0, 0)
    for j in range(8):
        jx, jy, jz = j // 4, j // 2 % 2, j % 2
        spots = [
            ((2 * ux + jx) * 8 + 2 * uy + jy) * 16 + jz * 8 for ux in range(4) for uy in range(4)
        ]
        a = jnp.concatenate([act_ref[pl.ds(s, 8), :] for s in spots], axis=0)
        g = 1.0 / (1.0 + jnp.exp(-a))
        patch_ref[:, pl.ds(j * LANES, LANES)] = (a * g).astype(BF16)
        slope = g * (1.0 + a * (1.0 - g))
        grad = back[:, j * LANES : (j + 1) * LANES] * slope
        for n, s in enumerate(spots):
            act_ref[pl.ds(s, 8), :] = grad[n * 8 : n * 8 + 8, :]
    grad_ref[...] = act_ref[...].astype(BF16)

    turned = act_ref[...].T[:C, :].astype(BF16)
    conv_ref[:, pl.ds(20 * LANES, LANES)] = jnp.zeros((C, LANES), F32)
    for tap in range(9):
        part = dot(turned, window(cols_ref, tap // 3, tap % 3))
        for dz in range(3):
            conv_ref[:, pl.ds((tap * 3 + dz) * C, C)] = part[:, dz * LANES : dz * LANES + C]
    part = dot(cot_ref[...], patch_ref[...])
    for j in range(8):
        down_ref[:, pl.ds(j * C, C)] = part[:, j * LANES : j * LANES + C]
    core = core_ref[0]
    for ref, half in ((keep_ref, core), (send_ref, 1 - core)):
        for lt in range(21):
            ref[pl.ds(lt * 48, 48), :] = conv_ref[
                pl.ds(pl.multiple_of(half * 48, 16), 48), pl.ds(lt * LANES, LANES)
            ].astype(ref.dtype)
        for lt in range(6):
            ref[pl.ds(CONV_ROWS + lt * 96, 96), :] = down_ref[
                pl.ds(pl.multiple_of(half * 96, 32), 96), pl.ds(lt * LANES, LANES)
            ].astype(ref.dtype)
        ref[pl.ds(1584, HALF_ROWS - 1584), :] = jnp.zeros((HALF_ROWS - 1584, LANES), ref.dtype)


def side_kernel(grad_ref, patch_ref, dw_ref, send_ref, coarse_ref, src_ref, row_ref):
    src_ref[...] = grad_ref[...].astype(F32)
    spread_rows(src_ref, row_ref, True)
    send_ref[...] = row_ref[...].astype(BF16)
    coarse_ref[...] = dot(dw_ref[...], patch_ref[...], 1, 1).astype(BF16)


def backward_kernel(grad_ref, halo_ref, w_ref, out_ref, pad_ref, cols_ref, act_ref):
    for x in range(SIDE):
        for y in range(SIDE):
            base = ((x + 1) * 10 + y + 1) * COL
            for par in range(2):
                pad_ref[pl.ds(base + 1 + par, 8, stride=2), :] = grad_ref[
                    pl.ds((x * 8 + y) * 16 + par * 8, 8), :
                ].astype(F32)
    fill_halo(pad_ref, halo_ref)
    shifted_columns(pad_ref, cols_ref)
    full = conv(cols_ref, w_ref)
    for n in range(64):
        for par in range(2):
            act_ref[pl.ds(n * 16 + par, 8, stride=2), :] = full[n * 16 + par * 8 : n * 16 + par * 8 + 8, :]
    out_ref[...] = act_ref[...].T[:C, :]


def finish_kernel(core_ref, mine_ref, other_ref, conv_ref, down_ref):
    def scale(first, last, count):
        total = jnp.zeros((8, LANES), F32)
        for ref in (mine_ref, other_ref):
            values = ref[pl.ds(first, last - first), :].astype(F32)
            total = total + jnp.sum((values * values).reshape(-1, 8, LANES), axis=0)
        return lax.rsqrt(jnp.sum(total, keepdims=True) * (1.0 / count) + EPSILON)

    conv_scale = scale(0, CONV_ROWS, C * 27 * C)
    down_scale = scale(CONV_ROWS, 1584, C2 * 8 * C)
    core = core_ref[0]
    for ref, half in ((mine_ref, core), (other_ref, 1 - core)):
        for lt in range(21):
            width = min(LANES, 27 * C - lt * LANES)
            values = ref[pl.ds(lt * 48, 48), :].astype(F32) * conv_scale
            conv_ref[pl.ds(pl.multiple_of(half * 48, 16), 48), pl.ds(lt * LANES, width)] = values[:, :width]
        for lt in range(6):
            values = ref[pl.ds(CONV_ROWS + lt * 96, 96), :].astype(F32) * down_scale
            down_ref[pl.ds(pl.multiple_of(half * 96, 32), 96), pl.ds(lt * LANES, LANES)] = values


def call(body, outs, scratch=(), scalars=0, ins=0, name=None):
    specs = [pl.BlockSpec(memory_space=pltpu.SMEM)] * scalars + [
        pl.BlockSpec(memory_space=pltpu.VMEM)
    ] * ins
    return pl.pallas_call(
        body,
        out_shape=[jax.ShapeDtypeStruct(shape, kind) for shape, kind in outs],
        in_specs=specs,
        out_specs=[pl.BlockSpec(memory_space=pltpu.VMEM)] * len(outs),
        scratch_shapes=list(scratch),
        compiler_params=PARAMS,
        name=name,
    )


CHIPS = ("y", "z")
SPACE = ("y", "z", "c")


def trade(rows, axes):
    return lax.all_to_all(rows, axes, 0, 0, tiled=True)


def shards(features, cotangent, conv_weight, down_weight, neighbours):
    block = features[0, 0]
    cot = cotangent[0, 0]
    core = lax.axis_index("c").astype(jnp.int32).reshape(1)
    rows_shape = ((SLOTS, LANES), BF16)
    by_chip = (32, 32, LANES)
    row_scratch = pltpu.VMEM((SLOTS, LANES), F32)

    def swap(rows):
        return lax.ppermute(rows, "c", [(0, 1), (1, 0)])

    (spread,) = call(spread_kernel, [rows_shape], [row_scratch, row_scratch], scalars=1, ins=1, name="spread")(
        neighbours[0], block
    )
    middle = trade(spread.reshape(by_chip), CHIPS)
    route = call(route_kernel, [(by_chip, BF16)], [pltpu.VMEM(by_chip, F32)], scalars=1, ins=3, name="route")
    (routed,) = route(core, middle, middle, swap(middle))
    halo = trade(routed, CHIPS).reshape(SLOTS, LANES)

    taps = conv_weight.reshape(C, 27, C)
    pad = ((0, 0), (0, LANES - C), (0, LANES - C))
    forward_w = jnp.pad(taps.transpose(1, 2, 0), pad).reshape(9, 3 * LANES, LANES)
    backward_w = jnp.pad(taps.transpose(1, 0, 2)[::-1], pad).reshape(9, 3 * LANES, LANES)
    down_w = jnp.pad(down_weight.reshape(C2, 8, C), ((0, 0), (0, 0), (0, LANES - C))).reshape(C2, 8 * LANES)

    pad_scratch = pltpu.VMEM((100 * COL, LANES), F32)
    cols_scratch = pltpu.VMEM((10, 10, DEPTH, 3 * LANES), BF16)
    grad, patch, keep, send = call(
        forward_kernel,
        [rows_shape, ((LANES, 8 * LANES), BF16), ((HALF_ROWS, LANES), F32), ((HALF_ROWS, LANES), BF16)],
        [pad_scratch, cols_scratch, row_scratch, pltpu.VMEM((C, 21 * LANES), F32), pltpu.VMEM((C2, 8 * C), F32)],
        scalars=1,
        ins=5,
        name="forward",
    )(core, block, halo, cot, forward_w, down_w)
    spread2, coarse = call(
        side_kernel, [rows_shape, ((C2, LANES), BF16)], [row_scratch, row_scratch], ins=3, name="side"
    )(grad, patch, down_w)

    pair = (keep + swap(send).astype(F32)).astype(BF16)
    out = jnp.concatenate([spread2.reshape(by_chip), pair.reshape(32, 56, LANES)], axis=1)
    got = trade(out, CHIPS)
    middle2 = got[:, :32]
    part = jnp.sum(got[:, 32:].astype(F32), axis=0)
    line = trade(jnp.broadcast_to(part, (4, 56, LANES)), "x")
    whole = jnp.sum(line, axis=0).astype(BF16)
    (routed2,) = route(core, middle, middle2, swap(middle2))
    out = jnp.concatenate([routed2, jnp.broadcast_to(whole, (32, 56, LANES))], axis=1)
    got = trade(out, CHIPS)
    halo2 = got[:, :32].reshape(SLOTS, LANES)
    mine = got[:, 32:].reshape(HALF_ROWS, LANES)
    theirs = swap(mine)
    (grad_features,) = call(
        backward_kernel,
        [((C, VOX), F32)],
        [pad_scratch, cols_scratch, row_scratch],
        ins=3,
        name="backward",
    )(grad, halo2, backward_w)
    grad_conv, grad_down = call(
        finish_kernel, [((C, 27 * C), F32), ((C2, 8 * C), F32)], scalars=1, ins=2, name="finish"
    )(core, mine, theirs)
    return coarse[None, None], grad_features[None, None], grad_conv, grad_down


def solution(mesh):
    devices = mesh.devices
    fine = Mesh(devices.reshape(devices.shape[0], 4, -1, 2), ("x", "y", "z", "c"))
    block = P("x", SPACE, None, None)
    return jax.shard_map(
        shards,
        mesh=fine,
        in_specs=(block, block, P(), P(), P("x", SPACE, None)),
        out_specs=(block, block, P(), P()),
        check_vma=False,
    )
```

```python
import jax
import jax.numpy as jnp
from jax import lax
from jax.experimental import pallas as pl
from jax.experimental.pallas import tpu as pltpu
from jax.sharding import Mesh, PartitionSpec as P

C = 96
C2 = 192
SIDE = 8
DEPTH = 16
VOX = 1024
LANES = 128
SLOTS = 1024
COL = 24
HALF_ROWS = 1792
CONV_ROWS = 1008
EPSILON = 1e-06
F32 = jnp.float32
BF16 = jnp.bfloat16
PARAMS = pltpu.CompilerParams(vmem_limit_bytes=32 << 20)


RIM = [(x, y) for x in range(10) for y in range(10) if x in (0, 9) or y in (0, 9)]


def side(position, extent):
    if position == 0:
        return -1, extent - 1
    if position == extent + 1:
        return 1, 0
    return 0, position - 1


def direction(ex, ey, ez):
    place = ((ex + 1) * 3 + ey + 1) * 3 + ez + 1
    return place - (place > 13)


def one_hot(index, count):
    wide = lax.broadcasted_iota(jnp.int32, (index.shape[0], count), 1)
    return jnp.where(wide == index, 1.0, 0.0).astype(BF16)


def dot(a, b, ca=1, cb=0):
    return lax.dot_general(a, b, (((ca,), (cb,)), ((), ())), preferred_element_type=F32)


def spread_rows(src_ref, out_ref, parity):
    for place, (px, py) in enumerate(RIM):
        base = (side(px, SIDE)[1] * SIDE + side(py, SIDE)[1]) * DEPTH
        first = place * COL
        if parity:
            for par in range(2):
                out_ref[pl.ds(first + 1 + par, 8, stride=2), :] = src_ref[pl.ds(base + par * 8, 8), :]
        else:
            out_ref[pl.ds(first + 1, DEPTH), :] = src_ref[pl.ds(base, DEPTH), :]
        out_ref[pl.ds(first, 1), :] = src_ref[pl.ds(base + 15, 1), :]
        out_ref[pl.ds(first + 17, 1), :] = src_ref[pl.ds(base, 1), :]
        out_ref[pl.ds(first + 18, 6), :] = jnp.zeros((6, LANES), F32)
    for x in range(SIDE):
        out_ref[pl.ds(864 + x * 8, 8), :] = src_ref[pl.ds(x * 128 + 15, 8, stride=DEPTH), :]
        out_ref[pl.ds(928 + x * 8, 8), :] = src_ref[pl.ds(x * 128, 8, stride=DEPTH), :]
    out_ref[pl.ds(992, 32), :] = jnp.zeros((32, LANES), F32)


def spread_kernel(nbr_ref, f_ref, out_ref, src_ref, row_ref):
    wide = jnp.concatenate([f_ref[...].astype(F32), jnp.zeros((LANES - C, VOX), F32)], axis=0)
    src_ref[...] = wide.T
    spread_rows(src_ref, row_ref, False)

    def owner(ex, ey, ez):
        return nbr_ref[0, direction(ex, ey, ez)].astype(F32)

    lane = lax.broadcasted_iota(jnp.int32, (COL, LANES), 1)
    z = lax.broadcasted_iota(jnp.int32, (COL, LANES), 0)
    for place, (px, py) in enumerate(RIM):
        ex, ey = side(px, SIDE)[0], side(py, SIDE)[0]
        low, mid, high = (owner(ex, ey, ez) for ez in (-1, 0, 1))
        held = jnp.where(z == 0, low, jnp.where(z < 17, mid, jnp.where(z == 17, high, -1.0)))
        rows = pl.ds(place * COL, COL)
        row_ref[rows, :] = jnp.where(lane >= C, held, row_ref[rows, :])
    lane = lax.broadcasted_iota(jnp.int32, (64, LANES), 1)
    for first, ez in ((864, -1), (928, 1)):
        rows = pl.ds(first, 64)
        row_ref[rows, :] = jnp.where(lane >= C, owner(0, 0, ez), row_ref[rows, :])
    out_ref[...] = row_ref[...].astype(BF16)


def route_kernel(core_ref, owner_ref, mine_ref, other_ref, out_ref, row_ref):
    core = core_ref[0]
    for group in range(4):
        slots = slice(group * 8, group * 8 + 8)

        def pick(ref):
            return ref[...].astype(F32)[:, slots].reshape(256, LANES)

        owner = pick(owner_ref)[:, C : C + 1].astype(jnp.int32)
        place = lax.broadcasted_iota(jnp.int32, (256, 1), 0) & 7
        held = jnp.bitwise_and(owner, 1)
        spot = lax.shift_right_arithmetic(owner, 1) * 8 + place + jnp.where(held == core, 0, 256)
        spot = jnp.where(owner < 0, -1, spot)
        source = jnp.concatenate([pick(mine_ref), pick(other_ref)], axis=0).astype(BF16)
        row_ref[:, slots] = dot(one_hot(spot, 512), source).reshape(32, 8, LANES)
    out_ref[...] = row_ref[...].astype(BF16)


def fill_halo(pad_ref, halo_ref):
    def put(first, count, place):
        pad_ref[pl.ds(first * COL, count * COL), :] = halo_ref[
            pl.ds(place * COL, count * COL), :
        ].astype(F32)

    put(0, 11, 0)
    for x in range(1, 8):
        put(x * 10 + 9, 2, 11 + 2 * (x - 1))
    put(89, 11, 25)
    for x in range(SIDE):
        start = ((x + 1) * 10 + 1) * COL
        pad_ref[pl.ds(start, 8, stride=COL), :] = halo_ref[pl.ds(864 + x * 8, 8), :].astype(F32)
        pad_ref[pl.ds(start + DEPTH + 1, 8, stride=COL), :] = halo_ref[
            pl.ds(928 + x * 8, 8), :
        ].astype(F32)


def shifted_columns(pad_ref, cols_ref):
    for x in range(10):
        for y in range(10):
            base = (x * 10 + y) * COL
            rows = [pad_ref[pl.ds(base + s, 8, stride=2), :] for s in range(4)]
            for dz in range(3):
                cols_ref[x, y, :, pl.ds(dz * LANES, LANES)] = jnp.concatenate(
                    [rows[dz], rows[dz + 1]], axis=0
                ).astype(BF16)


def window(cols_ref, dx, dy):
    return cols_ref[dx : dx + 8, dy : dy + 8].reshape(VOX, 3 * LANES)


def conv(cols_ref, w_ref):
    total = None
    for tap in range(9):
        part = dot(window(cols_ref, tap // 3, tap % 3), w_ref[tap])
        total = part if total is None else total + part
    return total


def forward_kernel(
    core_ref, f_ref, halo_ref, cot_ref, w_ref, dw_ref,
    grad_ref, patch_ref, keep_ref, send_ref,
    pad_ref, cols_ref, act_ref, conv_ref, down_ref,
):
    wide = jnp.concatenate([f_ref[...].astype(F32), jnp.zeros((LANES - C, VOX), F32)], axis=0)
    own = wide.T
    for x in range(SIDE):
        for y in range(SIDE):
            pad_ref[pl.ds(((x + 1) * 10 + y + 1) * COL + 1, DEPTH), :] = own[
                (x * 8 + y) * 16 : (x * 8 + y + 1) * 16, :
            ]
    fill_halo(pad_ref, halo_ref)
    shifted_columns(pad_ref, cols_ref)
    act_ref[...] = conv(cols_ref, w_ref)
    back = dot(cot_ref[...], dw_ref[...], 0, 0)
    for j in range(8):
        jx, jy, jz = j // 4, j // 2 % 2, j % 2
        spots = [
            ((2 * ux + jx) * 8 + 2 * uy + jy) * 16 + jz * 8 for ux in range(4) for uy in range(4)
        ]
        a = jnp.concatenate([act_ref[pl.ds(s, 8), :] for s in spots], axis=0)
        g = 1.0 / (1.0 + jnp.exp(-a))
        patch_ref[:, pl.ds(j * LANES, LANES)] = (a * g).astype(BF16)
        slope = g * (1.0 + a * (1.0 - g))
        grad = back[:, j * LANES : (j + 1) * LANES] * slope
        for n, s in enumerate(spots):
            act_ref[pl.ds(s, 8), :] = grad[n * 8 : n * 8 + 8, :]
    grad_ref[...] = act_ref[...].astype(BF16)

    turned = act_ref[...].T[:C, :].astype(BF16)
    conv_ref[:, pl.ds(20 * LANES, LANES)] = jnp.zeros((C, LANES), F32)
    for tap in range(9):
        part = dot(turned, window(cols_ref, tap // 3, tap % 3))
        for dz in range(3):
            conv_ref[:, pl.ds((tap * 3 + dz) * C, C)] = part[:, dz * LANES : dz * LANES + C]
    part = dot(cot_ref[...], patch_ref[...])
    for j in range(8):
        down_ref[:, pl.ds(j * C, C)] = part[:, j * LANES : j * LANES + C]
    core = core_ref[0]
    for ref, half in ((keep_ref, core), (send_ref, 1 - core)):
        for lt in range(21):
            ref[pl.ds(lt * 48, 48), :] = conv_ref[
                pl.ds(pl.multiple_of(half * 48, 16), 48), pl.ds(lt * LANES, LANES)
            ].astype(ref.dtype)
        for lt in range(6):
            ref[pl.ds(CONV_ROWS + lt * 96, 96), :] = down_ref[
                pl.ds(pl.multiple_of(half * 96, 32), 96), pl.ds(lt * LANES, LANES)
            ].astype(ref.dtype)
        ref[pl.ds(1584, HALF_ROWS - 1584), :] = jnp.zeros((HALF_ROWS - 1584, LANES), ref.dtype)


def side_kernel(grad_ref, patch_ref, dw_ref, send_ref, coarse_ref, src_ref, row_ref):
    src_ref[...] = grad_ref[...].astype(F32)
    spread_rows(src_ref, row_ref, True)
    send_ref[...] = row_ref[...].astype(BF16)
    coarse_ref[...] = dot(dw_ref[...], patch_ref[...], 1, 1).astype(BF16)


def backward_kernel(grad_ref, halo_ref, w_ref, out_ref, pad_ref, cols_ref, act_ref):
    for x in range(SIDE):
        for y in range(SIDE):
            base = ((x + 1) * 10 + y + 1) * COL
            for par in range(2):
                pad_ref[pl.ds(base + 1 + par, 8, stride=2), :] = grad_ref[
                    pl.ds((x * 8 + y) * 16 + par * 8, 8), :
                ].astype(F32)
    fill_halo(pad_ref, halo_ref)
    shifted_columns(pad_ref, cols_ref)
    full = conv(cols_ref, w_ref)
    for n in range(64):
        for par in range(2):
            act_ref[pl.ds(n * 16 + par, 8, stride=2), :] = full[n * 16 + par * 8 : n * 16 + par * 8 + 8, :]
    out_ref[...] = act_ref[...].T[:C, :]


def finish_kernel(core_ref, mine_ref, other_ref, conv_ref, down_ref):
    def scale(first, last, count):
        total = jnp.zeros((8, LANES), F32)
        for ref in (mine_ref, other_ref):
            values = ref[pl.ds(first, last - first), :].astype(F32)
            total = total + jnp.sum((values * values).reshape(-1, 8, LANES), axis=0)
        return lax.rsqrt(jnp.sum(total, keepdims=True) * (1.0 / count) + EPSILON)

    conv_scale = scale(0, CONV_ROWS, C * 27 * C)
    down_scale = scale(CONV_ROWS, 1584, C2 * 8 * C)
    core = core_ref[0]
    for ref, half in ((mine_ref, core), (other_ref, 1 - core)):
        for lt in range(21):
            width = min(LANES, 27 * C - lt * LANES)
            values = ref[pl.ds(lt * 48, 48), :].astype(F32) * conv_scale
            conv_ref[pl.ds(pl.multiple_of(half * 48, 16), 48), pl.ds(lt * LANES, width)] = values[:, :width]
        for lt in range(6):
            values = ref[pl.ds(CONV_ROWS + lt * 96, 96), :].astype(F32) * down_scale
            down_ref[pl.ds(pl.multiple_of(half * 96, 32), 96), pl.ds(lt * LANES, LANES)] = values


def here(rows):
    return pltpu.with_memory_space_constraint(rows, pltpu.VMEM)


def call(body, outs, scratch=(), scalars=0, ins=0, name=None):
    specs = [pl.BlockSpec(memory_space=pltpu.SMEM)] * scalars + [
        pl.BlockSpec(memory_space=pltpu.VMEM)
    ] * ins
    return pl.pallas_call(
        body,
        out_shape=[
            jax.ShapeDtypeStruct(shape, kind) if leaves else pltpu.VMEM(shape, kind)
            for shape, kind, *leaves in outs
        ],
        in_specs=specs,
        out_specs=[pl.BlockSpec(memory_space=pltpu.VMEM)] * len(outs),
        scratch_shapes=list(scratch),
        compiler_params=PARAMS,
        name=name,
    )


CHIPS = ("y", "z")
SPACE = ("y", "z", "c")


def trade(rows, axes):
    return lax.all_to_all(rows, axes, 0, 0, tiled=True)


def shards(features, cotangent, conv_weight, down_weight, neighbours):
    block = features[0, 0]
    cot = cotangent[0, 0]
    core = lax.axis_index("c").astype(jnp.int32).reshape(1)
    rows_shape = ((SLOTS, LANES), BF16)
    by_chip = (32, 32, LANES)
    row_scratch = pltpu.VMEM((SLOTS, LANES), F32)

    def swap(rows):
        return lax.ppermute(rows, "c", [(0, 1), (1, 0)])

    (spread,) = call(spread_kernel, [rows_shape], [row_scratch, row_scratch], scalars=1, ins=1, name="spread")(
        neighbours[0], block
    )
    middle = here(trade(spread.reshape(by_chip), CHIPS))
    route = call(route_kernel, [(by_chip, BF16)], [pltpu.VMEM(by_chip, F32)], scalars=1, ins=3, name="route")
    (routed,) = route(core, middle, middle, here(swap(middle)))
    halo = trade(routed, CHIPS).reshape(SLOTS, LANES)

    taps = conv_weight.reshape(C, 27, C)
    pad = ((0, 0), (0, LANES - C), (0, LANES - C))
    forward_w = jnp.pad(taps.transpose(1, 2, 0), pad).reshape(9, 3 * LANES, LANES)
    backward_w = jnp.pad(taps.transpose(1, 0, 2)[::-1], pad).reshape(9, 3 * LANES, LANES)
    down_w = jnp.pad(down_weight.reshape(C2, 8, C), ((0, 0), (0, 0), (0, LANES - C))).reshape(C2, 8 * LANES)
    halo, forward_w, backward_w, down_w = lax.optimization_barrier((halo, forward_w, backward_w, down_w))
    forward_w, backward_w, down_w = here(forward_w), here(backward_w), here(down_w)

    pad_scratch = pltpu.VMEM((100 * COL, LANES), F32)
    cols_scratch = pltpu.VMEM((10, 10, DEPTH, 3 * LANES), BF16)
    grad, patch, keep, send = call(
        forward_kernel,
        [rows_shape, ((LANES, 8 * LANES), BF16), ((HALF_ROWS, LANES), F32), ((HALF_ROWS, LANES), BF16)],
        [pad_scratch, cols_scratch, row_scratch, pltpu.VMEM((C, 21 * LANES), F32), pltpu.VMEM((C2, 8 * C), F32)],
        scalars=1,
        ins=5,
        name="forward",
    )(core, block, here(halo), cot, forward_w, down_w)
    spread2, coarse = call(
        side_kernel, [rows_shape, ((C2, LANES), BF16, True)], [row_scratch, row_scratch], ins=3, name="side"
    )(grad, patch, down_w)

    pair = (keep + swap(send).astype(F32)).astype(BF16)
    out = jnp.concatenate([spread2.reshape(by_chip), pair.reshape(32, 56, LANES)], axis=1)
    got = trade(out, CHIPS)
    middle2 = got[:, :32]
    part = jnp.sum(got[:, 32:].astype(F32), axis=0)
    other2, part = lax.optimization_barrier((swap(middle2), part))
    line = trade(jnp.broadcast_to(part, (4, 56, LANES)), "x")
    whole = jnp.sum(line, axis=0).astype(BF16)
    (routed2,) = route(core, middle, here(middle2), here(other2))
    out = jnp.concatenate([routed2, jnp.broadcast_to(whole, (32, 56, LANES))], axis=1)
    got = trade(out, CHIPS)
    halo2 = got[:, :32].reshape(SLOTS, LANES)
    mine = got[:, 32:].reshape(HALF_ROWS, LANES)
    theirs = swap(mine)
    (grad_features,) = call(
        backward_kernel,
        [((C, VOX), F32, True)],
        [pad_scratch, cols_scratch, row_scratch],
        ins=3,
        name="backward",
    )(grad, here(halo2), backward_w)
    grad_conv, grad_down = call(
        finish_kernel, [((C, 27 * C), F32, True), ((C2, 8 * C), F32, True)], scalars=1, ins=2, name="finish"
    )(core, here(mine), here(theirs))
    return coarse[None, None], grad_features[None, None], grad_conv, grad_down


def solution(mesh):
    devices = mesh.devices
    fine = Mesh(devices.reshape(devices.shape[0], 4, -1, 2), ("x", "y", "z", "c"))
    block = P("x", SPACE, None, None)
    return jax.shard_map(
        shards,
        mesh=fine,
        in_specs=(block, block, P(), P(), P("x", SPACE, None)),
        out_specs=(block, block, P(), P()),
        check_vma=False,
    )
```

```python
import jax
import jax.numpy as jnp
from jax import lax
from jax.experimental import pallas as pl
from jax.experimental.pallas import tpu as pltpu
from jax.sharding import Mesh, PartitionSpec as P

C = 96
C2 = 192
SIDE = 8
DEPTH = 16
VOX = 1024
LANES = 128
SLOTS = 1024
COL = 24
HALF_ROWS = 1792
CONV_ROWS = 1008
EPSILON = 1e-06
F32 = jnp.float32
BF16 = jnp.bfloat16
PARAMS = pltpu.CompilerParams(vmem_limit_bytes=32 << 20)


RIM = [(x, y) for x in range(10) for y in range(10) if x in (0, 9) or y in (0, 9)]


def side(position, extent):
    if position == 0:
        return -1, extent - 1
    if position == extent + 1:
        return 1, 0
    return 0, position - 1


def direction(ex, ey, ez):
    place = ((ex + 1) * 3 + ey + 1) * 3 + ez + 1
    return place - (place > 13)


def one_hot(index, count):
    wide = lax.broadcasted_iota(jnp.int32, (index.shape[0], count), 1)
    return jnp.where(wide == index, 1.0, 0.0).astype(BF16)


def dot(a, b, ca=1, cb=0):
    return lax.dot_general(a, b, (((ca,), (cb,)), ((), ())), preferred_element_type=F32)


def spread_rows(src_ref, out_ref, parity):
    for place, (px, py) in enumerate(RIM):
        base = (side(px, SIDE)[1] * SIDE + side(py, SIDE)[1]) * DEPTH
        first = place * COL
        if parity:
            for par in range(2):
                out_ref[pl.ds(first + 1 + par, 8, stride=2), :] = src_ref[pl.ds(base + par * 8, 8), :]
        else:
            out_ref[pl.ds(first + 1, DEPTH), :] = src_ref[pl.ds(base, DEPTH), :]
        out_ref[pl.ds(first, 1), :] = src_ref[pl.ds(base + 15, 1), :]
        out_ref[pl.ds(first + 17, 1), :] = src_ref[pl.ds(base, 1), :]
        out_ref[pl.ds(first + 18, 6), :] = jnp.zeros((6, LANES), F32)
    for x in range(SIDE):
        out_ref[pl.ds(864 + x * 8, 8), :] = src_ref[pl.ds(x * 128 + 15, 8, stride=DEPTH), :]
        out_ref[pl.ds(928 + x * 8, 8), :] = src_ref[pl.ds(x * 128, 8, stride=DEPTH), :]
    out_ref[pl.ds(992, 32), :] = jnp.zeros((32, LANES), F32)


def lanes_of(rows):
    return lax.broadcasted_iota(jnp.int32, rows.shape, len(rows.shape) - 1)


def pack(row_ref, out_ref):
    extra = row_ref[:, 24:32]
    for part in range(3):
        rows = row_ref[:, part * 8 : part * 8 + 8]
        moved = pltpu.roll(extra, C - 32 * part, 2)
        out_ref[:, part * 8 : part * 8 + 8] = jnp.where(lanes_of(rows) < C, rows, moved).astype(BF16)


def slot_groups(ref):
    rows = ref[...].astype(F32)
    count = rows.shape[1] // 8
    groups = [rows[:, g * 8 : g * 8 + 8] for g in range(count)]
    if count == 3:
        lane = lanes_of(groups[0])
        moved = [pltpu.roll(rows, 32 * (part + 1), 2) for part, rows in enumerate(groups)]
        groups.append(jnp.where(lane < 32, moved[0], jnp.where(lane < 64, moved[1], moved[2])))
    return groups


def spread_kernel(nbr_hbm, f_hbm, out_ref, nbr_ref, f_ref, sems, src_ref, row_ref):
    copies = [
        pltpu.make_async_copy(nbr_hbm, nbr_ref, sems.at[0]),
        pltpu.make_async_copy(f_hbm, f_ref, sems.at[1]),
    ]
    for copy in copies:
        copy.start()
    for copy in copies:
        copy.wait()
    wide = jnp.concatenate([f_ref[...].astype(F32), jnp.zeros((LANES - C, VOX), F32)], axis=0)
    src_ref[...] = wide.T
    spread_rows(src_ref, row_ref, False)

    def owner(ex, ey, ez):
        return nbr_ref[0, direction(ex, ey, ez)].astype(F32)

    lane = lax.broadcasted_iota(jnp.int32, (COL, LANES), 1)
    z = lax.broadcasted_iota(jnp.int32, (COL, LANES), 0)
    for place, (px, py) in enumerate(RIM):
        ex, ey = side(px, SIDE)[0], side(py, SIDE)[0]
        low, mid, high = (owner(ex, ey, ez) for ez in (-1, 0, 1))
        held = jnp.where(z == 0, low, jnp.where(z < 17, mid, jnp.where(z == 17, high, -1.0)))
        rows = pl.ds(place * COL, COL)
        row_ref[rows, :] = jnp.where(lane >= C, held, row_ref[rows, :])
    lane = lax.broadcasted_iota(jnp.int32, (64, LANES), 1)
    for first, ez in ((864, -1), (928, 1)):
        rows = pl.ds(first, 64)
        row_ref[rows, :] = jnp.where(lane >= C, owner(0, 0, ez), row_ref[rows, :])
    out_ref[...] = row_ref[...].astype(BF16)


def route_kernel(core_ref, owner_ref, mine_ref, other_ref, out_ref, row_ref):
    core = core_ref[0]
    owners, mine, other = slot_groups(owner_ref), slot_groups(mine_ref), slot_groups(other_ref)
    for group in range(4):
        owner = owners[group].reshape(256, LANES)[:, C : C + 1].astype(jnp.int32)
        place = lax.broadcasted_iota(jnp.int32, (256, 1), 0) & 7
        held = jnp.bitwise_and(owner, 1)
        spot = lax.shift_right_arithmetic(owner, 1) * 8 + place + jnp.where(held == core, 0, 256)
        spot = jnp.where(owner < 0, -1, spot)
        source = jnp.concatenate(
            [mine[group].reshape(256, LANES), other[group].reshape(256, LANES)], axis=0
        ).astype(BF16)
        row_ref[:, group * 8 : group * 8 + 8] = dot(one_hot(spot, 512), source).reshape(32, 8, LANES)
    pack(row_ref, out_ref)


def fill_halo(pad_ref, packed_ref, row_ref):
    for group, rows in enumerate(slot_groups(packed_ref)):
        row_ref[:, group * 8 : group * 8 + 8] = rows
    halo_ref = row_ref.reshape(SLOTS, LANES)

    def put(first, count, place):
        pad_ref[pl.ds(first * COL, count * COL), :] = halo_ref[pl.ds(place * COL, count * COL), :]

    put(0, 11, 0)
    for x in range(1, 8):
        put(x * 10 + 9, 2, 11 + 2 * (x - 1))
    put(89, 11, 25)
    for x in range(SIDE):
        start = ((x + 1) * 10 + 1) * COL
        pad_ref[pl.ds(start, 8, stride=COL), :] = halo_ref[pl.ds(864 + x * 8, 8), :]
        pad_ref[pl.ds(start + DEPTH + 1, 8, stride=COL), :] = halo_ref[pl.ds(928 + x * 8, 8), :]


def shifted_columns(pad_ref, cols_ref):
    for x in range(10):
        for y in range(10):
            base = (x * 10 + y) * COL
            rows = [pad_ref[pl.ds(base + s, 8, stride=2), :] for s in range(4)]
            for dz in range(3):
                cols_ref[x, y, :, pl.ds(dz * LANES, LANES)] = jnp.concatenate(
                    [rows[dz], rows[dz + 1]], axis=0
                ).astype(BF16)


def window(cols_ref, dx, dy):
    return cols_ref[dx : dx + 8, dy : dy + 8].reshape(VOX, 3 * LANES)


def conv(cols_ref, w_ref):
    total = None
    for tap in range(9):
        part = dot(window(cols_ref, tap // 3, tap % 3), w_ref[tap])
        total = part if total is None else total + part
    return total


def forward_kernel(
    core_ref, f_ref, halo_ref, cot_ref, w_ref, dw_ref,
    grad_ref, patch_ref, keep_ref, send_ref,
    pad_ref, cols_ref, act_ref, row_ref, conv_ref, down_ref,
):
    wide = jnp.concatenate([f_ref[...].astype(F32), jnp.zeros((LANES - C, VOX), F32)], axis=0)
    own = wide.T
    for x in range(SIDE):
        for y in range(SIDE):
            pad_ref[pl.ds(((x + 1) * 10 + y + 1) * COL + 1, DEPTH), :] = own[
                (x * 8 + y) * 16 : (x * 8 + y + 1) * 16, :
            ]
    fill_halo(pad_ref, halo_ref, row_ref)
    shifted_columns(pad_ref, cols_ref)
    act_ref[...] = conv(cols_ref, w_ref)
    back = dot(cot_ref[...], dw_ref[...], 0, 0)
    for j in range(8):
        jx, jy, jz = j // 4, j // 2 % 2, j % 2
        spots = [
            ((2 * ux + jx) * 8 + 2 * uy + jy) * 16 + jz * 8 for ux in range(4) for uy in range(4)
        ]
        a = jnp.concatenate([act_ref[pl.ds(s, 8), :] for s in spots], axis=0)
        g = 1.0 / (1.0 + jnp.exp(-a))
        patch_ref[:, pl.ds(j * LANES, LANES)] = (a * g).astype(BF16)
        slope = g * (1.0 + a * (1.0 - g))
        grad = back[:, j * LANES : (j + 1) * LANES] * slope
        for n, s in enumerate(spots):
            act_ref[pl.ds(s, 8), :] = grad[n * 8 : n * 8 + 8, :]
    grad_ref[...] = act_ref[...].astype(BF16)

    turned = act_ref[...].T[:C, :].astype(BF16)
    conv_ref[:, pl.ds(20 * LANES, LANES)] = jnp.zeros((C, LANES), F32)
    for tap in range(9):
        part = dot(turned, window(cols_ref, tap // 3, tap % 3))
        for dz in range(3):
            conv_ref[:, pl.ds((tap * 3 + dz) * C, C)] = part[:, dz * LANES : dz * LANES + C]
    part = dot(cot_ref[...], patch_ref[...])
    for j in range(8):
        down_ref[:, pl.ds(j * C, C)] = part[:, j * LANES : j * LANES + C]
    core = core_ref[0]
    for ref, half in ((keep_ref, core), (send_ref, 1 - core)):
        for lt in range(21):
            ref[pl.ds(lt * 48, 48), :] = conv_ref[
                pl.ds(pl.multiple_of(half * 48, 16), 48), pl.ds(lt * LANES, LANES)
            ].astype(ref.dtype)
        for lt in range(6):
            ref[pl.ds(CONV_ROWS + lt * 96, 96), :] = down_ref[
                pl.ds(pl.multiple_of(half * 96, 32), 96), pl.ds(lt * LANES, LANES)
            ].astype(ref.dtype)
        ref[pl.ds(1584, HALF_ROWS - 1584), :] = jnp.zeros((HALF_ROWS - 1584, LANES), ref.dtype)


def side_kernel(grad_ref, patch_ref, dw_ref, send_ref, coarse_ref, src_ref, row_ref):
    src_ref[...] = grad_ref[...].astype(F32)
    spread_rows(src_ref, row_ref.reshape(SLOTS, LANES), True)
    pack(row_ref, send_ref)
    coarse_ref[...] = dot(dw_ref[...], patch_ref[...], 1, 1).astype(BF16)


def backward_kernel(grad_ref, halo_ref, w_ref, out_ref, pad_ref, cols_ref, act_ref, row_ref):
    for x in range(SIDE):
        for y in range(SIDE):
            base = ((x + 1) * 10 + y + 1) * COL
            for par in range(2):
                pad_ref[pl.ds(base + 1 + par, 8, stride=2), :] = grad_ref[
                    pl.ds((x * 8 + y) * 16 + par * 8, 8), :
                ].astype(F32)
    fill_halo(pad_ref, halo_ref, row_ref)
    shifted_columns(pad_ref, cols_ref)
    full = conv(cols_ref, w_ref)
    for n in range(64):
        for par in range(2):
            act_ref[pl.ds(n * 16 + par, 8, stride=2), :] = full[n * 16 + par * 8 : n * 16 + par * 8 + 8, :]
    out_ref[...] = act_ref[...].T[:C, :]


def finish_kernel(core_ref, mine_ref, other_ref, conv_ref, down_ref):
    def scale(first, last, count):
        total = jnp.zeros((8, LANES), F32)
        for ref in (mine_ref, other_ref):
            values = ref[pl.ds(first, last - first), :].astype(F32)
            total = total + jnp.sum((values * values).reshape(-1, 8, LANES), axis=0)
        return lax.rsqrt(jnp.sum(total, keepdims=True) * (1.0 / count) + EPSILON)

    conv_scale = scale(0, CONV_ROWS, C * 27 * C)
    down_scale = scale(CONV_ROWS, 1584, C2 * 8 * C)
    core = core_ref[0]
    for ref, half in ((mine_ref, core), (other_ref, 1 - core)):
        for lt in range(21):
            width = min(LANES, 27 * C - lt * LANES)
            values = ref[pl.ds(lt * 48, 48), :].astype(F32) * conv_scale
            conv_ref[pl.ds(pl.multiple_of(half * 48, 16), 48), pl.ds(lt * LANES, width)] = values[:, :width]
        for lt in range(6):
            values = ref[pl.ds(CONV_ROWS + lt * 96, 96), :].astype(F32) * down_scale
            down_ref[pl.ds(pl.multiple_of(half * 96, 32), 96), pl.ds(lt * LANES, LANES)] = values


def here(rows):
    return pltpu.with_memory_space_constraint(rows, pltpu.VMEM)


def call(body, outs, scratch=(), scalars=0, ins=0, name=None):
    specs = [pl.BlockSpec(memory_space=pltpu.SMEM)] * scalars + [
        pl.BlockSpec(memory_space=pltpu.VMEM)
    ] * ins
    return pl.pallas_call(
        body,
        out_shape=[
            jax.ShapeDtypeStruct(shape, kind) if leaves else pltpu.VMEM(shape, kind)
            for shape, kind, *leaves in outs
        ],
        in_specs=specs,
        out_specs=[pl.BlockSpec(memory_space=pltpu.VMEM)] * len(outs),
        scratch_shapes=list(scratch),
        compiler_params=PARAMS,
        name=name,
    )


CHIPS = ("y", "z")
SPACE = ("y", "z", "c")


def trade(rows, axes):
    return lax.all_to_all(rows, axes, 0, 0, tiled=True)


def shards(features, cotangent, conv_weight, down_weight, neighbours):
    block = features[0, 0]
    cot = cotangent[0, 0]
    core = lax.axis_index("c").astype(jnp.int32).reshape(1)
    rows_shape = ((SLOTS, LANES), BF16)
    by_chip = (32, 32, LANES)
    packed = (32, 24, LANES)
    flat_scratch = pltpu.VMEM((SLOTS, LANES), F32)
    slot_scratch = pltpu.VMEM(by_chip, F32)

    def swap(rows):
        return lax.ppermute(rows, "c", [(0, 1), (1, 0)])

    (spread,) = pl.pallas_call(
        spread_kernel,
        out_shape=[pltpu.VMEM(*rows_shape)],
        in_specs=[pl.BlockSpec(memory_space=pltpu.HBM)] * 2,
        out_specs=[pl.BlockSpec(memory_space=pltpu.VMEM)],
        scratch_shapes=[
            pltpu.SMEM((1, 26), jnp.int32),
            pltpu.VMEM((C, VOX), BF16),
            pltpu.SemaphoreType.DMA((2,)),
            flat_scratch,
            flat_scratch,
        ],
        compiler_params=PARAMS,
        name="spread",
    )(neighbours[0], block)
    middle = here(trade(spread.reshape(by_chip), CHIPS))
    route = call(route_kernel, [(packed, BF16)], [slot_scratch], scalars=1, ins=3, name="route")
    (routed,) = route(core, middle, middle, here(swap(middle)))
    halo = trade(routed, CHIPS)

    taps = conv_weight.reshape(C, 27, C)
    pad = ((0, 0), (0, LANES - C), (0, LANES - C))
    forward_w = jnp.pad(taps.transpose(1, 2, 0), pad).reshape(9, 3 * LANES, LANES)
    backward_w = jnp.pad(taps.transpose(1, 0, 2)[::-1], pad).reshape(9, 3 * LANES, LANES)
    down_w = jnp.pad(down_weight.reshape(C2, 8, C), ((0, 0), (0, 0), (0, LANES - C))).reshape(C2, 8 * LANES)
    halo, forward_w, backward_w, down_w = lax.optimization_barrier((halo, forward_w, backward_w, down_w))
    forward_w, backward_w, down_w = here(forward_w), here(backward_w), here(down_w)

    pad_scratch = pltpu.VMEM((100 * COL, LANES), F32)
    cols_scratch = pltpu.VMEM((10, 10, DEPTH, 3 * LANES), BF16)
    grad, patch, keep, send = call(
        forward_kernel,
        [rows_shape, ((LANES, 8 * LANES), BF16), ((HALF_ROWS, LANES), F32), ((HALF_ROWS, LANES), BF16)],
        [pad_scratch, cols_scratch, flat_scratch, slot_scratch, pltpu.VMEM((C, 21 * LANES), F32), pltpu.VMEM((C2, 8 * C), F32)],
        scalars=1,
        ins=5,
        name="forward",
    )(core, block, here(halo), cot, forward_w, down_w)
    spread2, coarse = call(
        side_kernel, [(packed, BF16), ((C2, LANES), BF16, True)], [flat_scratch, slot_scratch], ins=3, name="side"
    )(grad, patch, down_w)

    pair = (keep + swap(send).astype(F32)).astype(BF16)
    out = jnp.concatenate([spread2, pair.reshape(32, 56, LANES)], axis=1)
    got = trade(out, CHIPS)
    middle2 = got[:, :24]
    part = jnp.sum(got[:, 24:].astype(F32), axis=0)
    other2, part = lax.optimization_barrier((swap(middle2), part))
    line = trade(jnp.broadcast_to(part, (4, 56, LANES)), "x")
    whole = jnp.sum(line, axis=0).astype(BF16)
    (routed2,) = route(core, middle, here(middle2), here(other2))
    out = jnp.concatenate([routed2, jnp.broadcast_to(whole, (32, 56, LANES))], axis=1)
    got = trade(out, CHIPS)
    halo2 = got[:, :24]
    mine = got[:, 24:].reshape(HALF_ROWS, LANES)
    theirs = swap(mine)
    (grad_features,) = call(
        backward_kernel,
        [((C, VOX), F32, True)],
        [pad_scratch, cols_scratch, flat_scratch, slot_scratch],
        ins=3,
        name="backward",
    )(grad, here(halo2), backward_w)
    grad_conv, grad_down = call(
        finish_kernel, [((C, 27 * C), F32, True), ((C2, 8 * C), F32, True)], scalars=1, ins=2, name="finish"
    )(core, here(mine), here(theirs))
    return coarse[None, None], grad_features[None, None], grad_conv, grad_down


def solution(mesh):
    devices = mesh.devices
    fine = Mesh(devices.reshape(devices.shape[0], 4, -1, 2), ("x", "y", "z", "c"))
    block = P("x", SPACE, None, None)
    return jax.shard_map(
        shards,
        mesh=fine,
        in_specs=(block, block, P(), P(), P("x", SPACE, None)),
        out_specs=(block, block, P(), P()),
        check_vma=False,
    )
```

```python
import jax
import jax.numpy as jnp
from jax import lax
from jax.experimental import pallas as pl
from jax.experimental.pallas import tpu as pltpu
from jax.sharding import Mesh, PartitionSpec as P

C = 96
C2 = 192
SIDE = 8
DEPTH = 16
VOX = 1024
LANES = 128
SLOTS = 1024
COL = 24
HALF_ROWS = 1792
CONV_ROWS = 1008
EPSILON = 1e-06
F32 = jnp.float32
BF16 = jnp.bfloat16
PARAMS = pltpu.CompilerParams(vmem_limit_bytes=32 << 20)


RIM = [(x, y) for x in range(10) for y in range(10) if x in (0, 9) or y in (0, 9)]


def side(position, extent):
    if position == 0:
        return -1, extent - 1
    if position == extent + 1:
        return 1, 0
    return 0, position - 1


def direction(ex, ey, ez):
    place = ((ex + 1) * 3 + ey + 1) * 3 + ez + 1
    return place - (place > 13)


def one_hot(index, count):
    wide = lax.broadcasted_iota(jnp.int32, (index.shape[0], count), 1)
    return jnp.where(wide == index, 1.0, 0.0).astype(BF16)


def dot(a, b, ca=1, cb=0):
    return lax.dot_general(a, b, (((ca,), (cb,)), ((), ())), preferred_element_type=F32)


def spread_rows(src_ref, out_ref, parity):
    for place, (px, py) in enumerate(RIM):
        base = (side(px, SIDE)[1] * SIDE + side(py, SIDE)[1]) * DEPTH
        first = place * COL
        if parity:
            for par in range(2):
                out_ref[pl.ds(first + 1 + par, 8, stride=2), :] = src_ref[pl.ds(base + par * 8, 8), :]
        else:
            out_ref[pl.ds(first + 1, DEPTH), :] = src_ref[pl.ds(base, DEPTH), :]
        out_ref[pl.ds(first, 1), :] = src_ref[pl.ds(base + 15, 1), :]
        out_ref[pl.ds(first + 17, 1), :] = src_ref[pl.ds(base, 1), :]
        out_ref[pl.ds(first + 18, 6), :] = jnp.zeros((6, LANES), F32)
    for x in range(SIDE):
        out_ref[pl.ds(864 + x * 8, 8), :] = src_ref[pl.ds(x * 128 + 15, 8, stride=DEPTH), :]
        out_ref[pl.ds(928 + x * 8, 8), :] = src_ref[pl.ds(x * 128, 8, stride=DEPTH), :]
    out_ref[pl.ds(992, 32), :] = jnp.zeros((32, LANES), F32)


def lanes_of(rows):
    return lax.broadcasted_iota(jnp.int32, rows.shape, len(rows.shape) - 1)


def pack(row_ref, out_ref):
    extra = row_ref[:, 24:32]
    for part in range(3):
        rows = row_ref[:, part * 8 : part * 8 + 8]
        moved = pltpu.roll(extra, C - 32 * part, 2)
        out_ref[:, part * 8 : part * 8 + 8] = jnp.where(lanes_of(rows) < C, rows, moved).astype(BF16)


def slot_groups(ref):
    rows = ref[...].astype(F32)
    count = rows.shape[1] // 8
    groups = [rows[:, g * 8 : g * 8 + 8] for g in range(count)]
    if count == 3:
        lane = lanes_of(groups[0])
        moved = [pltpu.roll(rows, 32 * (part + 1), 2) for part, rows in enumerate(groups)]
        groups.append(jnp.where(lane < 32, moved[0], jnp.where(lane < 64, moved[1], moved[2])))
    return groups


def spread_kernel(nbr_hbm, f_hbm, out_ref, nbr_ref, f_ref, sems, src_ref, row_ref):
    copies = [
        pltpu.make_async_copy(nbr_hbm, nbr_ref, sems.at[0]),
        pltpu.make_async_copy(f_hbm, f_ref, sems.at[1]),
    ]
    for copy in copies:
        copy.start()
    for copy in copies:
        copy.wait()
    wide = jnp.concatenate([f_ref[...].astype(F32), jnp.zeros((LANES - C, VOX), F32)], axis=0)
    src_ref[...] = wide.T
    spread_rows(src_ref, row_ref, False)

    def owner(ex, ey, ez):
        return nbr_ref[0, direction(ex, ey, ez)].astype(F32)

    lane = lax.broadcasted_iota(jnp.int32, (COL, LANES), 1)
    z = lax.broadcasted_iota(jnp.int32, (COL, LANES), 0)
    for place, (px, py) in enumerate(RIM):
        ex, ey = side(px, SIDE)[0], side(py, SIDE)[0]
        low, mid, high = (owner(ex, ey, ez) for ez in (-1, 0, 1))
        held = jnp.where(z == 0, low, jnp.where(z < 17, mid, jnp.where(z == 17, high, -1.0)))
        rows = pl.ds(place * COL, COL)
        row_ref[rows, :] = jnp.where(lane >= C, held, row_ref[rows, :])
    lane = lax.broadcasted_iota(jnp.int32, (64, LANES), 1)
    for first, ez in ((864, -1), (928, 1)):
        rows = pl.ds(first, 64)
        row_ref[rows, :] = jnp.where(lane >= C, owner(0, 0, ez), row_ref[rows, :])
    out_ref[...] = row_ref[...].astype(BF16)


def route_kernel(core_ref, owner_ref, mine_ref, other_ref, out_ref, row_ref):
    core = core_ref[0]
    owners, mine, other = slot_groups(owner_ref), slot_groups(mine_ref), slot_groups(other_ref)
    for group in range(4):
        owner = owners[group].reshape(256, LANES)[:, C : C + 1].astype(jnp.int32)
        place = lax.broadcasted_iota(jnp.int32, (256, 1), 0) & 7
        held = jnp.bitwise_and(owner, 1)
        spot = lax.shift_right_arithmetic(owner, 1) * 8 + place + jnp.where(held == core, 0, 256)
        spot = jnp.where(owner < 0, -1, spot)
        source = jnp.concatenate(
            [mine[group].reshape(256, LANES), other[group].reshape(256, LANES)], axis=0
        ).astype(BF16)
        row_ref[:, group * 8 : group * 8 + 8] = dot(one_hot(spot, 512), source).reshape(32, 8, LANES)
    pack(row_ref, out_ref)


def fill_halo(pad_ref, packed_ref, row_ref):
    for group, rows in enumerate(slot_groups(packed_ref)):
        row_ref[:, group * 8 : group * 8 + 8] = rows
    halo_ref = row_ref.reshape(SLOTS, LANES)

    def put(first, count, place):
        pad_ref[pl.ds(first * COL, count * COL), :] = halo_ref[pl.ds(place * COL, count * COL), :]

    put(0, 11, 0)
    for x in range(1, 8):
        put(x * 10 + 9, 2, 11 + 2 * (x - 1))
    put(89, 11, 25)
    for x in range(SIDE):
        start = ((x + 1) * 10 + 1) * COL
        pad_ref[pl.ds(start, 8, stride=COL), :] = halo_ref[pl.ds(864 + x * 8, 8), :]
        pad_ref[pl.ds(start + DEPTH + 1, 8, stride=COL), :] = halo_ref[pl.ds(928 + x * 8, 8), :]


def shifted_columns(pad_ref, cols_ref):
    for x in range(10):
        for y in range(10):
            base = (x * 10 + y) * COL
            rows = [pad_ref[pl.ds(base + s, 8, stride=2), :] for s in range(4)]
            for dz in range(3):
                cols_ref[x, y, :, pl.ds(dz * LANES, LANES)] = jnp.concatenate(
                    [rows[dz], rows[dz + 1]], axis=0
                ).astype(BF16)


def window(cols_ref, dx, dy):
    return cols_ref[dx : dx + 8, dy : dy + 8].reshape(VOX, 3 * LANES)


def conv(cols_ref, w_ref):
    total = None
    for tap in range(9):
        part = dot(window(cols_ref, tap // 3, tap % 3), w_ref[tap])
        total = part if total is None else total + part
    return total


def forward_kernel(
    core_ref, f_ref, halo_ref, cot_ref, w_ref, dw_ref,
    grad_ref, patch_ref, keep_ref, send_ref,
    pad_ref, cols_ref, act_ref, row_ref, conv_ref, down_ref,
):
    wide = jnp.concatenate([f_ref[...].astype(F32), jnp.zeros((LANES - C, VOX), F32)], axis=0)
    own = wide.T
    for x in range(SIDE):
        for y in range(SIDE):
            pad_ref[pl.ds(((x + 1) * 10 + y + 1) * COL + 1, DEPTH), :] = own[
                (x * 8 + y) * 16 : (x * 8 + y + 1) * 16, :
            ]
    fill_halo(pad_ref, halo_ref, row_ref)
    shifted_columns(pad_ref, cols_ref)
    act_ref[...] = conv(cols_ref, w_ref)
    back = dot(cot_ref[...], dw_ref[...], 0, 0)
    for j in range(8):
        jx, jy, jz = j // 4, j // 2 % 2, j % 2
        spots = [
            ((2 * ux + jx) * 8 + 2 * uy + jy) * 16 + jz * 8 for ux in range(4) for uy in range(4)
        ]
        a = jnp.concatenate([act_ref[pl.ds(s, 8), :] for s in spots], axis=0)
        g = 1.0 / (1.0 + jnp.exp(-a))
        patch_ref[:, pl.ds(j * LANES, LANES)] = (a * g).astype(BF16)
        slope = g * (1.0 + a * (1.0 - g))
        grad = back[:, j * LANES : (j + 1) * LANES] * slope
        for n, s in enumerate(spots):
            act_ref[pl.ds(s, 8), :] = grad[n * 8 : n * 8 + 8, :]
    grad_ref[...] = act_ref[...].astype(BF16)

    turned = act_ref[...].T[:C, :].astype(BF16)
    conv_ref[:, pl.ds(20 * LANES, LANES)] = jnp.zeros((C, LANES), F32)
    for tap in range(9):
        part = dot(turned, window(cols_ref, tap // 3, tap % 3))
        for dz in range(3):
            conv_ref[:, pl.ds((tap * 3 + dz) * C, C)] = part[:, dz * LANES : dz * LANES + C]
    part = dot(cot_ref[...], patch_ref[...])
    for j in range(8):
        down_ref[:, pl.ds(j * C, C)] = part[:, j * LANES : j * LANES + C]
    core = core_ref[0]
    for ref, half in ((keep_ref, core), (send_ref, 1 - core)):
        for lt in range(21):
            ref[pl.ds(lt * 48, 48), :] = conv_ref[
                pl.ds(pl.multiple_of(half * 48, 16), 48), pl.ds(lt * LANES, LANES)
            ].astype(ref.dtype)
        for lt in range(6):
            ref[pl.ds(CONV_ROWS + lt * 96, 96), :] = down_ref[
                pl.ds(pl.multiple_of(half * 96, 32), 96), pl.ds(lt * LANES, LANES)
            ].astype(ref.dtype)
        ref[pl.ds(1584, HALF_ROWS - 1584), :] = jnp.zeros((HALF_ROWS - 1584, LANES), ref.dtype)


def side_kernel(grad_ref, patch_ref, dw_ref, send_ref, coarse_ref, src_ref, row_ref):
    src_ref[...] = grad_ref[...].astype(F32)
    spread_rows(src_ref, row_ref.reshape(SLOTS, LANES), True)
    pack(row_ref, send_ref)
    coarse_ref[...] = dot(dw_ref[...], patch_ref[...], 1, 1).astype(BF16)


def backward_kernel(grad_ref, halo_ref, w_ref, out_ref, pad_ref, cols_ref, act_ref, row_ref):
    for x in range(SIDE):
        for y in range(SIDE):
            base = ((x + 1) * 10 + y + 1) * COL
            for par in range(2):
                pad_ref[pl.ds(base + 1 + par, 8, stride=2), :] = grad_ref[
                    pl.ds((x * 8 + y) * 16 + par * 8, 8), :
                ].astype(F32)
    fill_halo(pad_ref, halo_ref, row_ref)
    shifted_columns(pad_ref, cols_ref)
    full = conv(cols_ref, w_ref)
    for n in range(64):
        for par in range(2):
            act_ref[pl.ds(n * 16 + par, 8, stride=2), :] = full[n * 16 + par * 8 : n * 16 + par * 8 + 8, :]
    out_ref[...] = act_ref[...].T[:C, :]


def finish_kernel(core_ref, mine_ref, other_ref, conv_ref, down_ref):
    def scale(first, last, count):
        total = jnp.zeros((8, LANES), F32)
        for ref in (mine_ref, other_ref):
            values = ref[pl.ds(first, last - first), :].astype(F32)
            total = total + jnp.sum((values * values).reshape(-1, 8, LANES), axis=0)
        return lax.rsqrt(jnp.sum(total, keepdims=True) * (1.0 / count) + EPSILON)

    conv_scale = scale(0, CONV_ROWS, C * 27 * C)
    down_scale = scale(CONV_ROWS, 1584, C2 * 8 * C)
    core = core_ref[0]
    for ref, half in ((mine_ref, core), (other_ref, 1 - core)):
        for lt in range(21):
            width = min(LANES, 27 * C - lt * LANES)
            values = ref[pl.ds(lt * 48, 48), :].astype(F32) * conv_scale
            conv_ref[pl.ds(pl.multiple_of(half * 48, 16), 48), pl.ds(lt * LANES, width)] = values[:, :width]
        for lt in range(6):
            values = ref[pl.ds(CONV_ROWS + lt * 96, 96), :].astype(F32) * down_scale
            down_ref[pl.ds(pl.multiple_of(half * 96, 32), 96), pl.ds(lt * LANES, LANES)] = values


def here(rows):
    return pltpu.with_memory_space_constraint(rows, pltpu.VMEM)


def there(rows):
    return pltpu.with_memory_space_constraint(rows, pltpu.HBM)


def call(body, outs, scratch=(), scalars=0, ins=0, name=None):
    specs = [pl.BlockSpec(memory_space=pltpu.SMEM)] * scalars + [
        pl.BlockSpec(memory_space=pltpu.VMEM)
    ] * ins
    return pl.pallas_call(
        body,
        out_shape=[
            jax.ShapeDtypeStruct(shape, kind) if leaves else pltpu.VMEM(shape, kind)
            for shape, kind, *leaves in outs
        ],
        in_specs=specs,
        out_specs=[pl.BlockSpec(memory_space=pltpu.VMEM)] * len(outs),
        scratch_shapes=list(scratch),
        compiler_params=PARAMS,
        name=name,
    )


CHIPS = ("y", "z")
SPACE = ("y", "z", "c")


def trade(rows, axes):
    return lax.all_to_all(rows, axes, 0, 0, tiled=True)


def shards(features, cotangent, conv_weight, down_weight, neighbours):
    block = features[0, 0]
    cot = cotangent[0, 0]
    core = lax.axis_index("c").astype(jnp.int32).reshape(1)
    rows_shape = ((SLOTS, LANES), BF16)
    by_chip = (32, 32, LANES)
    packed = (32, 24, LANES)
    flat_scratch = pltpu.VMEM((SLOTS, LANES), F32)
    slot_scratch = pltpu.VMEM(by_chip, F32)

    def swap(rows):
        return lax.ppermute(rows, "c", [(0, 1), (1, 0)])

    (spread,) = pl.pallas_call(
        spread_kernel,
        out_shape=[pltpu.VMEM(*rows_shape)],
        in_specs=[pl.BlockSpec(memory_space=pltpu.HBM)] * 2,
        out_specs=[pl.BlockSpec(memory_space=pltpu.VMEM)],
        scratch_shapes=[
            pltpu.SMEM((1, 26), jnp.int32),
            pltpu.VMEM((C, VOX), BF16),
            pltpu.SemaphoreType.DMA((2,)),
            flat_scratch,
            flat_scratch,
        ],
        compiler_params=PARAMS,
        name="spread",
    )(there(neighbours[0]), there(block))
    middle = here(trade(spread.reshape(by_chip), CHIPS))
    route = call(route_kernel, [(packed, BF16)], [slot_scratch], scalars=1, ins=3, name="route")
    (routed,) = route(core, middle, middle, here(swap(middle)))
    halo = trade(routed, CHIPS)

    taps = conv_weight.reshape(C, 27, C)
    pad = ((0, 0), (0, LANES - C), (0, LANES - C))
    forward_w = jnp.pad(taps.transpose(1, 2, 0), pad).reshape(9, 3 * LANES, LANES)
    backward_w = jnp.pad(taps.transpose(1, 0, 2)[::-1], pad).reshape(9, 3 * LANES, LANES)
    down_w = jnp.pad(down_weight.reshape(C2, 8, C), ((0, 0), (0, 0), (0, LANES - C))).reshape(C2, 8 * LANES)
    halo, forward_w, backward_w, down_w = lax.optimization_barrier((halo, forward_w, backward_w, down_w))
    forward_w, backward_w, down_w = here(forward_w), here(backward_w), here(down_w)

    pad_scratch = pltpu.VMEM((100 * COL, LANES), F32)
    cols_scratch = pltpu.VMEM((10, 10, DEPTH, 3 * LANES), BF16)
    grad, patch, keep, send = call(
        forward_kernel,
        [rows_shape, ((LANES, 8 * LANES), BF16), ((HALF_ROWS, LANES), F32), ((HALF_ROWS, LANES), BF16)],
        [pad_scratch, cols_scratch, flat_scratch, slot_scratch, pltpu.VMEM((C, 21 * LANES), F32), pltpu.VMEM((C2, 8 * C), F32)],
        scalars=1,
        ins=5,
        name="forward",
    )(core, block, here(halo), cot, forward_w, down_w)
    spread2, coarse = call(
        side_kernel, [(packed, BF16), ((C2, LANES), BF16, True)], [flat_scratch, slot_scratch], ins=3, name="side"
    )(grad, patch, down_w)

    pair = (keep + swap(send).astype(F32)).astype(BF16)
    out = jnp.concatenate([spread2, pair.reshape(32, 56, LANES)], axis=1)
    got = trade(out, CHIPS)
    middle2 = got[:, :24]
    part = jnp.sum(got[:, 24:].astype(F32), axis=0)
    (routed2,) = route(core, middle, here(middle2), here(swap(middle2)))
    routed2, part = lax.optimization_barrier((routed2, part))
    halo2 = trade(routed2, CHIPS)
    for step in (1, 2):
        part = part + lax.ppermute(part, "x", [(i, i ^ step) for i in range(4)])
    halo2, part = lax.optimization_barrier((halo2, part))
    mine = trade(jnp.broadcast_to(part.astype(BF16), (32, 56, LANES)), CHIPS).reshape(HALF_ROWS, LANES)
    (grad_features,) = call(
        backward_kernel,
        [((C, VOX), F32, True)],
        [pad_scratch, cols_scratch, flat_scratch, slot_scratch],
        ins=3,
        name="backward",
    )(grad, here(halo2), backward_w)
    mine, grad_features = lax.optimization_barrier((mine, grad_features))
    theirs = swap(mine)
    grad_conv, grad_down = call(
        finish_kernel, [((C, 27 * C), F32, True), ((C2, 8 * C), F32, True)], scalars=1, ins=2, name="finish"
    )(core, here(mine), here(theirs))
    return coarse[None, None], grad_features[None, None], grad_conv, grad_down


def solution(mesh):
    devices = mesh.devices
    fine = Mesh(devices.reshape(devices.shape[0], 4, -1, 2), ("x", "y", "z", "c"))
    block = P("x", SPACE, None, None)
    return jax.shard_map(
        shards,
        mesh=fine,
        in_specs=(block, block, P(), P(), P("x", SPACE, None)),
        out_specs=(block, block, P(), P()),
        check_vma=False,
    )
```

```python
import jax
import jax.numpy as jnp
import numpy as np
from jax import lax
from jax.experimental import pallas as pl
from jax.experimental.pallas import tpu as pltpu
from jax.sharding import Mesh, PartitionSpec as P

C = 96
C2 = 192
SIDE = 8
DEPTH = 16
VOX = 1024
LANES = 128
SLOTS = 992
COL = 24
MAIN_ROWS = 1536
HALF_ROWS = MAIN_ROWS + 128
CONV_CHIPS = 20
EPSILON = 1e-06
F32 = jnp.float32
BF16 = jnp.bfloat16
PARAMS = pltpu.CompilerParams(vmem_limit_bytes=32 << 20)


RIM = [(x, y) for x in range(10) for y in range(10) if x in (0, 9) or y in (0, 9)]


def side(position, extent):
    if position == 0:
        return -1, extent - 1
    if position == extent + 1:
        return 1, 0
    return 0, position - 1


def direction(ex, ey, ez):
    place = ((ex + 1) * 3 + ey + 1) * 3 + ez + 1
    return place - (place > 13)


def direction_table():
    table = np.full((32, LANES), -1, np.int32)

    def put(slot, px, py, pz):
        steps = (side(px, SIDE)[0], side(py, SIDE)[0], side(pz, DEPTH)[0])
        table[slot // 31, slot % 31] = direction(*steps)

    for place, (px, py) in enumerate(RIM):
        for pz in range(DEPTH + 2):
            put(place * COL + pz, px, py, pz)
    for n in range(64):
        put(864 + n, n // 8 + 1, n % 8 + 1, 0)
        put(928 + n, n // 8 + 1, n % 8 + 1, DEPTH + 1)
    return table


def one_hot(index, count):
    wide = lax.broadcasted_iota(jnp.int32, (index.shape[0], count), 1)
    return jnp.where(wide == index, 1.0, 0.0).astype(BF16)


def dot(a, b, ca=1, cb=0):
    return lax.dot_general(a, b, (((ca,), (cb,)), ((), ())), preferred_element_type=F32)


def spread_rows(src_ref, out_ref, parity):
    for place, (px, py) in enumerate(RIM):
        base = (side(px, SIDE)[1] * SIDE + side(py, SIDE)[1]) * DEPTH
        first = place * COL
        if parity:
            for par in range(2):
                out_ref[pl.ds(first + 1 + par, 8, stride=2), :] = src_ref[pl.ds(base + par * 8, 8), :]
        else:
            out_ref[pl.ds(first + 1, DEPTH), :] = src_ref[pl.ds(base, DEPTH), :]
        out_ref[pl.ds(first, 1), :] = src_ref[pl.ds(base + 15, 1), :]
        out_ref[pl.ds(first + 17, 1), :] = src_ref[pl.ds(base, 1), :]
        out_ref[pl.ds(first + 18, 6), :] = jnp.zeros((6, LANES), F32)
    for x in range(SIDE):
        out_ref[pl.ds(864 + x * 8, 8), :] = src_ref[pl.ds(x * 128 + 15, 8, stride=DEPTH), :]
        out_ref[pl.ds(928 + x * 8, 8), :] = src_ref[pl.ds(x * 128, 8, stride=DEPTH), :]


def to_chips(flat_ref, row_ref):
    for chip in range(32):
        row_ref[chip, 0:31, :] = flat_ref[pl.ds(chip * 31, 31), :]


def from_chips(row_ref, flat_ref):
    for chip in range(32):
        flat_ref[pl.ds(chip * 31, 31), :] = row_ref[chip, 0:31, :]


def lanes_of(rows):
    return lax.broadcasted_iota(jnp.int32, rows.shape, len(rows.shape) - 1)


def pack(row_ref, out_ref):
    extra = row_ref[:, 24:32]
    for part in range(3):
        rows = row_ref[:, part * 8 : part * 8 + 8]
        moved = pltpu.roll(extra, C - 32 * part, 2)
        out_ref[:, part * 8 : part * 8 + 8] = jnp.where(lanes_of(rows) < C, rows, moved).astype(BF16)


def slot_groups(ref):
    rows = ref[...].astype(F32)
    groups = [rows[:, g * 8 : g * 8 + 8] for g in range(3)]
    lane = lanes_of(groups[0])
    moved = [pltpu.roll(rows, 32 * (part + 1), 2) for part, rows in enumerate(groups)]
    groups.append(jnp.where(lane < 32, moved[0], jnp.where(lane < 64, moved[1], moved[2])))
    return groups


def spread_kernel(nbr_hbm, f_hbm, table_hbm, out_ref, nbr_ref, f_ref, table_ref, sems, src_ref, flat_ref, row_ref):
    copies = [
        pltpu.make_async_copy(nbr_hbm, nbr_ref, sems.at[0]),
        pltpu.make_async_copy(f_hbm, f_ref, sems.at[1]),
        pltpu.make_async_copy(table_hbm, table_ref, sems.at[2]),
    ]
    for copy in copies:
        copy.start()
    for copy in copies:
        copy.wait()
    wide = jnp.concatenate([f_ref[...].astype(F32), jnp.zeros((LANES - C, VOX), F32)], axis=0)
    src_ref[...] = wide.T
    spread_rows(src_ref, flat_ref, False)
    to_chips(flat_ref, row_ref)
    table = table_ref[...]
    owner = jnp.full((32, LANES), -1, jnp.int32)
    for number in range(26):
        owner = jnp.where(table == number, nbr_ref[0, number], owner)
    row_ref[:, 31:32, :] = owner.astype(F32).reshape(32, 1, LANES)
    pack(row_ref, out_ref)


def route_kernel(core_ref, owner_ref, mine_ref, other_ref, out_ref, row_ref):
    core = core_ref[0]
    mine, other = slot_groups(mine_ref), slot_groups(other_ref)
    owners = jnp.broadcast_to(slot_groups(owner_ref)[3][:, 7:8, :], (32, 8, LANES))
    slot = lax.broadcasted_iota(jnp.int32, (32, 8, LANES), 1)
    for group in range(4):
        held = jnp.where(lanes_of(owners) == slot + group * 8, owners, 0.0)
        owner = jnp.sum(held, axis=2, keepdims=True).reshape(256, 1).astype(jnp.int32)
        place = lax.broadcasted_iota(jnp.int32, (256, 1), 0) & 7
        held = jnp.bitwise_and(owner, 1)
        spot = lax.shift_right_arithmetic(owner, 1) * 8 + place + jnp.where(held == core, 0, 256)
        spot = jnp.where(owner < 0, -1, spot)
        source = jnp.concatenate(
            [mine[group].reshape(256, LANES), other[group].reshape(256, LANES)], axis=0
        ).astype(BF16)
        row_ref[:, group * 8 : group * 8 + 8] = dot(one_hot(spot, 512), source).reshape(32, 8, LANES)
    pack(row_ref, out_ref)


def fill_halo(pad_ref, packed_ref, row_ref, halo_ref):
    for group, rows in enumerate(slot_groups(packed_ref)):
        row_ref[:, group * 8 : group * 8 + 8] = rows
    from_chips(row_ref, halo_ref)

    def put(first, count, place):
        pad_ref[pl.ds(first * COL, count * COL), :] = halo_ref[pl.ds(place * COL, count * COL), :]

    put(0, 11, 0)
    for x in range(1, 8):
        put(x * 10 + 9, 2, 11 + 2 * (x - 1))
    put(89, 11, 25)
    for x in range(SIDE):
        start = ((x + 1) * 10 + 1) * COL
        pad_ref[pl.ds(start, 8, stride=COL), :] = halo_ref[pl.ds(864 + x * 8, 8), :]
        pad_ref[pl.ds(start + DEPTH + 1, 8, stride=COL), :] = halo_ref[pl.ds(928 + x * 8, 8), :]


def shifted_columns(pad_ref, cols_ref):
    for x in range(10):
        for y in range(10):
            base = (x * 10 + y) * COL
            rows = [pad_ref[pl.ds(base + s, 8, stride=2), :] for s in range(4)]
            for dz in range(3):
                cols_ref[x, y, :, pl.ds(dz * LANES, LANES)] = jnp.concatenate(
                    [rows[dz], rows[dz + 1]], axis=0
                ).astype(BF16)


def window(cols_ref, dx, dy):
    return cols_ref[dx : dx + 8, dy : dy + 8].reshape(VOX, 3 * LANES)


def conv(cols_ref, w_ref):
    total = None
    for tap in range(9):
        part = dot(window(cols_ref, tap // 3, tap % 3), w_ref[tap])
        total = part if total is None else total + part
    return total


def forward_kernel(
    core_ref, f_ref, halo_ref, cot_ref, w_ref, dw_ref,
    grad_ref, patch_ref, keep_ref, send_ref,
    pad_ref, cols_ref, act_ref, row_ref, flat_ref, conv_ref, down_ref, free_ref,
):
    wide = jnp.concatenate([f_ref[...].astype(F32), jnp.zeros((LANES - C, VOX), F32)], axis=0)
    own = wide.T
    for x in range(SIDE):
        for y in range(SIDE):
            pad_ref[pl.ds(((x + 1) * 10 + y + 1) * COL + 1, DEPTH), :] = own[
                (x * 8 + y) * 16 : (x * 8 + y + 1) * 16, :
            ]
    fill_halo(pad_ref, halo_ref, row_ref, flat_ref)
    shifted_columns(pad_ref, cols_ref)
    act_ref[...] = conv(cols_ref, w_ref)
    back = dot(cot_ref[...], dw_ref[...], 0, 0)
    for j in range(8):
        jx, jy, jz = j // 4, j // 2 % 2, j % 2
        spots = [
            ((2 * ux + jx) * 8 + 2 * uy + jy) * 16 + jz * 8 for ux in range(4) for uy in range(4)
        ]
        a = jnp.concatenate([act_ref[pl.ds(s, 8), :] for s in spots], axis=0)
        g = 1.0 / (1.0 + jnp.exp(-a))
        patch_ref[:, pl.ds(j * LANES, LANES)] = (a * g).astype(BF16)
        slope = g * (1.0 + a * (1.0 - g))
        grad = back[:, j * LANES : (j + 1) * LANES] * slope
        for n, s in enumerate(spots):
            act_ref[pl.ds(s, 8), :] = grad[n * 8 : n * 8 + 8, :]
    grad_ref[...] = act_ref[...].astype(BF16)

    turned = act_ref[...].T[:C, :].astype(BF16)
    conv_ref[:, pl.ds(20 * LANES, LANES)] = jnp.zeros((C, LANES), F32)
    for tap in range(9):
        part = dot(turned, window(cols_ref, tap // 3, tap % 3))
        for dz in range(3):
            conv_ref[:, pl.ds((tap * 3 + dz) * C, C)] = part[:, dz * LANES : dz * LANES + C]
    part = dot(cot_ref[...], patch_ref[...])
    for j in range(8):
        down_ref[:, pl.ds(j * C, C)] = part[:, j * LANES : j * LANES + C]
    core = core_ref[0]
    for ref, half in ((keep_ref, core), (send_ref, 1 - core)):
        for lt in range(20):
            ref[pl.ds(lt * 48, 48), :] = conv_ref[
                pl.ds(pl.multiple_of(half * 48, 16), 48), pl.ds(lt * LANES, LANES)
            ].astype(ref.dtype)
        for lt in range(6):
            ref[pl.ds(960 + lt * 96, 96), :] = down_ref[
                pl.ds(pl.multiple_of(half * 96, 32), 96), pl.ds(lt * LANES, LANES)
            ].astype(ref.dtype)
        last = conv_ref[pl.ds(pl.multiple_of(half * 48, 16), 48), pl.ds(20 * LANES, LANES)]
        last = pltpu.roll(last, C, 1)
        free_ref[...] = jnp.zeros((16, 8, LANES), F32)
        for part in range(3):
            free_ref[:, part : part + 1, :] = last[part * 16 : part * 16 + 16, :].reshape(16, 1, LANES)
        ref[pl.ds(MAIN_ROWS, 128), :] = free_ref[...].reshape(128, LANES).astype(ref.dtype)


def side_kernel(grad_ref, patch_ref, dw_ref, send_ref, coarse_ref, src_ref, flat_ref, row_ref):
    src_ref[...] = grad_ref[...].astype(F32)
    spread_rows(src_ref, flat_ref, True)
    to_chips(flat_ref, row_ref)
    row_ref[:, 31:32, :] = jnp.zeros((32, 1, LANES), F32)
    pack(row_ref, send_ref)
    coarse_ref[...] = dot(dw_ref[...], patch_ref[...], 1, 1).astype(BF16)


def backward_kernel(grad_ref, halo_ref, w_ref, out_ref, pad_ref, cols_ref, act_ref, row_ref, flat_ref):
    for x in range(SIDE):
        for y in range(SIDE):
            base = ((x + 1) * 10 + y + 1) * COL
            for par in range(2):
                pad_ref[pl.ds(base + 1 + par, 8, stride=2), :] = grad_ref[
                    pl.ds((x * 8 + y) * 16 + par * 8, 8), :
                ].astype(F32)
    fill_halo(pad_ref, halo_ref, row_ref, flat_ref)
    shifted_columns(pad_ref, cols_ref)
    full = conv(cols_ref, w_ref)
    for n in range(64):
        for par in range(2):
            act_ref[pl.ds(n * 16 + par, 8, stride=2), :] = full[n * 16 + par * 8 : n * 16 + par * 8 + 8, :]
    out_ref[...] = act_ref[...].T[:C, :]


def finish_kernel(core_ref, mine_ref, other_ref, conv_ref, down_ref, last_ref):
    def squares(values):
        return jnp.sum((values * values).reshape(-1, 8, LANES), axis=0)

    conv_sum = jnp.zeros((8, LANES), F32)
    down_sum = jnp.zeros((8, LANES), F32)
    for n, ref in enumerate((mine_ref, other_ref)):
        conv_sum += squares(ref[0:CONV_CHIPS, 24:72, :].astype(F32))
        down_sum += squares(ref[CONV_CHIPS:32, 24:72, :].astype(F32))
        for part in range(3):
            rows = ref[0:16, part * 8 : part * 8 + 8, :].astype(F32)
            rows = pltpu.roll(rows, 32, 2)[:, 7:8, :].reshape(16, LANES)
            rows = jnp.where(lanes_of(rows) < 32, rows, 0.0)
            last_ref[n, pl.ds(part * 16, 16), :] = rows
            conv_sum += squares(rows)
    conv_scale = lax.rsqrt(jnp.sum(conv_sum, keepdims=True) * (1.0 / (C * 27 * C)) + EPSILON)
    down_scale = lax.rsqrt(jnp.sum(down_sum, keepdims=True) * (1.0 / (C2 * 8 * C)) + EPSILON)
    core = core_ref[0]
    for n, (ref, half) in enumerate(((mine_ref, core), (other_ref, 1 - core))):
        rows = pl.ds(pl.multiple_of(half * 48, 16), 48)
        for lt in range(20):
            conv_ref[rows, pl.ds(lt * LANES, LANES)] = ref[lt, 24:72, :].astype(F32) * conv_scale
        conv_ref[rows, pl.ds(20 * LANES, 32)] = (last_ref[n] * conv_scale)[:, :32]
        for lt in range(6):
            for part in range(2):
                rows = pl.ds(pl.multiple_of(half * 96 + part * 48, 16), 48)
                values = ref[CONV_CHIPS + lt * 2 + part, 24:72, :].astype(F32) * down_scale
                down_ref[rows, pl.ds(lt * LANES, LANES)] = values


def there(rows):
    return pltpu.with_memory_space_constraint(rows, pltpu.HBM)


def here(rows):
    return pltpu.with_memory_space_constraint(rows, pltpu.VMEM)


def call(body, outs, scratch=(), scalars=0, ins=0, name=None):
    specs = [pl.BlockSpec(memory_space=pltpu.SMEM)] * scalars + [
        pl.BlockSpec(memory_space=pltpu.VMEM)
    ] * ins
    return pl.pallas_call(
        body,
        out_shape=[
            jax.ShapeDtypeStruct(shape, kind) if leaves else pltpu.VMEM(shape, kind)
            for shape, kind, *leaves in outs
        ],
        in_specs=specs,
        out_specs=[pl.BlockSpec(memory_space=pltpu.VMEM)] * len(outs),
        scratch_shapes=list(scratch),
        compiler_params=PARAMS,
        name=name,
    )


CHIPS = ("y", "z")
SPACE = ("y", "z", "c")


def trade(rows, axes):
    return lax.all_to_all(rows, axes, 0, 0, tiled=True)


def shards(features, cotangent, conv_weight, down_weight, neighbours):
    block = features[0, 0]
    cot = cotangent[0, 0]
    core = lax.axis_index("c").astype(jnp.int32).reshape(1)
    rows_shape = ((VOX, LANES), BF16)
    by_chip = (32, 32, LANES)
    packed = (32, 24, LANES)
    flat_scratch = pltpu.VMEM((VOX, LANES), F32)
    slot_scratch = pltpu.VMEM(by_chip, F32)

    def swap(rows):
        return lax.ppermute(rows, "c", [(0, 1), (1, 0)])

    (spread,) = pl.pallas_call(
        spread_kernel,
        out_shape=[pltpu.VMEM(packed, BF16)],
        in_specs=[pl.BlockSpec(memory_space=pltpu.HBM)] * 3,
        out_specs=[pl.BlockSpec(memory_space=pltpu.VMEM)],
        scratch_shapes=[
            pltpu.SMEM((1, 26), jnp.int32),
            pltpu.VMEM((C, VOX), BF16),
            pltpu.VMEM((32, LANES), jnp.int32),
            pltpu.SemaphoreType.DMA((3,)),
            flat_scratch,
            flat_scratch,
            slot_scratch,
        ],
        compiler_params=PARAMS,
        name="spread",
    )(there(neighbours[0]), there(block), there(jnp.asarray(direction_table())))
    middle = here(trade(spread, CHIPS))
    route = call(route_kernel, [(packed, BF16)], [slot_scratch], scalars=1, ins=3, name="route")
    (routed,) = route(core, middle, middle, here(swap(middle)))
    halo = trade(routed, CHIPS)

    taps = conv_weight.reshape(C, 27, C)
    pad = ((0, 0), (0, LANES - C), (0, LANES - C))
    forward_w = jnp.pad(taps.transpose(1, 2, 0), pad).reshape(9, 3 * LANES, LANES)
    backward_w = jnp.pad(taps.transpose(1, 0, 2)[::-1], pad).reshape(9, 3 * LANES, LANES)
    down_w = jnp.pad(down_weight.reshape(C2, 8, C), ((0, 0), (0, 0), (0, LANES - C))).reshape(C2, 8 * LANES)
    halo, forward_w, backward_w, down_w = lax.optimization_barrier((halo, forward_w, backward_w, down_w))
    forward_w, backward_w, down_w = here(forward_w), here(backward_w), here(down_w)

    pad_scratch = pltpu.VMEM((100 * COL, LANES), F32)
    cols_scratch = pltpu.VMEM((10, 10, DEPTH, 3 * LANES), BF16)
    grad, patch, keep, send = call(
        forward_kernel,
        [rows_shape, ((LANES, 8 * LANES), BF16), ((HALF_ROWS, LANES), F32), ((HALF_ROWS, LANES), BF16)],
        [
            pad_scratch,
            cols_scratch,
            flat_scratch,
            slot_scratch,
            flat_scratch,
            pltpu.VMEM((C, 21 * LANES), F32),
            pltpu.VMEM((C2, 8 * C), F32),
            pltpu.VMEM((16, 8, LANES), F32),
        ],
        scalars=1,
        ins=5,
        name="forward",
    )(core, block, here(halo), cot, forward_w, down_w)
    spread2, coarse = call(
        side_kernel, [(packed, BF16), ((C2, LANES), BF16, True)], [flat_scratch, flat_scratch, slot_scratch], ins=3, name="side"
    )(grad, patch, down_w)

    pair = (keep + swap(send).astype(F32)).astype(BF16)
    main = pair[:MAIN_ROWS].reshape(32, 48, LANES)
    free = pair[MAIN_ROWS:].reshape(16, 8, LANES)[:, :3].reshape(16, 3, 1, LANES)
    free = jnp.pad(free, ((0, 16), (0, 0), (7, 0), (0, 0))).reshape(packed)
    got = trade(jnp.concatenate([spread2 + free, main], axis=1), CHIPS)
    middle2 = got[:, :24]
    part = jnp.sum(got.astype(F32), axis=0)
    other2, part = lax.optimization_barrier((swap(middle2), part))
    line = trade(jnp.broadcast_to(part, (4, 72, LANES)), "x")
    whole = jnp.sum(line, axis=0).astype(BF16)
    (routed2,) = route(core, middle, here(middle2), here(other2))
    row = lax.broadcasted_iota(jnp.int32, (24, LANES), 0)
    lane = lax.broadcasted_iota(jnp.int32, (24, LANES), 1)
    inside = (row % 8 == 7) & (lane >= C)
    routed2 = jnp.where(inside, whole[:24], routed2)
    got = trade(jnp.concatenate([routed2, jnp.broadcast_to(whole[24:], (32, 48, LANES))], axis=1), CHIPS)
    theirs = swap(got)
    (grad_features,) = call(
        backward_kernel,
        [((C, VOX), F32, True)],
        [pad_scratch, cols_scratch, flat_scratch, slot_scratch, flat_scratch],
        ins=3,
        name="backward",
    )(grad, here(got[:, :24]), backward_w)
    grad_conv, grad_down = call(
        finish_kernel,
        [((C, 27 * C), F32, True), ((C2, 8 * C), F32, True)],
        [pltpu.VMEM((2, 48, LANES), F32)],
        scalars=1,
        ins=2,
        name="finish",
    )(core, here(got), here(theirs))
    return coarse[None, None], grad_features[None, None], grad_conv, grad_down


def solution(mesh):
    devices = mesh.devices
    fine = Mesh(devices.reshape(devices.shape[0], 4, -1, 2), ("x", "y", "z", "c"))
    block = P("x", SPACE, None, None)
    return jax.shard_map(
        shards,
        mesh=fine,
        in_specs=(block, block, P(), P(), P("x", SPACE, None)),
        out_specs=(block, block, P(), P()),
        check_vma=False,
    )
```

```python
import jax
import jax.numpy as jnp
import numpy as np
from jax import lax
from jax.experimental import pallas as pl
from jax.experimental.pallas import tpu as pltpu
from jax.sharding import Mesh, PartitionSpec as P

C = 96
C2 = 192
SIDE = 8
DEPTH = 16
VOX = 1024
LANES = 128
SLOTS = 992
COL = 24
MAIN_ROWS = 1536
HALF_ROWS = MAIN_ROWS + 128
CONV_CHIPS = 20
EPSILON = 1e-06
F32 = jnp.float32
BF16 = jnp.bfloat16
PARAMS = pltpu.CompilerParams(vmem_limit_bytes=32 << 20)


RIM = [(x, y) for x in range(10) for y in range(10) if x in (0, 9) or y in (0, 9)]


def side(position, extent):
    if position == 0:
        return -1, extent - 1
    if position == extent + 1:
        return 1, 0
    return 0, position - 1


def direction(ex, ey, ez):
    place = ((ex + 1) * 3 + ey + 1) * 3 + ez + 1
    return place - (place > 13)


def direction_table():
    table = np.full((32, LANES), -1, np.int32)

    def put(slot, px, py, pz):
        steps = (side(px, SIDE)[0], side(py, SIDE)[0], side(pz, DEPTH)[0])
        table[slot // 31, slot % 31] = direction(*steps)

    for place, (px, py) in enumerate(RIM):
        for pz in range(DEPTH + 2):
            put(place * COL + pz, px, py, pz)
    for n in range(64):
        put(864 + n, n // 8 + 1, n % 8 + 1, 0)
        put(928 + n, n // 8 + 1, n % 8 + 1, DEPTH + 1)
    return table


def one_hot(index, count):
    wide = lax.broadcasted_iota(jnp.int32, (index.shape[0], count), 1)
    return jnp.where(wide == index, 1.0, 0.0).astype(BF16)


def dot(a, b, ca=1, cb=0):
    return lax.dot_general(a, b, (((ca,), (cb,)), ((), ())), preferred_element_type=F32)


def spread_rows(src_ref, out_ref, parity):
    for place, (px, py) in enumerate(RIM):
        base = (side(px, SIDE)[1] * SIDE + side(py, SIDE)[1]) * DEPTH
        first = place * COL
        if parity:
            for par in range(2):
                out_ref[pl.ds(first + 1 + par, 8, stride=2), :] = src_ref[pl.ds(base + par * 8, 8), :]
        else:
            out_ref[pl.ds(first + 1, DEPTH), :] = src_ref[pl.ds(base, DEPTH), :]
        out_ref[pl.ds(first, 1), :] = src_ref[pl.ds(base + 15, 1), :]
        out_ref[pl.ds(first + 17, 1), :] = src_ref[pl.ds(base, 1), :]
        out_ref[pl.ds(first + 18, 6), :] = jnp.zeros((6, LANES), F32)
    for x in range(SIDE):
        out_ref[pl.ds(864 + x * 8, 8), :] = src_ref[pl.ds(x * 128 + 15, 8, stride=DEPTH), :]
        out_ref[pl.ds(928 + x * 8, 8), :] = src_ref[pl.ds(x * 128, 8, stride=DEPTH), :]


def to_chips(flat_ref, row_ref):
    for chip in range(32):
        row_ref[chip, 0:31, :] = flat_ref[pl.ds(chip * 31, 31), :]


def from_chips(row_ref, flat_ref):
    for chip in range(32):
        flat_ref[pl.ds(chip * 31, 31), :] = row_ref[chip, 0:31, :]


def lanes_of(rows):
    return lax.broadcasted_iota(jnp.int32, rows.shape, len(rows.shape) - 1)


def pack(row_ref, out_ref):
    extra = row_ref[:, 24:32]
    for part in range(3):
        rows = row_ref[:, part * 8 : part * 8 + 8]
        moved = pltpu.roll(extra, C - 32 * part, 2)
        out_ref[:, part * 8 : part * 8 + 8] = jnp.where(lanes_of(rows) < C, rows, moved).astype(BF16)


def slot_groups(ref):
    rows = ref[:, 0:24].astype(F32)
    groups = [rows[:, g * 8 : g * 8 + 8] for g in range(3)]
    lane = lanes_of(groups[0])
    moved = [pltpu.roll(rows, 32 * (part + 1), 2) for part, rows in enumerate(groups)]
    groups.append(jnp.where(lane < 32, moved[0], jnp.where(lane < 64, moved[1], moved[2])))
    return groups


def spread_kernel(nbr_hbm, f_hbm, table_hbm, out_ref, nbr_ref, f_ref, table_ref, sems, src_ref, flat_ref, row_ref):
    copies = [
        pltpu.make_async_copy(nbr_hbm, nbr_ref, sems.at[0]),
        pltpu.make_async_copy(f_hbm, f_ref, sems.at[1]),
        pltpu.make_async_copy(table_hbm, table_ref, sems.at[2]),
    ]
    for copy in copies:
        copy.start()
    copies[0].wait()
    copies[2].wait()
    table = table_ref[...]
    owner = jnp.full((32, LANES), -1, jnp.int32)
    for number in range(26):
        owner = jnp.where(table == number, nbr_ref[0, number], owner)
    row_ref[:, 31:32, :] = owner.astype(F32).reshape(32, 1, LANES)
    copies[1].wait()
    wide = jnp.concatenate([f_ref[...].astype(F32), jnp.zeros((LANES - C, VOX), F32)], axis=0)
    src_ref[...] = wide.T
    spread_rows(src_ref, flat_ref, False)
    to_chips(flat_ref, row_ref)
    pack(row_ref, out_ref)


def prepare_kernel(f_ref, own_ref):
    wide = jnp.concatenate([f_ref[...].astype(F32), jnp.zeros((LANES - C, VOX), F32)], axis=0)
    own_ref[...] = wide.T


def merge_kernel(halo_ref, keep_ref, other_ref, out_ref):
    pair = keep_ref[...] + other_ref[...].astype(F32)
    out_ref[:, 24:72] = pair[:MAIN_ROWS].reshape(32, 48, LANES).astype(BF16)
    free = pair[MAIN_ROWS:].reshape(16, 8, LANES)
    place = lax.broadcasted_iota(jnp.int32, (16, 8, LANES), 1)
    for part in range(3):
        rows = halo_ref[:, part * 8 : part * 8 + 8].astype(F32)
        added = jnp.where(place == 7, jnp.broadcast_to(free[:, part : part + 1], (16, 8, LANES)), 0.0)
        out_ref[0:16, part * 8 : part * 8 + 8] = (rows[:16] + added).astype(BF16)
        out_ref[16:32, part * 8 : part * 8 + 8] = rows[16:].astype(BF16)


def total_kernel(got_ref, part_ref, rows_ref):
    total = jnp.sum(got_ref[...].astype(F32), axis=0)
    for n in range(4):
        part_ref[n] = total
    rows_ref[...] = got_ref[:, 0:24]


def join_kernel(line_ref, rows_ref, out_ref):
    whole = line_ref[0] + line_ref[1] + line_ref[2] + line_ref[3]
    out_ref[:, 24:72] = jnp.broadcast_to(whole[24:], (32, 48, LANES)).astype(BF16)
    place = lax.broadcasted_iota(jnp.int32, (32, 24, LANES), 1) & 7
    rows = rows_ref[...].astype(F32)
    free = (place == 7) & (lanes_of(rows) >= C)
    out_ref[:, 0:24] = jnp.where(free, jnp.broadcast_to(whole[:24], rows.shape), rows).astype(BF16)


def route_kernel(core_ref, owner_ref, mine_ref, other_ref, out_ref, row_ref):
    core = core_ref[0]
    mine, other = slot_groups(mine_ref), slot_groups(other_ref)
    owners = jnp.broadcast_to(slot_groups(owner_ref)[3][:, 7:8, :], (32, 8, LANES))
    slot = lax.broadcasted_iota(jnp.int32, (32, 8, LANES), 1)
    for group in range(4):
        held = jnp.where(lanes_of(owners) == slot + group * 8, owners, 0.0)
        owner = jnp.sum(held, axis=2, keepdims=True).reshape(256, 1).astype(jnp.int32)
        place = lax.broadcasted_iota(jnp.int32, (256, 1), 0) & 7
        held = jnp.bitwise_and(owner, 1)
        spot = lax.shift_right_arithmetic(owner, 1) * 8 + place + jnp.where(held == core, 0, 256)
        spot = jnp.where(owner < 0, -1, spot)
        source = jnp.concatenate(
            [mine[group].reshape(256, LANES), other[group].reshape(256, LANES)], axis=0
        ).astype(BF16)
        row_ref[:, group * 8 : group * 8 + 8] = dot(one_hot(spot, 512), source).reshape(32, 8, LANES)
    pack(row_ref, out_ref)


def fill_halo(pad_ref, packed_ref, row_ref, halo_ref):
    for group, rows in enumerate(slot_groups(packed_ref)):
        row_ref[:, group * 8 : group * 8 + 8] = rows
    from_chips(row_ref, halo_ref)

    def put(first, count, place):
        pad_ref[pl.ds(first * COL, count * COL), :] = halo_ref[pl.ds(place * COL, count * COL), :]

    put(0, 11, 0)
    for x in range(1, 8):
        put(x * 10 + 9, 2, 11 + 2 * (x - 1))
    put(89, 11, 25)
    for x in range(SIDE):
        start = ((x + 1) * 10 + 1) * COL
        pad_ref[pl.ds(start, 8, stride=COL), :] = halo_ref[pl.ds(864 + x * 8, 8), :]
        pad_ref[pl.ds(start + DEPTH + 1, 8, stride=COL), :] = halo_ref[pl.ds(928 + x * 8, 8), :]


def shifted_columns(pad_ref, cols_ref):
    for x in range(10):
        for y in range(10):
            base = (x * 10 + y) * COL
            rows = [pad_ref[pl.ds(base + s, 8, stride=2), :] for s in range(4)]
            for dz in range(3):
                cols_ref[x, y, :, pl.ds(dz * LANES, LANES)] = jnp.concatenate(
                    [rows[dz], rows[dz + 1]], axis=0
                ).astype(BF16)


def window(cols_ref, dx, dy):
    return cols_ref[dx : dx + 8, dy : dy + 8].reshape(VOX, 3 * LANES)


def conv(cols_ref, w_ref):
    total = None
    for tap in range(9):
        part = dot(window(cols_ref, tap // 3, tap % 3), w_ref[tap])
        total = part if total is None else total + part
    return total


def forward_kernel(
    core_ref, own_ref, halo_ref, cot_ref, w_ref, dw_ref,
    grad_ref, patch_ref, keep_ref, send_ref,
    pad_ref, cols_ref, act_ref, row_ref, flat_ref, conv_ref, down_ref, free_ref,
):
    for x in range(SIDE):
        for y in range(SIDE):
            pad_ref[pl.ds(((x + 1) * 10 + y + 1) * COL + 1, DEPTH), :] = own_ref[
                pl.ds((x * 8 + y) * 16, 16), :
            ]
    fill_halo(pad_ref, halo_ref, row_ref, flat_ref)
    shifted_columns(pad_ref, cols_ref)
    act_ref[...] = conv(cols_ref, w_ref)
    back = dot(cot_ref[...], dw_ref[...], 0, 0)
    for j in range(8):
        jx, jy, jz = j // 4, j // 2 % 2, j % 2
        spots = [
            ((2 * ux + jx) * 8 + 2 * uy + jy) * 16 + jz * 8 for ux in range(4) for uy in range(4)
        ]
        a = jnp.concatenate([act_ref[pl.ds(s, 8), :] for s in spots], axis=0)
        g = 1.0 / (1.0 + jnp.exp(-a))
        patch_ref[:, pl.ds(j * LANES, LANES)] = (a * g).astype(BF16)
        slope = g * (1.0 + a * (1.0 - g))
        grad = back[:, j * LANES : (j + 1) * LANES] * slope
        for n, s in enumerate(spots):
            act_ref[pl.ds(s, 8), :] = grad[n * 8 : n * 8 + 8, :]
    grad_ref[...] = act_ref[...].astype(BF16)

    turned = act_ref[...].T[:C, :].astype(BF16)
    conv_ref[:, pl.ds(20 * LANES, LANES)] = jnp.zeros((C, LANES), F32)
    for tap in range(9):
        part = dot(turned, window(cols_ref, tap // 3, tap % 3))
        for dz in range(3):
            conv_ref[:, pl.ds((tap * 3 + dz) * C, C)] = part[:, dz * LANES : dz * LANES + C]
    part = dot(cot_ref[...], patch_ref[...])
    for j in range(8):
        down_ref[:, pl.ds(j * C, C)] = part[:, j * LANES : j * LANES + C]
    core = core_ref[0]
    for ref, half in ((keep_ref, core), (send_ref, 1 - core)):
        for lt in range(20):
            ref[pl.ds(lt * 48, 48), :] = conv_ref[
                pl.ds(pl.multiple_of(half * 48, 16), 48), pl.ds(lt * LANES, LANES)
            ].astype(ref.dtype)
        for lt in range(6):
            ref[pl.ds(960 + lt * 96, 96), :] = down_ref[
                pl.ds(pl.multiple_of(half * 96, 32), 96), pl.ds(lt * LANES, LANES)
            ].astype(ref.dtype)
        last = conv_ref[pl.ds(pl.multiple_of(half * 48, 16), 48), pl.ds(20 * LANES, LANES)]
        last = pltpu.roll(last, C, 1)
        free_ref[...] = jnp.zeros((16, 8, LANES), F32)
        for part in range(3):
            free_ref[:, part : part + 1, :] = last[part * 16 : part * 16 + 16, :].reshape(16, 1, LANES)
        ref[pl.ds(MAIN_ROWS, 128), :] = free_ref[...].reshape(128, LANES).astype(ref.dtype)


def side_kernel(grad_ref, patch_ref, dw_ref, send_ref, coarse_ref, src_ref, flat_ref, row_ref):
    src_ref[...] = grad_ref[...].astype(F32)
    spread_rows(src_ref, flat_ref, True)
    to_chips(flat_ref, row_ref)
    row_ref[:, 31:32, :] = jnp.zeros((32, 1, LANES), F32)
    pack(row_ref, send_ref)
    coarse_ref[...] = dot(dw_ref[...], patch_ref[...], 1, 1).astype(BF16)


def backward_kernel(grad_ref, halo_ref, w_ref, out_ref, pad_ref, cols_ref, act_ref, row_ref, flat_ref):
    for x in range(SIDE):
        for y in range(SIDE):
            base = ((x + 1) * 10 + y + 1) * COL
            for par in range(2):
                pad_ref[pl.ds(base + 1 + par, 8, stride=2), :] = grad_ref[
                    pl.ds((x * 8 + y) * 16 + par * 8, 8), :
                ].astype(F32)
    fill_halo(pad_ref, halo_ref, row_ref, flat_ref)
    shifted_columns(pad_ref, cols_ref)
    full = conv(cols_ref, w_ref)
    for n in range(64):
        for par in range(2):
            act_ref[pl.ds(n * 16 + par, 8, stride=2), :] = full[n * 16 + par * 8 : n * 16 + par * 8 + 8, :]
    out_ref[...] = act_ref[...].T[:C, :]


def finish_kernel(core_ref, mine_ref, other_ref, conv_ref, down_ref, last_ref):
    def squares(values):
        return jnp.sum((values * values).reshape(-1, 8, LANES), axis=0)

    conv_sum = jnp.zeros((8, LANES), F32)
    down_sum = jnp.zeros((8, LANES), F32)
    for n, ref in enumerate((mine_ref, other_ref)):
        conv_sum += squares(ref[0:CONV_CHIPS, 24:72, :].astype(F32))
        down_sum += squares(ref[CONV_CHIPS:32, 24:72, :].astype(F32))
        for part in range(3):
            rows = ref[0:16, part * 8 : part * 8 + 8, :].astype(F32)
            rows = pltpu.roll(rows, 32, 2)[:, 7:8, :].reshape(16, LANES)
            rows = jnp.where(lanes_of(rows) < 32, rows, 0.0)
            last_ref[n, pl.ds(part * 16, 16), :] = rows
            conv_sum += squares(rows)
    conv_scale = lax.rsqrt(jnp.sum(conv_sum, keepdims=True) * (1.0 / (C * 27 * C)) + EPSILON)
    down_scale = lax.rsqrt(jnp.sum(down_sum, keepdims=True) * (1.0 / (C2 * 8 * C)) + EPSILON)
    core = core_ref[0]
    for n, (ref, half) in enumerate(((mine_ref, core), (other_ref, 1 - core))):
        rows = pl.ds(pl.multiple_of(half * 48, 16), 48)
        for lt in range(20):
            conv_ref[rows, pl.ds(lt * LANES, LANES)] = ref[lt, 24:72, :].astype(F32) * conv_scale
        conv_ref[rows, pl.ds(20 * LANES, 32)] = (last_ref[n] * conv_scale)[:, :32]
        for lt in range(6):
            for part in range(2):
                rows = pl.ds(pl.multiple_of(half * 96 + part * 48, 16), 48)
                values = ref[CONV_CHIPS + lt * 2 + part, 24:72, :].astype(F32) * down_scale
                down_ref[rows, pl.ds(lt * LANES, LANES)] = values


def there(rows):
    return pltpu.with_memory_space_constraint(rows, pltpu.HBM)


def here(rows):
    return pltpu.with_memory_space_constraint(rows, pltpu.VMEM)


def call(body, outs, scratch=(), scalars=0, ins=0, name=None):
    specs = [pl.BlockSpec(memory_space=pltpu.SMEM)] * scalars + [
        pl.BlockSpec(memory_space=pltpu.VMEM)
    ] * ins
    return pl.pallas_call(
        body,
        out_shape=[
            jax.ShapeDtypeStruct(shape, kind) if leaves else pltpu.VMEM(shape, kind)
            for shape, kind, *leaves in outs
        ],
        in_specs=specs,
        out_specs=[pl.BlockSpec(memory_space=pltpu.VMEM)] * len(outs),
        scratch_shapes=list(scratch),
        compiler_params=PARAMS,
        name=name,
    )


CHIPS = ("y", "z")
SPACE = ("y", "z", "c")


def trade(rows, axes):
    return lax.all_to_all(rows, axes, 0, 0, tiled=True)


def shards(features, cotangent, conv_weight, down_weight, neighbours):
    block = features[0, 0]
    cot = cotangent[0, 0]
    core = lax.axis_index("c").astype(jnp.int32).reshape(1)
    rows_shape = ((VOX, LANES), BF16)
    by_chip = (32, 32, LANES)
    packed = (32, 24, LANES)
    flat_scratch = pltpu.VMEM((VOX, LANES), F32)
    slot_scratch = pltpu.VMEM(by_chip, F32)

    def swap(rows):
        return lax.ppermute(rows, "c", [(0, 1), (1, 0)])

    (spread,) = pl.pallas_call(
        spread_kernel,
        out_shape=[pltpu.VMEM(packed, BF16)],
        in_specs=[pl.BlockSpec(memory_space=pltpu.HBM)] * 3,
        out_specs=[pl.BlockSpec(memory_space=pltpu.VMEM)],
        scratch_shapes=[
            pltpu.SMEM((1, 26), jnp.int32),
            pltpu.VMEM((C, VOX), BF16),
            pltpu.VMEM((32, LANES), jnp.int32),
            pltpu.SemaphoreType.DMA((3,)),
            flat_scratch,
            flat_scratch,
            slot_scratch,
        ],
        compiler_params=PARAMS,
        name="spread",
    )(there(neighbours[0]), there(block), there(jnp.asarray(direction_table())))
    middle = here(trade(spread, CHIPS))
    route = call(route_kernel, [(packed, BF16)], [slot_scratch], scalars=1, ins=3, name="route")
    (routed,) = route(core, middle, middle, here(swap(middle)))
    halo = trade(routed, CHIPS)

    taps = conv_weight.reshape(C, 27, C)
    pad = ((0, 0), (0, LANES - C), (0, LANES - C))
    forward_w = jnp.pad(taps.transpose(1, 2, 0), pad).reshape(9, 3 * LANES, LANES)
    backward_w = jnp.pad(taps.transpose(1, 0, 2)[::-1], pad).reshape(9, 3 * LANES, LANES)
    down_w = jnp.pad(down_weight.reshape(C2, 8, C), ((0, 0), (0, 0), (0, LANES - C))).reshape(C2, 8 * LANES)
    (own,) = call(prepare_kernel, [((VOX, LANES), F32)], ins=1, name="prepare")(block)
    halo, forward_w, backward_w, down_w, own = lax.optimization_barrier(
        (halo, forward_w, backward_w, down_w, own)
    )
    forward_w, backward_w, down_w = here(forward_w), here(backward_w), here(down_w)

    pad_scratch = pltpu.VMEM((100 * COL, LANES), F32)
    cols_scratch = pltpu.VMEM((10, 10, DEPTH, 3 * LANES), BF16)
    grad, patch, keep, send = call(
        forward_kernel,
        [rows_shape, ((LANES, 8 * LANES), BF16), ((HALF_ROWS, LANES), F32), ((HALF_ROWS, LANES), BF16)],
        [
            pad_scratch,
            cols_scratch,
            flat_scratch,
            slot_scratch,
            flat_scratch,
            pltpu.VMEM((C, 21 * LANES), F32),
            pltpu.VMEM((C2, 8 * C), F32),
            pltpu.VMEM((16, 8, LANES), F32),
        ],
        scalars=1,
        ins=5,
        name="forward",
    )(core, here(own), here(halo), cot, forward_w, down_w)
    spread2, coarse = call(
        side_kernel, [(packed, BF16), ((C2, LANES), BF16, True)], [flat_scratch, flat_scratch, slot_scratch], ins=3, name="side"
    )(grad, patch, down_w)

    message = (32, 72, LANES)
    (out,) = call(merge_kernel, [(message, BF16)], ins=3, name="merge")(spread2, keep, here(swap(send)))
    part, middle2 = call(total_kernel, [((4, 72, LANES), F32), (packed, BF16)], ins=1, name="total")(
        here(trade(out, CHIPS))
    )
    other2, part = lax.optimization_barrier((swap(middle2), part))
    line = trade(part, "x")
    (routed2,) = route(core, middle, middle2, here(other2))
    (out,) = call(join_kernel, [(message, BF16)], ins=2, name="join")(here(line), routed2)
    got = trade(out, CHIPS)
    theirs = swap(got)
    (grad_features,) = call(
        backward_kernel,
        [((C, VOX), F32, True)],
        [pad_scratch, cols_scratch, flat_scratch, slot_scratch, flat_scratch],
        ins=3,
        name="backward",
    )(grad, here(got), backward_w)
    grad_conv, grad_down = call(
        finish_kernel,
        [((C, 27 * C), F32, True), ((C2, 8 * C), F32, True)],
        [pltpu.VMEM((2, 48, LANES), F32)],
        scalars=1,
        ins=2,
        name="finish",
    )(core, here(got), here(theirs))
    return coarse[None, None], grad_features[None, None], grad_conv, grad_down


def solution(mesh):
    devices = mesh.devices
    fine = Mesh(devices.reshape(devices.shape[0], 4, -1, 2), ("x", "y", "z", "c"))
    block = P("x", SPACE, None, None)
    return jax.shard_map(
        shards,
        mesh=fine,
        in_specs=(block, block, P(), P(), P("x", SPACE, None)),
        out_specs=(block, block, P(), P()),
        check_vma=False,
    )
```

```python
import jax
import jax.numpy as jnp
import numpy as np
from jax import lax
from jax.experimental import pallas as pl
from jax.experimental.pallas import tpu as pltpu
from jax.sharding import Mesh, PartitionSpec as P

C = 96
C2 = 192
SIDE = 8
DEPTH = 16
VOX = 1024
LANES = 128
SLOTS = 992
COL = 24
MAIN_ROWS = 1536
HALF_ROWS = MAIN_ROWS + 128
CONV_CHIPS = 20
EPSILON = 1e-06
F32 = jnp.float32
BF16 = jnp.bfloat16
PARAMS = pltpu.CompilerParams(vmem_limit_bytes=32 << 20)


RIM = [(x, y) for x in range(10) for y in range(10) if x in (0, 9) or y in (0, 9)]


def side(position, extent):
    if position == 0:
        return -1, extent - 1
    if position == extent + 1:
        return 1, 0
    return 0, position - 1


def direction(ex, ey, ez):
    place = ((ex + 1) * 3 + ey + 1) * 3 + ez + 1
    return place - (place > 13)


def direction_table():
    table = np.full((32, LANES), -1, np.int32)

    def put(slot, px, py, pz):
        steps = (side(px, SIDE)[0], side(py, SIDE)[0], side(pz, DEPTH)[0])
        table[slot // 31, slot % 31] = direction(*steps)

    for place, (px, py) in enumerate(RIM):
        for pz in range(DEPTH + 2):
            put(place * COL + pz, px, py, pz)
    for n in range(64):
        put(864 + n, n // 8 + 1, n % 8 + 1, 0)
        put(928 + n, n // 8 + 1, n % 8 + 1, DEPTH + 1)
    return table


def one_hot(index, count):
    wide = lax.broadcasted_iota(jnp.int32, (index.shape[0], count), 1)
    return jnp.where(wide == index, 1.0, 0.0).astype(BF16)


def dot(a, b, ca=1, cb=0):
    return lax.dot_general(a, b, (((ca,), (cb,)), ((), ())), preferred_element_type=F32)


def spread_rows(src_ref, out_ref, parity):
    for place, (px, py) in enumerate(RIM):
        base = (side(px, SIDE)[1] * SIDE + side(py, SIDE)[1]) * DEPTH
        first = place * COL
        if parity:
            for par in range(2):
                out_ref[pl.ds(first + 1 + par, 8, stride=2), :] = src_ref[pl.ds(base + par * 8, 8), :]
        else:
            out_ref[pl.ds(first + 1, DEPTH), :] = src_ref[pl.ds(base, DEPTH), :]
        out_ref[pl.ds(first, 1), :] = src_ref[pl.ds(base + 15, 1), :]
        out_ref[pl.ds(first + 17, 1), :] = src_ref[pl.ds(base, 1), :]
        out_ref[pl.ds(first + 18, 6), :] = jnp.zeros((6, LANES), F32)
    for x in range(SIDE):
        out_ref[pl.ds(864 + x * 8, 8), :] = src_ref[pl.ds(x * 128 + 15, 8, stride=DEPTH), :]
        out_ref[pl.ds(928 + x * 8, 8), :] = src_ref[pl.ds(x * 128, 8, stride=DEPTH), :]


def to_chips(flat_ref, row_ref):
    for chip in range(32):
        row_ref[chip, 0:31, :] = flat_ref[pl.ds(chip * 31, 31), :]


def from_chips(row_ref, flat_ref):
    for chip in range(32):
        flat_ref[pl.ds(chip * 31, 31), :] = row_ref[chip, 0:31, :]


def lanes_of(rows):
    return lax.broadcasted_iota(jnp.int32, rows.shape, len(rows.shape) - 1)


def pack(row_ref, out_ref):
    extra = row_ref[:, 24:32]
    for part in range(3):
        rows = row_ref[:, part * 8 : part * 8 + 8]
        moved = pltpu.roll(extra, C - 32 * part, 2)
        out_ref[:, part * 8 : part * 8 + 8] = jnp.where(lanes_of(rows) < C, rows, moved).astype(BF16)


def slot_groups(ref):
    rows = ref[:, 0:24].astype(F32)
    groups = [rows[:, g * 8 : g * 8 + 8] for g in range(3)]
    lane = lanes_of(groups[0])
    moved = [pltpu.roll(rows, 32 * (part + 1), 2) for part, rows in enumerate(groups)]
    groups.append(jnp.where(lane < 32, moved[0], jnp.where(lane < 64, moved[1], moved[2])))
    return groups


def spread_kernel(nbr_hbm, f_hbm, table_hbm, out_ref, nbr_ref, f_ref, table_ref, sems, src_ref, flat_ref, row_ref):
    copies = [
        pltpu.make_async_copy(nbr_hbm, nbr_ref, sems.at[0]),
        pltpu.make_async_copy(f_hbm, f_ref, sems.at[1]),
        pltpu.make_async_copy(table_hbm, table_ref, sems.at[2]),
    ]
    for copy in copies:
        copy.start()
    copies[0].wait()
    copies[2].wait()
    table = table_ref[...]
    owner = jnp.full((32, LANES), -1, jnp.int32)
    for number in range(26):
        owner = jnp.where(table == number, nbr_ref[0, number], owner)
    row_ref[:, 31:32, :] = owner.astype(F32).reshape(32, 1, LANES)
    copies[1].wait()
    wide = jnp.concatenate([f_ref[...].astype(F32), jnp.zeros((LANES - C, VOX), F32)], axis=0)
    src_ref[...] = wide.T
    spread_rows(src_ref, flat_ref, False)
    to_chips(flat_ref, row_ref)
    pack(row_ref, out_ref)


def prepare_kernel(f_ref, own_ref):
    wide = jnp.concatenate([f_ref[...].astype(F32), jnp.zeros((LANES - C, VOX), F32)], axis=0)
    own_ref[...] = wide.T


def merge_kernel(halo_ref, keep_ref, other_ref, out_ref):
    pair = keep_ref[...] + other_ref[...].astype(F32)
    out_ref[:, 24:72] = pair[:MAIN_ROWS].reshape(32, 48, LANES).astype(BF16)
    free = pair[MAIN_ROWS:].reshape(16, 8, LANES)
    place = lax.broadcasted_iota(jnp.int32, (16, 8, LANES), 1)
    for part in range(3):
        rows = halo_ref[:, part * 8 : part * 8 + 8].astype(F32)
        added = jnp.where(place == 7, jnp.broadcast_to(free[:, part : part + 1], (16, 8, LANES)), 0.0)
        out_ref[0:16, part * 8 : part * 8 + 8] = (rows[:16] + added).astype(BF16)
        out_ref[16:32, part * 8 : part * 8 + 8] = rows[16:].astype(BF16)


def total_kernel(got_ref, part_ref, rows_ref):
    total = jnp.sum(got_ref[...].astype(F32), axis=0)
    for n in range(4):
        part_ref[n] = total
    rows_ref[...] = got_ref[:, 0:24]


def join_kernel(line_ref, rows_ref, out_ref):
    whole = line_ref[0] + line_ref[1] + line_ref[2] + line_ref[3]
    out_ref[:, 24:72] = jnp.broadcast_to(whole[24:], (32, 48, LANES)).astype(BF16)
    place = lax.broadcasted_iota(jnp.int32, (32, 24, LANES), 1) & 7
    rows = rows_ref[...].astype(F32)
    free = (place == 7) & (lanes_of(rows) >= C)
    out_ref[:, 0:24] = jnp.where(free, jnp.broadcast_to(whole[:24], rows.shape), rows).astype(BF16)


def route_kernel(core_ref, owner_ref, mine_ref, other_ref, out_ref, row_ref):
    core = core_ref[0]
    mine, other = slot_groups(mine_ref), slot_groups(other_ref)
    owners = jnp.broadcast_to(slot_groups(owner_ref)[3][:, 7:8, :], (32, 8, LANES))
    slot = lax.broadcasted_iota(jnp.int32, (32, 8, LANES), 1)
    for group in range(4):
        held = jnp.where(lanes_of(owners) == slot + group * 8, owners, 0.0)
        owner = jnp.sum(held, axis=2, keepdims=True).reshape(256, 1).astype(jnp.int32)
        place = lax.broadcasted_iota(jnp.int32, (256, 1), 0) & 7
        held = jnp.bitwise_and(owner, 1)
        spot = lax.shift_right_arithmetic(owner, 1) * 8 + place + jnp.where(held == core, 0, 256)
        spot = jnp.where(owner < 0, -1, spot)
        source = jnp.concatenate(
            [mine[group].reshape(256, LANES), other[group].reshape(256, LANES)], axis=0
        ).astype(BF16)
        row_ref[:, group * 8 : group * 8 + 8] = dot(one_hot(spot, 512), source).reshape(32, 8, LANES)
    pack(row_ref, out_ref)


def fill_halo(pad_ref, packed_ref, row_ref, halo_ref):
    for group, rows in enumerate(slot_groups(packed_ref)):
        row_ref[:, group * 8 : group * 8 + 8] = rows
    from_chips(row_ref, halo_ref)

    def put(first, count, place):
        pad_ref[pl.ds(first * COL, count * COL), :] = halo_ref[pl.ds(place * COL, count * COL), :]

    put(0, 11, 0)
    for x in range(1, 8):
        put(x * 10 + 9, 2, 11 + 2 * (x - 1))
    put(89, 11, 25)
    for x in range(SIDE):
        start = ((x + 1) * 10 + 1) * COL
        pad_ref[pl.ds(start, 8, stride=COL), :] = halo_ref[pl.ds(864 + x * 8, 8), :]
        pad_ref[pl.ds(start + DEPTH + 1, 8, stride=COL), :] = halo_ref[pl.ds(928 + x * 8, 8), :]


def shifted_columns(pad_ref, cols_ref):
    for x in range(10):
        for y in range(10):
            base = (x * 10 + y) * COL
            rows = [pad_ref[pl.ds(base + s, 8, stride=2), :] for s in range(4)]
            for dz in range(3):
                cols_ref[x, y, :, pl.ds(dz * LANES, LANES)] = jnp.concatenate(
                    [rows[dz], rows[dz + 1]], axis=0
                ).astype(BF16)


def window(cols_ref, dx, dy):
    return cols_ref[dx : dx + 8, dy : dy + 8].reshape(VOX, 3 * LANES)


def conv(cols_ref, w_ref):
    total = None
    for tap in range(9):
        part = dot(window(cols_ref, tap // 3, tap % 3), w_ref[tap])
        total = part if total is None else total + part
    return total


def forward_kernel(
    core_ref, own_ref, halo_ref, cot_ref, w_ref, dw_ref,
    grad_ref, patch_ref, keep_ref, send_ref,
    pad_ref, cols_ref, act_ref, row_ref, flat_ref, conv_ref, down_ref, free_ref,
):
    for x in range(SIDE):
        for y in range(SIDE):
            pad_ref[pl.ds(((x + 1) * 10 + y + 1) * COL + 1, DEPTH), :] = own_ref[
                pl.ds((x * 8 + y) * 16, 16), :
            ]
    fill_halo(pad_ref, halo_ref, row_ref, flat_ref)
    shifted_columns(pad_ref, cols_ref)
    act_ref[...] = conv(cols_ref, w_ref)
    back = dot(cot_ref[...], dw_ref[...], 0, 0)
    for j in range(8):
        jx, jy, jz = j // 4, j // 2 % 2, j % 2
        spots = [
            ((2 * ux + jx) * 8 + 2 * uy + jy) * 16 + jz * 8 for ux in range(4) for uy in range(4)
        ]
        a = jnp.concatenate([act_ref[pl.ds(s, 8), :] for s in spots], axis=0)
        g = 1.0 / (1.0 + jnp.exp(-a))
        patch_ref[:, pl.ds(j * LANES, LANES)] = (a * g).astype(BF16)
        slope = g * (1.0 + a * (1.0 - g))
        grad = back[:, j * LANES : (j + 1) * LANES] * slope
        for n, s in enumerate(spots):
            act_ref[pl.ds(s, 8), :] = grad[n * 8 : n * 8 + 8, :]
    grad_ref[...] = act_ref[...].astype(BF16)

    turned = act_ref[...].T[:C, :].astype(BF16)
    conv_ref[:, pl.ds(20 * LANES, LANES)] = jnp.zeros((C, LANES), F32)
    for tap in range(9):
        part = dot(turned, window(cols_ref, tap // 3, tap % 3))
        for dz in range(3):
            conv_ref[:, pl.ds((tap * 3 + dz) * C, C)] = part[:, dz * LANES : dz * LANES + C]
    part = dot(cot_ref[...], patch_ref[...])
    for j in range(8):
        down_ref[:, pl.ds(j * C, C)] = part[:, j * LANES : j * LANES + C]
    core = core_ref[0]
    for ref, half in ((keep_ref, core), (send_ref, 1 - core)):
        for lt in range(20):
            ref[pl.ds(lt * 48, 48), :] = conv_ref[
                pl.ds(pl.multiple_of(half * 48, 16), 48), pl.ds(lt * LANES, LANES)
            ].astype(ref.dtype)
        for lt in range(6):
            ref[pl.ds(960 + lt * 96, 96), :] = down_ref[
                pl.ds(pl.multiple_of(half * 96, 32), 96), pl.ds(lt * LANES, LANES)
            ].astype(ref.dtype)
        last = conv_ref[pl.ds(pl.multiple_of(half * 48, 16), 48), pl.ds(20 * LANES, LANES)]
        last = pltpu.roll(last, C, 1)
        free_ref[...] = jnp.zeros((16, 8, LANES), F32)
        for part in range(3):
            free_ref[:, part : part + 1, :] = last[part * 16 : part * 16 + 16, :].reshape(16, 1, LANES)
        ref[pl.ds(MAIN_ROWS, 128), :] = free_ref[...].reshape(128, LANES).astype(ref.dtype)


def side_kernel(grad_ref, patch_ref, dw_ref, send_ref, coarse_ref, src_ref, flat_ref, row_ref):
    src_ref[...] = grad_ref[...].astype(F32)
    spread_rows(src_ref, flat_ref, True)
    to_chips(flat_ref, row_ref)
    row_ref[:, 31:32, :] = jnp.zeros((32, 1, LANES), F32)
    pack(row_ref, send_ref)
    coarse_ref[...] = dot(dw_ref[...], patch_ref[...], 1, 1).astype(BF16)


def fetch_kernel(got_hbm, got_ref, sem):
    copy = pltpu.make_async_copy(got_hbm, got_ref, sem)
    copy.start()
    copy.wait()


def backward_kernel(grad_ref, halo_ref, w_ref, out_ref, pad_ref, cols_ref, act_ref, row_ref, flat_ref):
    for x in range(SIDE):
        for y in range(SIDE):
            base = ((x + 1) * 10 + y + 1) * COL
            for par in range(2):
                pad_ref[pl.ds(base + 1 + par, 8, stride=2), :] = grad_ref[
                    pl.ds((x * 8 + y) * 16 + par * 8, 8), :
                ].astype(F32)
    fill_halo(pad_ref, halo_ref, row_ref, flat_ref)
    shifted_columns(pad_ref, cols_ref)
    full = conv(cols_ref, w_ref)
    for n in range(64):
        for par in range(2):
            act_ref[pl.ds(n * 16 + par, 8, stride=2), :] = full[n * 16 + par * 8 : n * 16 + par * 8 + 8, :]
    out_ref[...] = act_ref[...].T[:C, :]


def finish_kernel(core_ref, mine_ref, other_ref, conv_ref, down_ref, last_ref):
    def squares(values):
        return jnp.sum((values * values).reshape(-1, 8, LANES), axis=0)

    conv_sum = jnp.zeros((8, LANES), F32)
    down_sum = jnp.zeros((8, LANES), F32)
    for n, ref in enumerate((mine_ref, other_ref)):
        conv_sum += squares(ref[0:CONV_CHIPS, 24:72, :].astype(F32))
        down_sum += squares(ref[CONV_CHIPS:32, 24:72, :].astype(F32))
        for part in range(3):
            rows = ref[0:16, part * 8 : part * 8 + 8, :].astype(F32)
            rows = pltpu.roll(rows, 32, 2)[:, 7:8, :].reshape(16, LANES)
            rows = jnp.where(lanes_of(rows) < 32, rows, 0.0)
            last_ref[n, pl.ds(part * 16, 16), :] = rows
            conv_sum += squares(rows)
    conv_scale = lax.rsqrt(jnp.sum(conv_sum, keepdims=True) * (1.0 / (C * 27 * C)) + EPSILON)
    down_scale = lax.rsqrt(jnp.sum(down_sum, keepdims=True) * (1.0 / (C2 * 8 * C)) + EPSILON)
    core = core_ref[0]
    for n, (ref, half) in enumerate(((mine_ref, core), (other_ref, 1 - core))):
        rows = pl.ds(pl.multiple_of(half * 48, 16), 48)
        for lt in range(20):
            conv_ref[rows, pl.ds(lt * LANES, LANES)] = ref[lt, 24:72, :].astype(F32) * conv_scale
        conv_ref[rows, pl.ds(20 * LANES, 32)] = (last_ref[n] * conv_scale)[:, :32]
        for lt in range(6):
            for part in range(2):
                rows = pl.ds(pl.multiple_of(half * 96 + part * 48, 16), 48)
                values = ref[CONV_CHIPS + lt * 2 + part, 24:72, :].astype(F32) * down_scale
                down_ref[rows, pl.ds(lt * LANES, LANES)] = values


def there(rows):
    return pltpu.with_memory_space_constraint(rows, pltpu.HBM)


def here(rows):
    return pltpu.with_memory_space_constraint(rows, pltpu.VMEM)


def call(body, outs, scratch=(), scalars=0, ins=0, name=None):
    specs = [pl.BlockSpec(memory_space=pltpu.SMEM)] * scalars + [
        pl.BlockSpec(memory_space=pltpu.VMEM)
    ] * ins
    return pl.pallas_call(
        body,
        out_shape=[
            jax.ShapeDtypeStruct(shape, kind) if leaves else pltpu.VMEM(shape, kind)
            for shape, kind, *leaves in outs
        ],
        in_specs=specs,
        out_specs=[pl.BlockSpec(memory_space=pltpu.VMEM)] * len(outs),
        scratch_shapes=list(scratch),
        compiler_params=PARAMS,
        name=name,
    )


CHIPS = ("y", "z")
SPACE = ("y", "z", "c")


def trade(rows, axes):
    return lax.all_to_all(rows, axes, 0, 0, tiled=True)


def shards(features, cotangent, conv_weight, down_weight, neighbours):
    block = features[0, 0]
    cot = cotangent[0, 0]
    core = lax.axis_index("c").astype(jnp.int32).reshape(1)
    rows_shape = ((VOX, LANES), BF16)
    by_chip = (32, 32, LANES)
    packed = (32, 24, LANES)
    flat_scratch = pltpu.VMEM((VOX, LANES), F32)
    slot_scratch = pltpu.VMEM(by_chip, F32)

    def swap(rows):
        return lax.ppermute(rows, "c", [(0, 1), (1, 0)])

    (spread,) = pl.pallas_call(
        spread_kernel,
        out_shape=[pltpu.VMEM(packed, BF16)],
        in_specs=[pl.BlockSpec(memory_space=pltpu.HBM)] * 3,
        out_specs=[pl.BlockSpec(memory_space=pltpu.VMEM)],
        scratch_shapes=[
            pltpu.SMEM((1, 26), jnp.int32),
            pltpu.VMEM((C, VOX), BF16),
            pltpu.VMEM((32, LANES), jnp.int32),
            pltpu.SemaphoreType.DMA((3,)),
            flat_scratch,
            flat_scratch,
            slot_scratch,
        ],
        compiler_params=PARAMS,
        name="spread",
    )(there(neighbours[0]), there(block), there(jnp.asarray(direction_table())))
    middle = here(trade(spread, CHIPS))
    route = call(route_kernel, [(packed, BF16)], [slot_scratch], scalars=1, ins=3, name="route")
    (routed,) = route(core, middle, middle, here(swap(middle)))
    halo = trade(routed, CHIPS)

    taps = conv_weight.reshape(C, 27, C)
    pad = ((0, 0), (0, LANES - C), (0, LANES - C))
    forward_w = jnp.pad(taps.transpose(1, 2, 0), pad).reshape(9, 3 * LANES, LANES)
    backward_w = jnp.pad(taps.transpose(1, 0, 2)[::-1], pad).reshape(9, 3 * LANES, LANES)
    down_w = jnp.pad(down_weight.reshape(C2, 8, C), ((0, 0), (0, 0), (0, LANES - C))).reshape(C2, 8 * LANES)
    (own,) = call(prepare_kernel, [((VOX, LANES), F32)], ins=1, name="prepare")(block)
    halo, forward_w, backward_w, down_w, own = lax.optimization_barrier(
        (halo, forward_w, backward_w, down_w, own)
    )
    forward_w, backward_w, down_w = here(forward_w), here(backward_w), here(down_w)

    pad_scratch = pltpu.VMEM((100 * COL, LANES), F32)
    cols_scratch = pltpu.VMEM((10, 10, DEPTH, 3 * LANES), BF16)
    grad, patch, keep, send = call(
        forward_kernel,
        [rows_shape, ((LANES, 8 * LANES), BF16), ((HALF_ROWS, LANES), F32), ((HALF_ROWS, LANES), BF16)],
        [
            pad_scratch,
            cols_scratch,
            flat_scratch,
            slot_scratch,
            flat_scratch,
            pltpu.VMEM((C, 21 * LANES), F32),
            pltpu.VMEM((C2, 8 * C), F32),
            pltpu.VMEM((16, 8, LANES), F32),
        ],
        scalars=1,
        ins=5,
        name="forward",
    )(core, here(own), here(halo), cot, forward_w, down_w)
    spread2, coarse = call(
        side_kernel, [(packed, BF16), ((C2, LANES), BF16, True)], [flat_scratch, flat_scratch, slot_scratch], ins=3, name="side"
    )(grad, patch, down_w)

    message = (32, 72, LANES)
    (out,) = call(merge_kernel, [(message, BF16)], ins=3, name="merge")(spread2, keep, here(swap(send)))
    part, middle2 = call(total_kernel, [((4, 72, LANES), F32), (packed, BF16)], ins=1, name="total")(
        there(trade(out, CHIPS))
    )
    other2, part = lax.optimization_barrier((swap(middle2), part))
    line = trade(part, "x")
    (routed2,) = route(core, middle, middle2, here(other2))
    (out,) = call(join_kernel, [(message, BF16)], ins=2, name="join")(here(line), routed2)
    (got,) = pl.pallas_call(
        fetch_kernel,
        out_shape=[pltpu.VMEM(message, BF16)],
        in_specs=[pl.BlockSpec(memory_space=pltpu.HBM)],
        out_specs=[pl.BlockSpec(memory_space=pltpu.VMEM)],
        scratch_shapes=[pltpu.SemaphoreType.DMA],
        compiler_params=PARAMS,
        name="fetch",
    )(there(trade(out, CHIPS)))
    theirs = swap(got)
    (grad_features,) = call(
        backward_kernel,
        [((C, VOX), F32, True)],
        [pad_scratch, cols_scratch, flat_scratch, slot_scratch, flat_scratch],
        ins=3,
        name="backward",
    )(grad, here(got), backward_w)
    grad_conv, grad_down = call(
        finish_kernel,
        [((C, 27 * C), F32, True), ((C2, 8 * C), F32, True)],
        [pltpu.VMEM((2, 48, LANES), F32)],
        scalars=1,
        ins=2,
        name="finish",
    )(core, here(got), here(theirs))
    return coarse[None, None], grad_features[None, None], grad_conv, grad_down


def solution(mesh):
    devices = mesh.devices
    fine = Mesh(devices.reshape(devices.shape[0], 4, -1, 2), ("x", "y", "z", "c"))
    block = P("x", SPACE, None, None)
    return jax.shard_map(
        shards,
        mesh=fine,
        in_specs=(block, block, P(), P(), P("x", SPACE, None)),
        out_specs=(block, block, P(), P()),
        check_vma=False,
    )
```

```python
import jax
import jax.numpy as jnp
import numpy as np
from jax import lax
from jax.experimental import pallas as pl
from jax.experimental.pallas import tpu as pltpu
from jax.sharding import Mesh, PartitionSpec as P

C = 96
C2 = 192
SIDE = 8
DEPTH = 16
VOX = 1024
LANES = 128
SLOTS = 992
COL = 24
MAIN_ROWS = 1536
HALF_ROWS = MAIN_ROWS + 128
CONV_CHIPS = 20
EPSILON = 1e-06
F32 = jnp.float32
BF16 = jnp.bfloat16
PARAMS = pltpu.CompilerParams(vmem_limit_bytes=32 << 20)


RIM = [(x, y) for x in range(10) for y in range(10) if x in (0, 9) or y in (0, 9)]


def side(position, extent):
    if position == 0:
        return -1, extent - 1
    if position == extent + 1:
        return 1, 0
    return 0, position - 1


def direction(ex, ey, ez):
    place = ((ex + 1) * 3 + ey + 1) * 3 + ez + 1
    return place - (place > 13)


def direction_table():
    table = np.full((32, LANES), -1, np.int32)

    def put(slot, px, py, pz):
        steps = (side(px, SIDE)[0], side(py, SIDE)[0], side(pz, DEPTH)[0])
        table[slot // 31, slot % 31] = direction(*steps)

    for place, (px, py) in enumerate(RIM):
        for pz in range(DEPTH + 2):
            put(place * COL + pz, px, py, pz)
    for n in range(64):
        put(864 + n, n // 8 + 1, n % 8 + 1, 0)
        put(928 + n, n // 8 + 1, n % 8 + 1, DEPTH + 1)
    return table


def one_hot(index, count):
    wide = lax.broadcasted_iota(jnp.int32, (index.shape[0], count), 1)
    return jnp.where(wide == index, 1.0, 0.0).astype(BF16)


def dot(a, b, ca=1, cb=0):
    return lax.dot_general(a, b, (((ca,), (cb,)), ((), ())), preferred_element_type=F32)


def spread_rows(src_ref, out_ref, parity):
    for place, (px, py) in enumerate(RIM):
        base = (side(px, SIDE)[1] * SIDE + side(py, SIDE)[1]) * DEPTH
        first = place * COL
        if parity:
            for par in range(2):
                out_ref[pl.ds(first + 1 + par, 8, stride=2), :] = src_ref[pl.ds(base + par * 8, 8), :]
        else:
            out_ref[pl.ds(first + 1, DEPTH), :] = src_ref[pl.ds(base, DEPTH), :]
        out_ref[pl.ds(first, 1), :] = src_ref[pl.ds(base + 15, 1), :]
        out_ref[pl.ds(first + 17, 1), :] = src_ref[pl.ds(base, 1), :]
        out_ref[pl.ds(first + 18, 6), :] = jnp.zeros((6, LANES), F32)
    for x in range(SIDE):
        out_ref[pl.ds(864 + x * 8, 8), :] = src_ref[pl.ds(x * 128 + 15, 8, stride=DEPTH), :]
        out_ref[pl.ds(928 + x * 8, 8), :] = src_ref[pl.ds(x * 128, 8, stride=DEPTH), :]


def to_chips(flat_ref, row_ref):
    for chip in range(32):
        row_ref[chip, 0:31, :] = flat_ref[pl.ds(chip * 31, 31), :]


def from_chips(row_ref, flat_ref):
    for chip in range(32):
        flat_ref[pl.ds(chip * 31, 31), :] = row_ref[chip, 0:31, :]


def lanes_of(rows):
    return lax.broadcasted_iota(jnp.int32, rows.shape, len(rows.shape) - 1)


def pack(row_ref, out_ref):
    extra = row_ref[:, 24:32]
    for part in range(3):
        rows = row_ref[:, part * 8 : part * 8 + 8]
        moved = pltpu.roll(extra, C - 32 * part, 2)
        out_ref[:, part * 8 : part * 8 + 8] = jnp.where(lanes_of(rows) < C, rows, moved).astype(BF16)


def slot_groups(ref):
    rows = ref[:, 0:24].astype(F32)
    groups = [rows[:, g * 8 : g * 8 + 8] for g in range(3)]
    lane = lanes_of(groups[0])
    moved = [pltpu.roll(rows, 32 * (part + 1), 2) for part, rows in enumerate(groups)]
    groups.append(jnp.where(lane < 32, moved[0], jnp.where(lane < 64, moved[1], moved[2])))
    return groups


def spread_kernel(nbr_hbm, f_hbm, table_hbm, out_ref, nbr_ref, f_ref, table_ref, sems, src_ref, flat_ref, row_ref):
    copies = [
        pltpu.make_async_copy(nbr_hbm, nbr_ref, sems.at[0]),
        pltpu.make_async_copy(f_hbm, f_ref, sems.at[1]),
        pltpu.make_async_copy(table_hbm, table_ref, sems.at[2]),
    ]
    for copy in copies:
        copy.start()
    copies[0].wait()
    copies[2].wait()
    table = table_ref[...]
    owner = jnp.full((32, LANES), -1, jnp.int32)
    for number in range(26):
        owner = jnp.where(table == number, nbr_ref[0, number], owner)
    row_ref[:, 31:32, :] = owner.astype(F32).reshape(32, 1, LANES)
    copies[1].wait()
    wide = jnp.concatenate([f_ref[...].astype(F32), jnp.zeros((LANES - C, VOX), F32)], axis=0)
    src_ref[...] = wide.T
    spread_rows(src_ref, flat_ref, False)
    to_chips(flat_ref, row_ref)
    pack(row_ref, out_ref)


def prepare_kernel(f_ref, own_ref):
    wide = jnp.concatenate([f_ref[...].astype(F32), jnp.zeros((LANES - C, VOX), F32)], axis=0)
    own_ref[...] = wide.T


def merge_kernel(halo_ref, keep_ref, other_ref, out_ref):
    pair = keep_ref[...] + other_ref[...].astype(F32)
    out_ref[:, 24:72] = pair[:MAIN_ROWS].reshape(32, 48, LANES).astype(BF16)
    free = pair[MAIN_ROWS:].reshape(16, 8, LANES)
    place = lax.broadcasted_iota(jnp.int32, (16, 8, LANES), 1)
    for part in range(3):
        rows = halo_ref[:, part * 8 : part * 8 + 8].astype(F32)
        added = jnp.where(place == 7, jnp.broadcast_to(free[:, part : part + 1], (16, 8, LANES)), 0.0)
        out_ref[0:16, part * 8 : part * 8 + 8] = (rows[:16] + added).astype(BF16)
        out_ref[16:32, part * 8 : part * 8 + 8] = rows[16:].astype(BF16)


def total_kernel(got_ref, part_ref, rows_ref):
    total = jnp.sum(got_ref[...].astype(F32), axis=0)
    for n in range(4):
        part_ref[n] = total
    rows_ref[...] = got_ref[:, 0:24]


def join_kernel(line_ref, rows_ref, out_ref):
    whole = line_ref[0] + line_ref[1] + line_ref[2] + line_ref[3]
    out_ref[:, 24:72] = jnp.broadcast_to(whole[24:], (32, 48, LANES)).astype(BF16)
    place = lax.broadcasted_iota(jnp.int32, (32, 24, LANES), 1) & 7
    rows = rows_ref[...].astype(F32)
    free = (place == 7) & (lanes_of(rows) >= C)
    out_ref[:, 0:24] = jnp.where(free, jnp.broadcast_to(whole[:24], rows.shape), rows).astype(BF16)


def route_kernel(core_ref, owner_ref, mine_ref, other_ref, out_ref, row_ref):
    core = core_ref[0]
    mine, other = slot_groups(mine_ref), slot_groups(other_ref)
    owners = jnp.broadcast_to(slot_groups(owner_ref)[3][:, 7:8, :], (32, 8, LANES))
    slot = lax.broadcasted_iota(jnp.int32, (32, 8, LANES), 1)
    for group in range(4):
        held = jnp.where(lanes_of(owners) == slot + group * 8, owners, 0.0)
        owner = jnp.sum(held, axis=2, keepdims=True).reshape(256, 1).astype(jnp.int32)
        place = lax.broadcasted_iota(jnp.int32, (256, 1), 0) & 7
        held = jnp.bitwise_and(owner, 1)
        spot = lax.shift_right_arithmetic(owner, 1) * 8 + place + jnp.where(held == core, 0, 256)
        spot = jnp.where(owner < 0, -1, spot)
        source = jnp.concatenate(
            [mine[group].reshape(256, LANES), other[group].reshape(256, LANES)], axis=0
        ).astype(BF16)
        row_ref[:, group * 8 : group * 8 + 8] = dot(one_hot(spot, 512), source).reshape(32, 8, LANES)
    pack(row_ref, out_ref)


def fill_halo(pad_ref, packed_ref, row_ref, halo_ref):
    for group, rows in enumerate(slot_groups(packed_ref)):
        row_ref[:, group * 8 : group * 8 + 8] = rows
    from_chips(row_ref, halo_ref)

    def put(first, count, place):
        pad_ref[pl.ds(first * COL, count * COL), :] = halo_ref[pl.ds(place * COL, count * COL), :]

    put(0, 11, 0)
    for x in range(1, 8):
        put(x * 10 + 9, 2, 11 + 2 * (x - 1))
    put(89, 11, 25)
    for x in range(SIDE):
        start = ((x + 1) * 10 + 1) * COL
        pad_ref[pl.ds(start, 8, stride=COL), :] = halo_ref[pl.ds(864 + x * 8, 8), :]
        pad_ref[pl.ds(start + DEPTH + 1, 8, stride=COL), :] = halo_ref[pl.ds(928 + x * 8, 8), :]


def shifted_columns(pad_ref, cols_ref):
    for x in range(10):
        for y in range(10):
            base = (x * 10 + y) * COL
            rows = [pad_ref[pl.ds(base + s, 8, stride=2), :] for s in range(4)]
            for dz in range(3):
                cols_ref[x, y, :, pl.ds(dz * LANES, LANES)] = jnp.concatenate(
                    [rows[dz], rows[dz + 1]], axis=0
                ).astype(BF16)


def window(cols_ref, dx, dy):
    return cols_ref[dx : dx + 8, dy : dy + 8].reshape(VOX, 3 * LANES)


def conv(cols_ref, w_ref):
    total = None
    for tap in range(9):
        part = dot(window(cols_ref, tap // 3, tap % 3), w_ref[tap])
        total = part if total is None else total + part
    return total


def planes(cols_ref, first, last, dy):
    return cols_ref[first:last, dy : dy + 8].reshape((last - first) * LANES, 3 * LANES)


def conv_wide(cols_ref, w_ref):
    both = last = 0.0
    for dy in range(3):
        pair = jnp.concatenate([w_ref[dy], w_ref[3 + dy]], axis=1)
        both = both + dot(planes(cols_ref, 0, 9, dy), pair)
        last = last + dot(planes(cols_ref, 2, 10, dy), w_ref[6 + dy])
    return both[:VOX, :LANES] + both[LANES:, LANES:] + last


def forward_kernel(
    core_ref, own_ref, halo_ref, cot_ref, w_ref, dw_ref,
    grad_ref, patch_ref, keep_ref, send_ref,
    pad_ref, cols_ref, act_ref, row_ref, flat_ref, conv_ref, down_ref, free_ref,
):
    for x in range(SIDE):
        for y in range(SIDE):
            pad_ref[pl.ds(((x + 1) * 10 + y + 1) * COL + 1, DEPTH), :] = own_ref[
                pl.ds((x * 8 + y) * 16, 16), :
            ]
    fill_halo(pad_ref, halo_ref, row_ref, flat_ref)
    shifted_columns(pad_ref, cols_ref)
    act_ref[...] = conv(cols_ref, w_ref)
    back = dot(cot_ref[...], dw_ref[...], 0, 0)
    for j in range(8):
        jx, jy, jz = j // 4, j // 2 % 2, j % 2
        spots = [
            ((2 * ux + jx) * 8 + 2 * uy + jy) * 16 + jz * 8 for ux in range(4) for uy in range(4)
        ]
        a = jnp.concatenate([act_ref[pl.ds(s, 8), :] for s in spots], axis=0)
        g = 1.0 / (1.0 + jnp.exp(-a))
        patch_ref[:, pl.ds(j * LANES, LANES)] = (a * g).astype(BF16)
        slope = g * (1.0 + a * (1.0 - g))
        grad = back[:, j * LANES : (j + 1) * LANES] * slope
        for n, s in enumerate(spots):
            act_ref[pl.ds(s, 8), :] = grad[n * 8 : n * 8 + 8, :]
    grad_ref[...] = act_ref[...].astype(BF16)

    turned = act_ref[...].T[:C, :].astype(BF16)
    conv_ref[:, pl.ds(20 * LANES, LANES)] = jnp.zeros((C, LANES), F32)
    for tap in range(9):
        part = dot(turned, window(cols_ref, tap // 3, tap % 3))
        for dz in range(3):
            conv_ref[:, pl.ds((tap * 3 + dz) * C, C)] = part[:, dz * LANES : dz * LANES + C]
    part = dot(cot_ref[...], patch_ref[...])
    for j in range(8):
        down_ref[:, pl.ds(j * C, C)] = part[:, j * LANES : j * LANES + C]
    core = core_ref[0]
    for ref, half in ((keep_ref, core), (send_ref, 1 - core)):
        for lt in range(20):
            ref[pl.ds(lt * 48, 48), :] = conv_ref[
                pl.ds(pl.multiple_of(half * 48, 16), 48), pl.ds(lt * LANES, LANES)
            ].astype(ref.dtype)
        for lt in range(6):
            ref[pl.ds(960 + lt * 96, 96), :] = down_ref[
                pl.ds(pl.multiple_of(half * 96, 32), 96), pl.ds(lt * LANES, LANES)
            ].astype(ref.dtype)
        last = conv_ref[pl.ds(pl.multiple_of(half * 48, 16), 48), pl.ds(20 * LANES, LANES)]
        last = pltpu.roll(last, C, 1)
        free_ref[...] = jnp.zeros((16, 8, LANES), F32)
        for part in range(3):
            free_ref[:, part : part + 1, :] = last[part * 16 : part * 16 + 16, :].reshape(16, 1, LANES)
        ref[pl.ds(MAIN_ROWS, 128), :] = free_ref[...].reshape(128, LANES).astype(ref.dtype)


def side_kernel(grad_ref, patch_ref, dw_ref, send_ref, coarse_ref, src_ref, flat_ref, row_ref):
    src_ref[...] = grad_ref[...].astype(F32)
    spread_rows(src_ref, flat_ref, True)
    to_chips(flat_ref, row_ref)
    row_ref[:, 31:32, :] = jnp.zeros((32, 1, LANES), F32)
    pack(row_ref, send_ref)
    coarse_ref[...] = dot(dw_ref[...], patch_ref[...], 1, 1).astype(BF16)


def backward_kernel(grad_ref, halo_ref, w_ref, out_ref, pad_ref, cols_ref, act_ref, row_ref, flat_ref):
    for x in range(SIDE):
        for y in range(SIDE):
            base = ((x + 1) * 10 + y + 1) * COL
            for par in range(2):
                pad_ref[pl.ds(base + 1 + par, 8, stride=2), :] = grad_ref[
                    pl.ds((x * 8 + y) * 16 + par * 8, 8), :
                ].astype(F32)
    fill_halo(pad_ref, halo_ref, row_ref, flat_ref)
    shifted_columns(pad_ref, cols_ref)
    full = conv_wide(cols_ref, w_ref)
    for n in range(64):
        for par in range(2):
            act_ref[pl.ds(n * 16 + par, 8, stride=2), :] = full[n * 16 + par * 8 : n * 16 + par * 8 + 8, :]
    out_ref[...] = act_ref[...].T[:C, :]


def finish_kernel(core_ref, mine_ref, other_ref, conv_ref, down_ref, last_ref):
    def squares(values):
        return jnp.sum((values * values).reshape(-1, 8, LANES), axis=0)

    conv_sum = jnp.zeros((8, LANES), F32)
    down_sum = jnp.zeros((8, LANES), F32)
    for n, ref in enumerate((mine_ref, other_ref)):
        conv_sum += squares(ref[0:CONV_CHIPS, 24:72, :].astype(F32))
        down_sum += squares(ref[CONV_CHIPS:32, 24:72, :].astype(F32))
        for part in range(3):
            rows = ref[0:16, part * 8 : part * 8 + 8, :].astype(F32)
            rows = pltpu.roll(rows, 32, 2)[:, 7:8, :].reshape(16, LANES)
            rows = jnp.where(lanes_of(rows) < 32, rows, 0.0)
            last_ref[n, pl.ds(part * 16, 16), :] = rows
            conv_sum += squares(rows)
    conv_scale = lax.rsqrt(jnp.sum(conv_sum, keepdims=True) * (1.0 / (C * 27 * C)) + EPSILON)
    down_scale = lax.rsqrt(jnp.sum(down_sum, keepdims=True) * (1.0 / (C2 * 8 * C)) + EPSILON)
    core = core_ref[0]
    for n, (ref, half) in enumerate(((mine_ref, core), (other_ref, 1 - core))):
        rows = pl.ds(pl.multiple_of(half * 48, 16), 48)
        for lt in range(20):
            conv_ref[rows, pl.ds(lt * LANES, LANES)] = ref[lt, 24:72, :].astype(F32) * conv_scale
        conv_ref[rows, pl.ds(20 * LANES, 32)] = (last_ref[n] * conv_scale)[:, :32]
        for lt in range(6):
            for part in range(2):
                rows = pl.ds(pl.multiple_of(half * 96 + part * 48, 16), 48)
                values = ref[CONV_CHIPS + lt * 2 + part, 24:72, :].astype(F32) * down_scale
                down_ref[rows, pl.ds(lt * LANES, LANES)] = values


def there(rows):
    return pltpu.with_memory_space_constraint(rows, pltpu.HBM)


def here(rows):
    return pltpu.with_memory_space_constraint(rows, pltpu.VMEM)


def call(body, outs, scratch=(), scalars=0, ins=0, name=None):
    specs = [pl.BlockSpec(memory_space=pltpu.SMEM)] * scalars + [
        pl.BlockSpec(memory_space=pltpu.VMEM)
    ] * ins
    return pl.pallas_call(
        body,
        out_shape=[
            jax.ShapeDtypeStruct(shape, kind) if leaves else pltpu.VMEM(shape, kind)
            for shape, kind, *leaves in outs
        ],
        in_specs=specs,
        out_specs=[pl.BlockSpec(memory_space=pltpu.VMEM)] * len(outs),
        scratch_shapes=list(scratch),
        compiler_params=PARAMS,
        name=name,
    )


CHIPS = ("y", "z")
SPACE = ("y", "z", "c")


def trade(rows, axes):
    return lax.all_to_all(rows, axes, 0, 0, tiled=True)


def shards(features, cotangent, conv_weight, down_weight, neighbours):
    block = features[0, 0]
    cot = cotangent[0, 0]
    core = lax.axis_index("c").astype(jnp.int32).reshape(1)
    rows_shape = ((VOX, LANES), BF16)
    by_chip = (32, 32, LANES)
    packed = (32, 24, LANES)
    flat_scratch = pltpu.VMEM((VOX, LANES), F32)
    slot_scratch = pltpu.VMEM(by_chip, F32)

    def swap(rows):
        return lax.ppermute(rows, "c", [(0, 1), (1, 0)])

    (spread,) = pl.pallas_call(
        spread_kernel,
        out_shape=[pltpu.VMEM(packed, BF16)],
        in_specs=[pl.BlockSpec(memory_space=pltpu.HBM)] * 3,
        out_specs=[pl.BlockSpec(memory_space=pltpu.VMEM)],
        scratch_shapes=[
            pltpu.SMEM((1, 26), jnp.int32),
            pltpu.VMEM((C, VOX), BF16),
            pltpu.VMEM((32, LANES), jnp.int32),
            pltpu.SemaphoreType.DMA((3,)),
            flat_scratch,
            flat_scratch,
            slot_scratch,
        ],
        compiler_params=PARAMS,
        name="spread",
    )(there(neighbours[0]), there(block), there(jnp.asarray(direction_table())))
    middle = here(trade(spread, CHIPS))
    route = call(route_kernel, [(packed, BF16)], [slot_scratch], scalars=1, ins=3, name="route")
    (routed,) = route(core, middle, middle, here(swap(middle)))
    halo = trade(routed, CHIPS)

    taps = conv_weight.reshape(C, 27, C)
    pad = ((0, 0), (0, LANES - C), (0, LANES - C))
    forward_w = jnp.pad(taps.transpose(1, 2, 0), pad).reshape(9, 3 * LANES, LANES)
    backward_w = jnp.pad(taps.transpose(1, 0, 2)[::-1], pad).reshape(9, 3 * LANES, LANES)
    down_w = jnp.pad(down_weight.reshape(C2, 8, C), ((0, 0), (0, 0), (0, LANES - C))).reshape(C2, 8 * LANES)
    (own,) = call(prepare_kernel, [((VOX, LANES), F32)], ins=1, name="prepare")(block)
    halo, forward_w, backward_w, down_w, own = lax.optimization_barrier(
        (halo, forward_w, backward_w, down_w, own)
    )
    forward_w, backward_w, down_w = here(forward_w), here(backward_w), here(down_w)

    pad_scratch = pltpu.VMEM((100 * COL, LANES), F32)
    cols_scratch = pltpu.VMEM((10, 10, DEPTH, 3 * LANES), BF16)
    grad, patch, keep, send = call(
        forward_kernel,
        [rows_shape, ((LANES, 8 * LANES), BF16), ((HALF_ROWS, LANES), F32), ((HALF_ROWS, LANES), BF16)],
        [
            pad_scratch,
            cols_scratch,
            flat_scratch,
            slot_scratch,
            flat_scratch,
            pltpu.VMEM((C, 21 * LANES), F32),
            pltpu.VMEM((C2, 8 * C), F32),
            pltpu.VMEM((16, 8, LANES), F32),
        ],
        scalars=1,
        ins=5,
        name="forward",
    )(core, here(own), here(halo), cot, forward_w, down_w)
    spread2, coarse = call(
        side_kernel, [(packed, BF16), ((C2, LANES), BF16, True)], [flat_scratch, flat_scratch, slot_scratch], ins=3, name="side"
    )(grad, patch, down_w)

    message = (32, 72, LANES)
    (out,) = call(merge_kernel, [(message, BF16)], ins=3, name="merge")(spread2, keep, here(swap(send)))
    part, middle2 = call(total_kernel, [((4, 72, LANES), F32), (packed, BF16)], ins=1, name="total")(
        here(trade(out, CHIPS))
    )
    other2 = swap(middle2)
    line = trade(part, "x")
    (routed2,) = route(core, middle, middle2, here(other2))
    (out,) = call(join_kernel, [(message, BF16)], ins=2, name="join")(here(line), routed2)
    got = trade(out, CHIPS)
    theirs = swap(got)
    (grad_features,) = call(
        backward_kernel,
        [((C, VOX), F32, True)],
        [pad_scratch, cols_scratch, flat_scratch, slot_scratch, flat_scratch],
        ins=3,
        name="backward",
    )(grad, here(got), backward_w)
    grad_conv, grad_down = call(
        finish_kernel,
        [((C, 27 * C), F32, True), ((C2, 8 * C), F32, True)],
        [pltpu.VMEM((2, 48, LANES), F32)],
        scalars=1,
        ins=2,
        name="finish",
    )(core, here(got), here(theirs))
    return coarse[None, None], grad_features[None, None], grad_conv, grad_down


def solution(mesh):
    devices = mesh.devices
    fine = Mesh(devices.reshape(devices.shape[0], 4, -1, 2), ("x", "y", "z", "c"))
    block = P("x", SPACE, None, None)
    return jax.shard_map(
        shards,
        mesh=fine,
        in_specs=(block, block, P(), P(), P("x", SPACE, None)),
        out_specs=(block, block, P(), P()),
        check_vma=False,
    )
```

```python
import jax
import jax.numpy as jnp
import numpy as np
from jax import lax
from jax.experimental import pallas as pl
from jax.experimental.pallas import tpu as pltpu
from jax.sharding import Mesh, PartitionSpec as P

C = 96
C2 = 192
SIDE = 8
DEPTH = 16
VOX = 1024
LANES = 128
SLOTS = 992
COL = 24
MAIN_ROWS = 1536
HALF_ROWS = MAIN_ROWS + 128
CONV_CHIPS = 20
EPSILON = 1e-06
F32 = jnp.float32
BF16 = jnp.bfloat16
PARAMS = pltpu.CompilerParams(vmem_limit_bytes=32 << 20)


RIM = [(x, y) for x in range(10) for y in range(10) if x in (0, 9) or y in (0, 9)]


def side(position, extent):
    if position == 0:
        return -1, extent - 1
    if position == extent + 1:
        return 1, 0
    return 0, position - 1


def direction(ex, ey, ez):
    place = ((ex + 1) * 3 + ey + 1) * 3 + ez + 1
    return place - (place > 13)


def direction_table():
    table = np.full((32, LANES), -1, np.int32)

    def put(slot, px, py, pz):
        steps = (side(px, SIDE)[0], side(py, SIDE)[0], side(pz, DEPTH)[0])
        table[slot // 31, slot % 31] = direction(*steps)

    for place, (px, py) in enumerate(RIM):
        for pz in range(DEPTH + 2):
            put(place * COL + pz, px, py, pz)
    for n in range(64):
        put(864 + n, n // 8 + 1, n % 8 + 1, 0)
        put(928 + n, n // 8 + 1, n % 8 + 1, DEPTH + 1)
    return table


def one_hot(index, count):
    wide = lax.broadcasted_iota(jnp.int32, (index.shape[0], count), 1)
    return jnp.where(wide == index, 1.0, 0.0).astype(BF16)


def dot(a, b, ca=1, cb=0):
    return lax.dot_general(a, b, (((ca,), (cb,)), ((), ())), preferred_element_type=F32)


def spread_rows(src_ref, out_ref, parity):
    for place, (px, py) in enumerate(RIM):
        base = (side(px, SIDE)[1] * SIDE + side(py, SIDE)[1]) * DEPTH
        first = place * COL
        if parity:
            for par in range(2):
                out_ref[pl.ds(first + 1 + par, 8, stride=2), :] = src_ref[pl.ds(base + par * 8, 8), :]
        else:
            out_ref[pl.ds(first + 1, DEPTH), :] = src_ref[pl.ds(base, DEPTH), :]
        out_ref[pl.ds(first, 1), :] = src_ref[pl.ds(base + 15, 1), :]
        out_ref[pl.ds(first + 17, 1), :] = src_ref[pl.ds(base, 1), :]
        out_ref[pl.ds(first + 18, 6), :] = jnp.zeros((6, LANES), F32)
    for x in range(SIDE):
        out_ref[pl.ds(864 + x * 8, 8), :] = src_ref[pl.ds(x * 128 + 15, 8, stride=DEPTH), :]
        out_ref[pl.ds(928 + x * 8, 8), :] = src_ref[pl.ds(x * 128, 8, stride=DEPTH), :]


def to_chips(flat_ref, row_ref):
    for chip in range(32):
        row_ref[chip, 0:31, :] = flat_ref[pl.ds(chip * 31, 31), :]


def from_chips(row_ref, flat_ref):
    for chip in range(32):
        flat_ref[pl.ds(chip * 31, 31), :] = row_ref[chip, 0:31, :]


def lanes_of(rows):
    return lax.broadcasted_iota(jnp.int32, rows.shape, len(rows.shape) - 1)


def pack(row_ref, out_ref):
    extra = row_ref[:, 24:32]
    for part in range(3):
        rows = row_ref[:, part * 8 : part * 8 + 8]
        moved = pltpu.roll(extra, C - 32 * part, 2)
        out_ref[:, part * 8 : part * 8 + 8] = jnp.where(lanes_of(rows) < C, rows, moved).astype(BF16)


def slot_groups(ref):
    rows = ref[:, 0:24].astype(F32)
    groups = [rows[:, g * 8 : g * 8 + 8] for g in range(3)]
    lane = lanes_of(groups[0])
    moved = [pltpu.roll(rows, 32 * (part + 1), 2) for part, rows in enumerate(groups)]
    groups.append(jnp.where(lane < 32, moved[0], jnp.where(lane < 64, moved[1], moved[2])))
    return groups


def spread_kernel(nbr_hbm, f_hbm, table_hbm, out_ref, nbr_ref, f_ref, table_ref, sems, src_ref, flat_ref, row_ref):
    copies = [
        pltpu.make_async_copy(nbr_hbm, nbr_ref, sems.at[0]),
        pltpu.make_async_copy(f_hbm, f_ref, sems.at[1]),
        pltpu.make_async_copy(table_hbm, table_ref, sems.at[2]),
    ]
    for copy in copies:
        copy.start()
    copies[0].wait()
    copies[2].wait()
    table = table_ref[...]
    owner = jnp.full((32, LANES), -1, jnp.int32)
    for number in range(26):
        owner = jnp.where(table == number, nbr_ref[0, number], owner)
    row_ref[:, 31:32, :] = owner.astype(F32).reshape(32, 1, LANES)
    copies[1].wait()
    wide = jnp.concatenate([f_ref[...].astype(F32), jnp.zeros((LANES - C, VOX), F32)], axis=0)
    src_ref[...] = wide.T
    spread_rows(src_ref, flat_ref, False)
    to_chips(flat_ref, row_ref)
    pack(row_ref, out_ref)


def prepare_kernel(f_ref, own_ref):
    wide = jnp.concatenate([f_ref[...].astype(F32), jnp.zeros((LANES - C, VOX), F32)], axis=0)
    own_ref[...] = wide.T


def merge_kernel(halo_ref, keep_ref, other_ref, out_ref):
    pair = keep_ref[...] + other_ref[...].astype(F32)
    out_ref[:, 24:72] = pair[:MAIN_ROWS].reshape(32, 48, LANES).astype(BF16)
    free = pair[MAIN_ROWS:].reshape(16, 8, LANES)
    place = lax.broadcasted_iota(jnp.int32, (16, 8, LANES), 1)
    for part in range(3):
        rows = halo_ref[:, part * 8 : part * 8 + 8].astype(F32)
        added = jnp.where(place == 7, jnp.broadcast_to(free[:, part : part + 1], (16, 8, LANES)), 0.0)
        out_ref[0:16, part * 8 : part * 8 + 8] = (rows[:16] + added).astype(BF16)
        out_ref[16:32, part * 8 : part * 8 + 8] = rows[16:].astype(BF16)


def total_kernel(got_ref, part_ref, rows_ref):
    total = jnp.sum(got_ref[...].astype(F32), axis=0)
    for n in range(4):
        part_ref[n, 0:48] = total[24:]
        part_ref[n, 48:56] = jnp.zeros((8, LANES), F32)
        for part in range(3):
            part_ref[n, 48 + part : 49 + part] = total[part * 8 + 7 : part * 8 + 8]
    rows_ref[...] = got_ref[:, 0:24]


def join_kernel(line_ref, rows_ref, out_ref):
    whole = line_ref[0] + line_ref[1] + line_ref[2] + line_ref[3]
    out_ref[:, 24:72] = jnp.broadcast_to(whole[:48], (32, 48, LANES)).astype(BF16)
    place = lax.broadcasted_iota(jnp.int32, (32, 8, LANES), 1)
    for part in range(3):
        rows = rows_ref[:, part * 8 : part * 8 + 8].astype(F32)
        free = (place == 7) & (lanes_of(rows) >= C)
        last = jnp.broadcast_to(whole[48 + part : 49 + part], rows.shape)
        out_ref[:, part * 8 : part * 8 + 8] = jnp.where(free, last, rows).astype(BF16)


def route_kernel(core_ref, owner_ref, mine_ref, other_ref, out_ref, row_ref):
    core = core_ref[0]
    mine, other = slot_groups(mine_ref), slot_groups(other_ref)
    owners = jnp.broadcast_to(slot_groups(owner_ref)[3][:, 7:8, :], (32, 8, LANES))
    slot = lax.broadcasted_iota(jnp.int32, (32, 8, LANES), 1)
    for group in range(4):
        held = jnp.where(lanes_of(owners) == slot + group * 8, owners, 0.0)
        owner = jnp.sum(held, axis=2, keepdims=True).reshape(256, 1).astype(jnp.int32)
        place = lax.broadcasted_iota(jnp.int32, (256, 1), 0) & 7
        held = jnp.bitwise_and(owner, 1)
        spot = lax.shift_right_arithmetic(owner, 1) * 8 + place + jnp.where(held == core, 0, 256)
        spot = jnp.where(owner < 0, -1, spot)
        source = jnp.concatenate(
            [mine[group].reshape(256, LANES), other[group].reshape(256, LANES)], axis=0
        ).astype(BF16)
        row_ref[:, group * 8 : group * 8 + 8] = dot(one_hot(spot, 512), source).reshape(32, 8, LANES)
    pack(row_ref, out_ref)


def fill_halo(pad_ref, packed_ref, row_ref, halo_ref):
    for group, rows in enumerate(slot_groups(packed_ref)):
        row_ref[:, group * 8 : group * 8 + 8] = rows
    from_chips(row_ref, halo_ref)

    def put(first, count, place):
        pad_ref[pl.ds(first * COL, count * COL), :] = halo_ref[pl.ds(place * COL, count * COL), :]

    put(0, 11, 0)
    for x in range(1, 8):
        put(x * 10 + 9, 2, 11 + 2 * (x - 1))
    put(89, 11, 25)
    for x in range(SIDE):
        start = ((x + 1) * 10 + 1) * COL
        pad_ref[pl.ds(start, 8, stride=COL), :] = halo_ref[pl.ds(864 + x * 8, 8), :]
        pad_ref[pl.ds(start + DEPTH + 1, 8, stride=COL), :] = halo_ref[pl.ds(928 + x * 8, 8), :]


def shifted_columns(pad_ref, cols_ref):
    for x in range(10):
        for y in range(10):
            base = (x * 10 + y) * COL
            rows = [pad_ref[pl.ds(base + s, 8, stride=2), :] for s in range(4)]
            for dz in range(3):
                cols_ref[x, y, :, pl.ds(dz * LANES, LANES)] = jnp.concatenate(
                    [rows[dz], rows[dz + 1]], axis=0
                ).astype(BF16)


def window(cols_ref, dx, dy):
    return cols_ref[dx : dx + 8, dy : dy + 8].reshape(VOX, 3 * LANES)


def conv(cols_ref, w_ref):
    total = None
    for tap in range(9):
        part = dot(window(cols_ref, tap // 3, tap % 3), w_ref[tap])
        total = part if total is None else total + part
    return total


def planes(cols_ref, first, last, dy):
    return cols_ref[first:last, dy : dy + 8].reshape((last - first) * LANES, 3 * LANES)


def conv_wide(cols_ref, w_ref):
    both = last = 0.0
    for dy in range(3):
        pair = jnp.concatenate([w_ref[dy], w_ref[3 + dy]], axis=1)
        both = both + dot(planes(cols_ref, 0, 9, dy), pair)
        last = last + dot(planes(cols_ref, 2, 10, dy), w_ref[6 + dy])
    return both[:VOX, :LANES] + both[LANES:, LANES:] + last


def forward_kernel(
    core_ref, own_ref, halo_ref, cot_ref, w_ref, dw_ref,
    grad_ref, patch_ref, keep_ref, send_ref,
    pad_ref, cols_ref, act_ref, row_ref, flat_ref, conv_ref, down_ref, free_ref,
):
    for x in range(SIDE):
        for y in range(SIDE):
            pad_ref[pl.ds(((x + 1) * 10 + y + 1) * COL + 1, DEPTH), :] = own_ref[
                pl.ds((x * 8 + y) * 16, 16), :
            ]
    fill_halo(pad_ref, halo_ref, row_ref, flat_ref)
    shifted_columns(pad_ref, cols_ref)
    act_ref[...] = conv(cols_ref, w_ref)
    back = dot(cot_ref[...], dw_ref[...], 0, 0)
    for j in range(8):
        jx, jy, jz = j // 4, j // 2 % 2, j % 2
        spots = [
            ((2 * ux + jx) * 8 + 2 * uy + jy) * 16 + jz * 8 for ux in range(4) for uy in range(4)
        ]
        a = jnp.concatenate([act_ref[pl.ds(s, 8), :] for s in spots], axis=0)
        g = 1.0 / (1.0 + jnp.exp(-a))
        patch_ref[:, pl.ds(j * LANES, LANES)] = (a * g).astype(BF16)
        slope = g * (1.0 + a * (1.0 - g))
        grad = back[:, j * LANES : (j + 1) * LANES] * slope
        for n, s in enumerate(spots):
            act_ref[pl.ds(s, 8), :] = grad[n * 8 : n * 8 + 8, :]
    grad_ref[...] = act_ref[...].astype(BF16)

    turned = act_ref[...].T[:C, :].astype(BF16)
    conv_ref[:, pl.ds(20 * LANES, LANES)] = jnp.zeros((C, LANES), F32)
    for tap in range(9):
        part = dot(turned, window(cols_ref, tap // 3, tap % 3))
        for dz in range(3):
            conv_ref[:, pl.ds((tap * 3 + dz) * C, C)] = part[:, dz * LANES : dz * LANES + C]
    part = dot(cot_ref[...], patch_ref[...])
    for j in range(8):
        down_ref[:, pl.ds(j * C, C)] = part[:, j * LANES : j * LANES + C]
    core = core_ref[0]
    for ref, half in ((keep_ref, core), (send_ref, 1 - core)):
        for lt in range(20):
            ref[pl.ds(lt * 48, 48), :] = conv_ref[
                pl.ds(pl.multiple_of(half * 48, 16), 48), pl.ds(lt * LANES, LANES)
            ].astype(ref.dtype)
        for lt in range(6):
            ref[pl.ds(960 + lt * 96, 96), :] = down_ref[
                pl.ds(pl.multiple_of(half * 96, 32), 96), pl.ds(lt * LANES, LANES)
            ].astype(ref.dtype)
        last = conv_ref[pl.ds(pl.multiple_of(half * 48, 16), 48), pl.ds(20 * LANES, LANES)]
        last = pltpu.roll(last, C, 1)
        free_ref[...] = jnp.zeros((16, 8, LANES), F32)
        for part in range(3):
            free_ref[:, part : part + 1, :] = last[part * 16 : part * 16 + 16, :].reshape(16, 1, LANES)
        ref[pl.ds(MAIN_ROWS, 128), :] = free_ref[...].reshape(128, LANES).astype(ref.dtype)


def side_kernel(grad_ref, patch_ref, dw_ref, send_ref, coarse_ref, src_ref, flat_ref, row_ref):
    src_ref[...] = grad_ref[...].astype(F32)
    spread_rows(src_ref, flat_ref, True)
    to_chips(flat_ref, row_ref)
    row_ref[:, 31:32, :] = jnp.zeros((32, 1, LANES), F32)
    pack(row_ref, send_ref)
    coarse_ref[...] = dot(dw_ref[...], patch_ref[...], 1, 1).astype(BF16)


def backward_kernel(grad_ref, halo_ref, w_ref, out_ref, pad_ref, cols_ref, act_ref, row_ref, flat_ref):
    for x in range(SIDE):
        for y in range(SIDE):
            base = ((x + 1) * 10 + y + 1) * COL
            for par in range(2):
                pad_ref[pl.ds(base + 1 + par, 8, stride=2), :] = grad_ref[
                    pl.ds((x * 8 + y) * 16 + par * 8, 8), :
                ].astype(F32)
    fill_halo(pad_ref, halo_ref, row_ref, flat_ref)
    shifted_columns(pad_ref, cols_ref)
    full = conv_wide(cols_ref, w_ref)
    for n in range(64):
        for par in range(2):
            act_ref[pl.ds(n * 16 + par, 8, stride=2), :] = full[n * 16 + par * 8 : n * 16 + par * 8 + 8, :]
    out_ref[...] = act_ref[...].T[:C, :]


def finish_kernel(core_ref, mine_ref, other_ref, conv_ref, down_ref, last_ref):
    def squares(values):
        return jnp.sum((values * values).reshape(-1, 8, LANES), axis=0)

    conv_sum = jnp.zeros((8, LANES), F32)
    down_sum = jnp.zeros((8, LANES), F32)
    for n, ref in enumerate((mine_ref, other_ref)):
        conv_sum += squares(ref[0:CONV_CHIPS, 24:72, :].astype(F32))
        down_sum += squares(ref[CONV_CHIPS:32, 24:72, :].astype(F32))
        for part in range(3):
            rows = ref[0:16, part * 8 : part * 8 + 8, :].astype(F32)
            rows = pltpu.roll(rows, 32, 2)[:, 7:8, :].reshape(16, LANES)
            rows = jnp.where(lanes_of(rows) < 32, rows, 0.0)
            last_ref[n, pl.ds(part * 16, 16), :] = rows
            conv_sum += squares(rows)
    conv_scale = lax.rsqrt(jnp.sum(conv_sum, keepdims=True) * (1.0 / (C * 27 * C)) + EPSILON)
    down_scale = lax.rsqrt(jnp.sum(down_sum, keepdims=True) * (1.0 / (C2 * 8 * C)) + EPSILON)
    core = core_ref[0]
    for n, (ref, half) in enumerate(((mine_ref, core), (other_ref, 1 - core))):
        rows = pl.ds(pl.multiple_of(half * 48, 16), 48)
        for lt in range(20):
            conv_ref[rows, pl.ds(lt * LANES, LANES)] = ref[lt, 24:72, :].astype(F32) * conv_scale
        conv_ref[rows, pl.ds(20 * LANES, 32)] = (last_ref[n] * conv_scale)[:, :32]
        for lt in range(6):
            for part in range(2):
                rows = pl.ds(pl.multiple_of(half * 96 + part * 48, 16), 48)
                values = ref[CONV_CHIPS + lt * 2 + part, 24:72, :].astype(F32) * down_scale
                down_ref[rows, pl.ds(lt * LANES, LANES)] = values


def there(rows):
    return pltpu.with_memory_space_constraint(rows, pltpu.HBM)


def here(rows):
    return pltpu.with_memory_space_constraint(rows, pltpu.VMEM)


def call(body, outs, scratch=(), scalars=0, ins=0, name=None):
    specs = [pl.BlockSpec(memory_space=pltpu.SMEM)] * scalars + [
        pl.BlockSpec(memory_space=pltpu.VMEM)
    ] * ins
    return pl.pallas_call(
        body,
        out_shape=[
            jax.ShapeDtypeStruct(shape, kind) if leaves else pltpu.VMEM(shape, kind)
            for shape, kind, *leaves in outs
        ],
        in_specs=specs,
        out_specs=[pl.BlockSpec(memory_space=pltpu.VMEM)] * len(outs),
        scratch_shapes=list(scratch),
        compiler_params=PARAMS,
        name=name,
    )


CHIPS = ("y", "z")
SPACE = ("y", "z", "c")


def trade(rows, axes):
    return lax.all_to_all(rows, axes, 0, 0, tiled=True)


def shards(features, cotangent, conv_weight, down_weight, neighbours):
    block = features[0, 0]
    cot = cotangent[0, 0]
    core = lax.axis_index("c").astype(jnp.int32).reshape(1)
    rows_shape = ((VOX, LANES), BF16)
    by_chip = (32, 32, LANES)
    packed = (32, 24, LANES)
    flat_scratch = pltpu.VMEM((VOX, LANES), F32)
    slot_scratch = pltpu.VMEM(by_chip, F32)

    def swap(rows):
        return lax.ppermute(rows, "c", [(0, 1), (1, 0)])

    (spread,) = pl.pallas_call(
        spread_kernel,
        out_shape=[pltpu.VMEM(packed, BF16)],
        in_specs=[pl.BlockSpec(memory_space=pltpu.HBM)] * 3,
        out_specs=[pl.BlockSpec(memory_space=pltpu.VMEM)],
        scratch_shapes=[
            pltpu.SMEM((1, 26), jnp.int32),
            pltpu.VMEM((C, VOX), BF16),
            pltpu.VMEM((32, LANES), jnp.int32),
            pltpu.SemaphoreType.DMA((3,)),
            flat_scratch,
            flat_scratch,
            slot_scratch,
        ],
        compiler_params=PARAMS,
        name="spread",
    )(there(neighbours[0]), there(block), there(jnp.asarray(direction_table())))
    middle = here(trade(spread, CHIPS))
    route = call(route_kernel, [(packed, BF16)], [slot_scratch], scalars=1, ins=3, name="route")
    (routed,) = route(core, middle, middle, here(swap(middle)))
    halo = trade(routed, CHIPS)

    taps = conv_weight.reshape(C, 27, C)
    pad = ((0, 0), (0, LANES - C), (0, LANES - C))
    forward_w = jnp.pad(taps.transpose(1, 2, 0), pad).reshape(9, 3 * LANES, LANES)
    backward_w = jnp.pad(taps.transpose(1, 0, 2)[::-1], pad).reshape(9, 3 * LANES, LANES)
    down_w = jnp.pad(down_weight.reshape(C2, 8, C), ((0, 0), (0, 0), (0, LANES - C))).reshape(C2, 8 * LANES)
    (own,) = call(prepare_kernel, [((VOX, LANES), F32)], ins=1, name="prepare")(block)
    halo, forward_w, backward_w, down_w, own = lax.optimization_barrier(
        (halo, forward_w, backward_w, down_w, own)
    )
    forward_w, backward_w, down_w = here(forward_w), here(backward_w), here(down_w)

    pad_scratch = pltpu.VMEM((100 * COL, LANES), F32)
    cols_scratch = pltpu.VMEM((10, 10, DEPTH, 3 * LANES), BF16)
    grad, patch, keep, send = call(
        forward_kernel,
        [rows_shape, ((LANES, 8 * LANES), BF16), ((HALF_ROWS, LANES), F32), ((HALF_ROWS, LANES), BF16)],
        [
            pad_scratch,
            cols_scratch,
            flat_scratch,
            slot_scratch,
            flat_scratch,
            pltpu.VMEM((C, 21 * LANES), F32),
            pltpu.VMEM((C2, 8 * C), F32),
            pltpu.VMEM((16, 8, LANES), F32),
        ],
        scalars=1,
        ins=5,
        name="forward",
    )(core, here(own), here(halo), cot, forward_w, down_w)
    spread2, coarse = call(
        side_kernel, [(packed, BF16), ((C2, LANES), BF16, True)], [flat_scratch, flat_scratch, slot_scratch], ins=3, name="side"
    )(grad, patch, down_w)

    message = (32, 72, LANES)
    (out,) = call(merge_kernel, [(message, BF16)], ins=3, name="merge")(spread2, keep, here(swap(send)))
    part, middle2 = call(total_kernel, [((4, 56, LANES), F32), (packed, BF16)], ins=1, name="total")(
        here(trade(out, CHIPS))
    )
    other2 = swap(middle2)
    line = trade(part, "x")
    (routed2,) = route(core, middle, middle2, here(other2))
    (out,) = call(join_kernel, [(message, BF16)], ins=2, name="join")(here(line), routed2)
    got = trade(out, CHIPS)
    theirs = swap(got)
    (grad_features,) = call(
        backward_kernel,
        [((C, VOX), F32, True)],
        [pad_scratch, cols_scratch, flat_scratch, slot_scratch, flat_scratch],
        ins=3,
        name="backward",
    )(grad, here(got), backward_w)
    grad_conv, grad_down = call(
        finish_kernel,
        [((C, 27 * C), F32, True), ((C2, 8 * C), F32, True)],
        [pltpu.VMEM((2, 48, LANES), F32)],
        scalars=1,
        ins=2,
        name="finish",
    )(core, here(got), here(theirs))
    return coarse[None, None], grad_features[None, None], grad_conv, grad_down


def solution(mesh):
    devices = mesh.devices
    fine = Mesh(devices.reshape(devices.shape[0], 4, -1, 2), ("x", "y", "z", "c"))
    block = P("x", SPACE, None, None)
    return jax.shard_map(
        shards,
        mesh=fine,
        in_specs=(block, block, P(), P(), P("x", SPACE, None)),
        out_specs=(block, block, P(), P()),
        check_vma=False,
    )
```
